32 devices in a mesh: dp: 2 (over y), gx: 4 (over x, core), gy: 4 (over z).
Axes of the slice: x: 2, y: 2, z: 4, core: 2. Of those that a mesh axis runs over, the one named last changes fastest.
Arguments:
- tokens: bfloat16 [2, 11664, 1152], P(None, ('dp', 'gy'), 'gx'), may hold values from -6 to 6
- cotangent: bfloat16 [2, 11664, 1152], P(None, ('dp', 'gy'), 'gx'), may hold values from -6 to 6
- ln1_gain: bfloat16 [1152], P('gx'), may hold values from 0.25 to 1.75
- ln1_bias: bfloat16 [1152], P('gx'), may hold values from -3 to 3
- qkv_weight: bfloat16 [1152, 3, 1152], P('gx', None, 'gy'), may hold values from -0.1875 to 0.1875
- qv_bias: bfloat16 [2, 1152], P(None, 'gy'), may hold values from -3 to 3
- out_weight: bfloat16 [1152, 1152], P('gy', 'gx'), may hold values from -1.5 to 1.5
- out_bias: bfloat16 [1152], P('gx'), may hold values from -3 to 3
- ln2_gain: bfloat16 [1152], P('gx'), may hold values from 0.25 to 1.75
- ln2_bias: bfloat16 [1152], P('gx'), may hold values from -3 to 3
- fc1_weight: bfloat16 [1152, 4304], P('gx', 'gy'), may hold values from -0.1875 to 0.1875
- fc1_bias: bfloat16 [4304], P('gy'), may hold values from -3 to 3
- fc2_weight: bfloat16 [4304, 1152], P('gy', 'gx'), may hold values from -0.09375 to 0.09375
- fc2_bias: bfloat16 [1152], P('gx'), may hold values from -3 to 3
Outputs:
- layer_out: bfloat16 [2, 11664, 1152], P(None, ('dp', 'gy'), 'gx')
- tokens_grad: bfloat16 [2, 11664, 1152], P(None, ('dp', 'gy'), 'gx')
- ln1_gain_grad: float32 [1152], P('gx')
- ln1_bias_grad: float32 [1152], P('gx')
- qkv_weight_grad: float32 [1152, 3, 1152], P('gx', None, 'gy')
- qv_bias_grad: float32 [2, 1152], P(None, 'gy')
- out_weight_grad: float32 [1152, 1152], P('gy', 'gx')
- out_bias_grad: float32 [1152], P('gx')
- ln2_gain_grad: float32 [1152], P('gx')
- ln2_bias_grad: float32 [1152], P('gx')
- fc1_weight_grad: float32 [1152, 4304], P('gx', 'gy')
- fc1_bias_grad: float32 [4304], P('gy')
- fc2_weight_grad: float32 [4304, 1152], P('gy', 'gx')
- fc2_bias_grad: float32 [1152], P('gx')
The draws below stay inside these ranges and needn't reach their ends.
All inputs are finite; a program needn't handle non-finite values.
Results may differ from the reference program's by a relative error of at most 0.013.
The reference program's roundings to bfloat16 on the way count: a program that leaves them out, or rounds other values in their place, can miss the bound.
Values may be sent and summed in bfloat16 or wider, within the bound.
No kernel may reach another device: no remote copies, remote signals or barrier semaphores. Data moves between devices by JAX's collectives and lax.ppermute only.
A program may use at most 384 MiB of HBM per device.

```python
import jax
import jax.numpy as jnp
from jax import lax

D = 1152
HEADS = 16
HEAD_DIM = 72
FF = 4304
SEQ = 729
MICRO = 2
TOKENS = 11664


def level_of(rng, shape, cuts, least, largest):
    def one(position, blocks):
        draws = jax.random.uniform(jax.random.fold_in(jax.random.fold_in(rng, 6), position), (blocks,), jnp.float32, least / len(cuts), largest / len(cuts))
        return jnp.repeat(jnp.exp(draws), shape[position] // blocks).reshape((-1,) + (1,) * (len(shape) - position - 1))

    gain = one(*cuts[0])
    for cut in cuts[1:]:
        gain = gain * one(*cut)
    return gain


def scatter_about(own_key, dims, deviation, most, split=(), kind=jnp.bfloat16):
    entries = deviation * jax.random.normal(own_key, dims, jnp.float32)
    if split:
        entries = entries * level_of(own_key, dims, split, -0.22, 0.18)
    return jnp.clip(entries, -most, most).astype(kind)


def setup_inputs(seed: int = 0) -> dict:
    arg_keys = jax.random.split(jax.random.key(seed), 15)
    return {
        "tokens": scatter_about(arg_keys[0], (MICRO, TOKENS, D), 1.0, 6.0, ((1, 8), (2, 4))),
        "cotangent": scatter_about(arg_keys[1], (MICRO, TOKENS, D), 1.0, 6.0, ((1, 8), (2, 4))),
        "ln1_gain": jnp.clip(1.0 + 0.15 * jax.random.normal(arg_keys[2], (D,), jnp.float32), 0.25, 1.75).astype(jnp.bfloat16),
        "ln1_bias": scatter_about(arg_keys[3], (D,), 0.5, 3.0, ((0, 4),)),
        "qkv_weight": scatter_about(arg_keys[4], (D, 3, D), D ** -0.5, 0.1875, ((0, 4), (2, 4))),
        "qv_bias": scatter_about(arg_keys[5], (2, D), 0.5, 3.0, ((1, 4),)),
        "out_weight": scatter_about(arg_keys[6], (D, D), (D // 64) ** -0.5, 1.5, ((0, 4), (1, 4))),
        "out_bias": scatter_about(arg_keys[7], (D,), 0.5, 3.0, ((0, 4),)),
        "ln2_gain": jnp.clip(1.0 + 0.15 * jax.random.normal(arg_keys[8], (D,), jnp.float32), 0.25, 1.75).astype(jnp.bfloat16),
        "ln2_bias": scatter_about(arg_keys[9], (D,), 0.5, 3.0, ((0, 4),)),
        "fc1_weight": scatter_about(arg_keys[10], (D, FF), D ** -0.5, 0.1875, ((0, 4), (1, 4))),
        "fc1_bias": scatter_about(arg_keys[11], (FF,), 0.5, 3.0, ((0, 4),)),
        "fc2_weight": scatter_about(arg_keys[12], (FF, D), FF ** -0.5, 0.09375, ((0, 4), (1, 4))),
        "fc2_bias": scatter_about(arg_keys[13], (D,), 0.5, 3.0, ((0, 4),)),
    }


epsilon = 1e-06
highest = lax.Precision.HIGHEST

@jax.custom_vjp
def low(v):
    return lax.optimization_barrier(v.astype(jnp.bfloat16)).astype(jnp.float32)

@jax.custom_vjp
def low_back(v):
    return v

def low_keep(v):
    return (low(v), None)

def low_pass(kept, grad):
    return (grad,)

def back_keep(v):
    return (v, None)

def back_low(kept, grad):
    return (low(grad),)
low.defvjp(low_keep, low_pass)
low_back.defvjp(back_keep, back_low)

def layer_norm(values, norm_gain, norm_shift):
    center = lax.optimization_barrier(jnp.mean(values, axis=-1, keepdims=True))
    spread = lax.optimization_barrier(jnp.mean(jnp.square(values - center), axis=-1, keepdims=True))
    return (values - center) * lax.rsqrt(spread + epsilon) * norm_gain + norm_shift

def matmul(left_side, right_side):
    return jnp.dot(left_side, right_side, preferred_element_type=jnp.float32, precision=highest)

def whole_layer(picture, params):
    ln1_gain, ln1_bias, qkv_weight, qv_bias, out_weight, out_bias, ln2_gain, ln2_bias, fc1_weight, fc1_bias, fc2_weight, fc2_bias = params
    normed = low(layer_norm(picture, ln1_gain, ln1_bias))
    bias_rows = jnp.stack([qv_bias[0], jnp.zeros_like(qv_bias[0]), qv_bias[1]])
    projected = matmul(normed, qkv_weight.reshape(D, 3 * D)).reshape(SEQ, 3, D) + bias_rows
    packed = low(low_back(projected)).reshape(SEQ, 3, HEADS, HEAD_DIM)
    queries = packed[:, 0]
    key_rows = packed[:, 1]
    values = packed[:, 2]
    scores = low_back(jnp.einsum('qhd,khd->hqk', queries, key_rows, precision=highest) * HEAD_DIM ** (-0.5))
    probability = low(jax.nn.softmax(scores, axis=-1))
    mixture = jnp.einsum('hqk,khd->qhd', probability, values, precision=highest).reshape(SEQ, D)
    mixture = low(low_back(mixture))
    hidden = picture + low_back(matmul(mixture, out_weight) + out_bias)
    normed_two = low(layer_norm(hidden, ln2_gain, ln2_bias))
    first_out = low_back(matmul(normed_two, fc1_weight) + fc1_bias)
    active = low(jax.nn.gelu(first_out, approximate=True))
    return hidden + low_back(matmul(active, fc2_weight) + fc2_bias)

def reference(tokens, cotangent, ln1_gain, ln1_bias, qkv_weight, qv_bias, out_weight, out_bias, ln2_gain, ln2_bias, fc1_weight, fc1_bias, fc2_weight, fc2_bias):
    params = tuple((array_in.astype(jnp.float32) for array_in in (ln1_gain, ln1_bias, qkv_weight, qv_bias, out_weight, out_bias, ln2_gain, ln2_bias, fc1_weight, fc1_bias, fc2_weight, fc2_bias)))
    images = tokens.astype(jnp.float32).reshape(-1, SEQ, D)
    grads_in = cotangent.astype(jnp.float32).reshape(-1, SEQ, D)
    starting = jax.tree.map(jnp.zeros_like, params)

    def one_image(running, element):
        picture, picture_grad = element
        result, pullback = jax.vjp(whole_layer, picture, params)
        grad_picture, grad_params = pullback(picture_grad)
        return (jax.tree.map(jnp.add, running, grad_params), (result, grad_picture))
    totals, (results, grad_tokens) = lax.scan(one_image, starting, (images, grads_in))
    return (results.reshape(tokens.shape).astype(jnp.bfloat16), grad_tokens.reshape(tokens.shape).astype(jnp.bfloat16), totals[0], totals[1], totals[2], totals[3], totals[4], totals[5], totals[6], totals[7], totals[8], totals[9], totals[10], totals[11])
```

```python
import functools

import jax
import jax.numpy as jnp
from jax import lax
from jax.experimental import pallas as pl
from jax.experimental.pallas import tpu as pltpu
from jax.sharding import PartitionSpec as P

HEAD_DIM = 72
SEQ = 729
MICRO = 2
EPSILON = 1e-06
QUERY_ROWS = 384
BF16 = jnp.bfloat16
F32 = jnp.float32
VMEM_BYTES = 60 * 2**20


def contract(left, right, left_dim, right_dim):
    return lax.dot_general(
        left, right, (((left_dim,), (right_dim,)), ((), ())), preferred_element_type=F32
    )


def row_blocks(total, size):
    return [(low, min(low + size, total)) for low in range(0, total, size)]


def attend_kernel(heads, packed_ref, mix_ref, total_ref):
    seq = packed_ref.shape[1]
    width = heads * HEAD_DIM
    scaling = HEAD_DIM ** (-0.5)
    for head in range(heads):
        first = head * HEAD_DIM
        last = first + HEAD_DIM
        keys = packed_ref[0, :, width + first : width + last]
        values = packed_ref[0, :, 2 * width + first : 2 * width + last]
        for low, high in row_blocks(seq, QUERY_ROWS):
            queries = packed_ref[0, low:high, first:last]
            scores = contract(queries, keys, 1, 1) * scaling
            row_max = jnp.max(scores, axis=1, keepdims=True)
            exponent = jnp.exp(scores - row_max)
            row_total = jnp.sum(exponent, axis=1, keepdims=True)
            probability = (exponent * (1.0 / row_total)).astype(BF16)
            mix_ref[0, low:high, first:last] = contract(probability, values, 1, 0).astype(BF16)
            total_ref[0, low:high, head : head + 1] = row_max + jnp.log(row_total)


def attend(packed, heads):
    groups, seq, _ = packed.shape
    width = heads * HEAD_DIM
    return pl.pallas_call(
        functools.partial(attend_kernel, heads),
        grid=(groups,),
        in_specs=[pl.BlockSpec((1, seq, 3 * width), lambda i: (i, 0, 0))],
        out_specs=[
            pl.BlockSpec((1, seq, width), lambda i: (i, 0, 0)),
            pl.BlockSpec((1, seq, heads), lambda i: (i, 0, 0)),
        ],
        out_shape=[
            jax.ShapeDtypeStruct((groups, seq, width), BF16),
            jax.ShapeDtypeStruct((groups, seq, heads), F32),
        ],
        compiler_params=pltpu.CompilerParams(vmem_limit_bytes=VMEM_BYTES),
        cost_estimate=pl.CostEstimate(
            flops=12 * groups * heads * seq * seq * HEAD_DIM,
            bytes_accessed=8 * groups * seq * width,
            transcendentals=groups * heads * seq * seq,
        ),
        name="attend",
    )(packed)


def attend_back_kernel(heads, packed_ref, total_ref, grad_ref, out_ref, key_sum, value_sum):
    seq = packed_ref.shape[1]
    width = heads * HEAD_DIM
    scaling = HEAD_DIM ** (-0.5)
    for head in range(heads):
        first = head * HEAD_DIM
        last = first + HEAD_DIM
        keys = packed_ref[0, :, width + first : width + last]
        values = packed_ref[0, :, 2 * width + first : 2 * width + last]
        for low, high in row_blocks(seq, QUERY_ROWS):
            queries = packed_ref[0, low:high, first:last]
            grads = grad_ref[0, low:high, first:last]
            scores = contract(keys, queries, 1, 1) * scaling
            probability = jnp.exp(scores - total_ref[0, head : head + 1, low:high])
            grad_values = contract(probability.astype(BF16), grads, 1, 0)
            grad_prob = contract(values, grads, 1, 1)
            inner = jnp.sum(probability * grad_prob, axis=0, keepdims=True)
            grad_scores = (probability * (grad_prob - inner)).astype(BF16)
            grad_keys = contract(grad_scores, queries, 1, 0)
            grad_queries = contract(grad_scores, keys, 0, 0) * scaling
            out_ref[0, low:high, first:last] = grad_queries.astype(BF16)
            if low == 0:
                key_sum[...] = grad_keys
                value_sum[...] = grad_values
            else:
                key_sum[...] += grad_keys
                value_sum[...] += grad_values
        out_ref[0, :, width + first : width + last] = (key_sum[...] * scaling).astype(BF16)
        out_ref[0, :, 2 * width + first : 2 * width + last] = value_sum[...].astype(BF16)


def attend_back(packed, total, grads, heads):
    groups, seq, _ = packed.shape
    width = heads * HEAD_DIM
    return pl.pallas_call(
        functools.partial(attend_back_kernel, heads),
        grid=(groups,),
        in_specs=[
            pl.BlockSpec((1, seq, 3 * width), lambda i: (i, 0, 0)),
            pl.BlockSpec((1, heads, seq), lambda i: (i, 0, 0)),
            pl.BlockSpec((1, seq, width), lambda i: (i, 0, 0)),
        ],
        out_specs=pl.BlockSpec((1, seq, 3 * width), lambda i: (i, 0, 0)),
        out_shape=jax.ShapeDtypeStruct((groups, seq, 3 * width), BF16),
        scratch_shapes=[pltpu.VMEM((seq, HEAD_DIM), F32), pltpu.VMEM((seq, HEAD_DIM), F32)],
        compiler_params=pltpu.CompilerParams(vmem_limit_bytes=VMEM_BYTES),
        cost_estimate=pl.CostEstimate(
            flops=30 * groups * heads * seq * seq * HEAD_DIM,
            bytes_accessed=14 * groups * seq * width,
            transcendentals=groups * heads * seq * seq,
        ),
        name="attend_back",
    )(packed, total, grads)


def norm_forward(values):
    center = jnp.mean(values, axis=1, keepdims=True)
    shifted = values - center
    inverse = lax.rsqrt(jnp.mean(shifted * shifted, axis=1, keepdims=True) + EPSILON)
    return shifted * inverse, inverse


def norm_backward(grad_norm, normed, inverse, gain):
    grad_hat = grad_norm * gain
    return inverse * (
        grad_hat
        - jnp.mean(grad_hat, axis=1, keepdims=True)
        - normed * jnp.mean(grad_hat * normed, axis=1, keepdims=True)
    )


def gelu_pair(values):
    slope = 0.7978845608028654
    cubic = 0.044715
    bent = jnp.tanh(slope * (values + cubic * (values * values * values)))
    half = 0.5 * (1.0 + bent)
    result = values * half
    grad = half + 0.5 * values * (1.0 - bent * bent) * slope * (
        1.0 + (3.0 * cubic) * (values * values)
    )
    return result, grad


def images_here(block, copies):
    rows = block.shape[0] * block.shape[1]
    images = block.reshape(rows // SEQ, SEQ, block.shape[2])
    if copies > 1:
        images = jnp.repeat(images, copies, axis=0)
    whole = lax.all_to_all(images, "gx", split_axis=0, concat_axis=2, tiled=True)
    return whole.reshape(SEQ, whole.shape[2])


def images_back(image, copies, shape):
    parts = lax.all_to_all(image[None], "gx", split_axis=2, concat_axis=0, tiled=True)
    if copies > 1:
        parts = parts[::copies]
    return parts.reshape(shape)


def collect(block, order):
    return lax.all_gather(block, order, axis=0, tiled=True)


def shares(grads, order, extra):
    summed = lax.psum_scatter(grads.astype(BF16), order, scatter_dimension=0, tiled=True)
    return lax.psum(summed.astype(F32), "dp") * extra


def on_device(
    tokens,
    cotangent,
    ln1_gain,
    ln1_bias,
    qkv_weight,
    qv_bias,
    out_weight,
    out_bias,
    ln2_gain,
    ln2_bias,
    fc1_weight,
    fc1_bias,
    fc2_weight,
    fc2_bias,
):
    gx = lax.axis_size("gx")
    gy = lax.axis_size("gy")
    shape = tokens.shape
    part = shape[2]
    head_cols = qkv_weight.shape[2]
    heads = head_cols // HEAD_DIM
    hidden_cols = fc1_weight.shape[1]
    width = part * gx
    copies = gx // (MICRO * shape[1] // SEQ)
    extra = 1.0 / copies
    along = ("gy", "gx")

    image = images_here(tokens, copies).astype(F32)
    whole_qkv = collect(qkv_weight.reshape(part, 3 * head_cols), along)
    whole_qkv = whole_qkv.reshape(gy, width, 3 * head_cols)
    whole_out = collect(out_weight, ("gx", "gy")).reshape(gx, gy * head_cols, part)
    whole_out = jnp.concatenate([whole_out[i] for i in range(gx)], axis=1)
    whole_fc1 = collect(fc1_weight, along).reshape(gy, width, hidden_cols)
    whole_fc2 = collect(fc2_weight.T, along).reshape(gy, width, hidden_cols)

    wide = jnp.stack([ln1_gain, ln1_bias, out_bias, ln2_gain, ln2_bias, fc2_bias])
    wide = lax.all_gather(wide.astype(F32), "gx", axis=1, tiled=True)
    gain_one, shift_one, bias_mix, gain_two, shift_two, bias_second = [wide[i] for i in range(6)]
    deep = jnp.concatenate([qv_bias[0], qv_bias[1], fc1_bias]).astype(F32)
    deep = lax.all_gather(deep, "gy", axis=0, tiled=False)
    bias_qkv = jnp.concatenate(
        [deep[:, :head_cols], jnp.zeros((gy, head_cols), F32), deep[:, head_cols : 2 * head_cols]],
        axis=1,
    )
    bias_first = deep[:, 2 * head_cols :]

    normed_one, inverse_one = norm_forward(image)
    ready_one = (normed_one * gain_one + shift_one).astype(BF16)
    packed = jnp.stack(
        [
            (contract(ready_one, whole_qkv[j], 1, 0) + bias_qkv[j]).astype(BF16)
            for j in range(gy)
        ]
    )
    mixture, log_total = attend(packed, heads)
    mixture = jnp.concatenate([mixture[j] for j in range(gy)], axis=1)
    hidden = image + (contract(mixture, whole_out, 1, 0) + bias_mix)
    normed_two, inverse_two = norm_forward(hidden)
    ready_two = (normed_two * gain_two + shift_two).astype(BF16)
    active = []
    slopes = []
    second = bias_second
    for j in range(gy):
        result, slope = gelu_pair(contract(ready_two, whole_fc1[j], 1, 0) + bias_first[j])
        active.append(result.astype(BF16))
        slopes.append(slope)
        second = second + contract(active[j], whole_fc2[j], 1, 1)
    layer_out = images_back((hidden + second).astype(BF16), copies, shape)

    grad_low = images_here(cotangent, copies)
    grad_out = grad_low.astype(F32)
    grad_fc2 = jnp.stack([contract(grad_low, active[j], 0, 0).astype(BF16) for j in range(gy)])
    grad_fc2 = shares(grad_fc2.reshape(gy * width, hidden_cols), along, extra).T
    grad_first = []
    grad_ready_two = None
    for j in range(gy):
        grad_active = contract(grad_low, whole_fc2[j], 1, 0)
        grad_first.append((grad_active * slopes[j]).astype(BF16))
        term = contract(grad_first[j], whole_fc1[j], 1, 1)
        grad_ready_two = term if j == 0 else grad_ready_two + term
    grad_fc1 = jnp.stack([contract(ready_two, grad_first[j], 0, 0).astype(BF16) for j in range(gy)])
    grad_fc1 = shares(grad_fc1.reshape(gy * width, hidden_cols), along, extra)
    grad_hidden = grad_out + norm_backward(grad_ready_two, normed_two, inverse_two, gain_two)
    grad_hidden_low = grad_hidden.astype(BF16)
    grad_out_weight = contract(mixture, grad_hidden_low, 0, 0).astype(BF16)
    grad_out_weight = jnp.concatenate(
        [grad_out_weight[:, i * part : (i + 1) * part] for i in range(gx)], axis=0
    )
    grad_out_weight = shares(grad_out_weight, ("gx", "gy"), extra)
    grad_mixture = contract(grad_hidden_low, whole_out, 1, 1).astype(BF16)
    grad_mixture = jnp.stack(
        [grad_mixture[:, j * head_cols : (j + 1) * head_cols] for j in range(gy)]
    )
    grad_packed = attend_back(packed, jnp.swapaxes(log_total, 1, 2), grad_mixture, heads)
    grad_qkv = jnp.stack(
        [contract(ready_one, grad_packed[j], 0, 0).astype(BF16) for j in range(gy)]
    )
    grad_qkv = shares(grad_qkv.reshape(gy * width, 3 * head_cols), along, extra)
    grad_ready_one = None
    for j in range(gy):
        term = contract(grad_packed[j], whole_qkv[j], 1, 1)
        grad_ready_one = term if j == 0 else grad_ready_one + term
    tokens_grad = grad_hidden + norm_backward(grad_ready_one, normed_one, inverse_one, gain_one)
    tokens_grad = images_back(tokens_grad.astype(BF16), copies, shape)

    everywhere = ("dp", "gx", "gy")
    wide_sums = jnp.stack(
        [
            jnp.sum(grad_ready_one * normed_one, axis=0),
            jnp.sum(grad_ready_one, axis=0),
            jnp.sum(grad_hidden_low, axis=0, dtype=F32),
            jnp.sum(grad_ready_two * normed_two, axis=0),
            jnp.sum(grad_ready_two, axis=0),
            jnp.sum(grad_low, axis=0, dtype=F32),
        ]
    )
    packed_sums = jnp.sum(grad_packed, axis=1, dtype=F32)
    deep_sums = jnp.concatenate(
        [
            packed_sums[:, :head_cols],
            packed_sums[:, 2 * head_cols :],
            jnp.stack([jnp.sum(grad_first[j], axis=0, dtype=F32) for j in range(gy)]),
        ],
        axis=1,
    )
    wide_sums, deep_sums = lax.psum((wide_sums, deep_sums), everywhere)
    wide_sums = extra * lax.dynamic_slice_in_dim(wide_sums, lax.axis_index("gx") * part, part, 1)
    deep_sums = extra * lax.dynamic_index_in_dim(deep_sums, lax.axis_index("gy"), 0, False)
    return (
        layer_out,
        tokens_grad,
        wide_sums[0],
        wide_sums[1],
        grad_qkv.reshape(part, 3, head_cols),
        deep_sums[: 2 * head_cols].reshape(2, head_cols),
        grad_out_weight,
        wide_sums[2],
        wide_sums[3],
        wide_sums[4],
        grad_fc1,
        deep_sums[2 * head_cols :],
        grad_fc2,
        wide_sums[5],
    )


def solution(mesh):
    specs = (
        P(None, ("dp", "gy"), "gx"),
        P(None, ("dp", "gy"), "gx"),
        P("gx"),
        P("gx"),
        P("gx", None, "gy"),
        P(None, "gy"),
        P("gy", "gx"),
        P("gx"),
        P("gx"),
        P("gx"),
        P("gx", "gy"),
        P("gy"),
        P("gy", "gx"),
        P("gx"),
    )
    return jax.shard_map(
        on_device,
        mesh=mesh,
        in_specs=specs,
        out_specs=specs,
        check_vma=False,
    )
```

```python
import functools

import jax
import jax.numpy as jnp
from jax import lax
from jax.experimental import pallas as pl
from jax.experimental.pallas import tpu as pltpu
from jax.sharding import PartitionSpec as P

HEAD_DIM = 72
SEQ = 729
MICRO = 2
EPSILON = 1e-06
QUERY_ROWS = 384
ROWS = 256
COLS = 256
BF16 = jnp.bfloat16
F32 = jnp.float32
VMEM_BYTES = 60 * 2**20


def contract(left, right, left_dim, right_dim):
    return lax.dot_general(
        left, right, (((left_dim,), (right_dim,)), ((), ())), preferred_element_type=F32
    )


def blocks_of(total, size):
    return [(low, min(low + size, total)) for low in range(0, total, size)]


def whole(shape):
    return pl.BlockSpec(shape, lambda i, *_: (0,) * len(shape))


def nth(shape):
    return pl.BlockSpec((1,) + tuple(shape[1:]), lambda i, *_: (i,) + (0,) * (len(shape) - 1))


def call(kernel, name, steps, ins, outs, flops, scratch=(), prefetch=()):
    moved = sum(a.size * a.dtype.itemsize for a, _ in list(ins) + list(outs))
    return pl.pallas_call(
        kernel,
        grid_spec=pltpu.PrefetchScalarGridSpec(
            num_scalar_prefetch=len(prefetch),
            grid=(steps,),
            in_specs=[spec for _, spec in ins],
            out_specs=[spec for _, spec in outs],
            scratch_shapes=list(scratch),
        ),
        out_shape=[shape for shape, _ in outs],
        compiler_params=pltpu.CompilerParams(vmem_limit_bytes=VMEM_BYTES),
        cost_estimate=pl.CostEstimate(flops=flops, bytes_accessed=moved, transcendentals=0),
        name=name,
    )(*prefetch, *[a for a, _ in ins])


def struct(shape, dtype):
    return jax.ShapeDtypeStruct(tuple(shape), dtype)


def attend_kernel(heads, packed_ref, mix_ref, total_ref):
    seq = packed_ref.shape[1]
    width = heads * HEAD_DIM
    scaling = HEAD_DIM ** (-0.5)
    for head in range(heads):
        first = head * HEAD_DIM
        last = first + HEAD_DIM
        keys = packed_ref[0, :, width + first : width + last]
        values = packed_ref[0, :, 2 * width + first : 2 * width + last]
        for low, high in blocks_of(seq, QUERY_ROWS):
            queries = packed_ref[0, low:high, first:last]
            scores = contract(queries, keys, 1, 1) * scaling
            row_max = jnp.max(scores, axis=1, keepdims=True)
            exponent = jnp.exp(scores - row_max)
            row_total = jnp.sum(exponent, axis=1, keepdims=True)
            probability = (exponent * (1.0 / row_total)).astype(BF16)
            mix_ref[0, low:high, first:last] = contract(probability, values, 1, 0).astype(BF16)
            total_ref[0, low:high, head : head + 1] = row_max + jnp.log(row_total)


def attend(packed, heads):
    groups, seq, _ = packed.shape
    mix = struct((groups, seq, heads * HEAD_DIM), BF16)
    total = struct((groups, seq, heads), F32)
    return call(
        functools.partial(attend_kernel, heads),
        "attend",
        groups,
        [(packed, nth(packed.shape))],
        [(mix, nth(mix.shape)), (total, nth(total.shape))],
        12 * groups * heads * seq * seq * HEAD_DIM,
    )


def attend_back_kernel(
    heads, packed_ref, total_ref, grad_ref, out_ref, sum_ref, key_sum, value_sum
):
    seq = packed_ref.shape[1]
    width = heads * HEAD_DIM
    scaling = HEAD_DIM ** (-0.5)
    for head in range(heads):
        first = head * HEAD_DIM
        last = first + HEAD_DIM
        keys = packed_ref[0, :, width + first : width + last]
        values = packed_ref[0, :, 2 * width + first : 2 * width + last]
        for low, high in blocks_of(seq, QUERY_ROWS):
            queries = packed_ref[0, low:high, first:last]
            grads = grad_ref[0, low:high, first:last]
            scores = contract(keys, queries, 1, 1) * scaling
            probability = jnp.exp(scores - total_ref[0, head : head + 1, low:high])
            grad_values = contract(probability.astype(BF16), grads, 1, 0)
            grad_prob = contract(values, grads, 1, 1)
            inner = jnp.sum(probability * grad_prob, axis=0, keepdims=True)
            grad_scores = (probability * (grad_prob - inner)).astype(BF16)
            grad_keys = contract(grad_scores, queries, 1, 0)
            grad_queries = contract(grad_scores, keys, 0, 0) * scaling
            out_ref[0, low:high, first:last] = grad_queries.astype(BF16)
            if low == 0:
                key_sum[...] = grad_keys
                value_sum[...] = grad_values
            else:
                key_sum[...] += grad_keys
                value_sum[...] += grad_values
        out_ref[0, :, width + first : width + last] = (key_sum[...] * scaling).astype(BF16)
        out_ref[0, :, 2 * width + first : 2 * width + last] = value_sum[...].astype(BF16)
    sum_ref[0] = jnp.sum(out_ref[0].astype(F32), axis=0, keepdims=True)


def attend_back(packed, total, grads, heads):
    groups, seq, triple = packed.shape
    out = struct(packed.shape, BF16)
    sums = struct((groups, 1, triple), F32)
    return call(
        functools.partial(attend_back_kernel, heads),
        "attend_back",
        groups,
        [(packed, nth(packed.shape)), (total, nth(total.shape)), (grads, nth(grads.shape))],
        [(out, nth(out.shape)), (sums, nth(sums.shape))],
        30 * groups * heads * seq * seq * HEAD_DIM,
        [pltpu.VMEM((seq, HEAD_DIM), F32), pltpu.VMEM((seq, HEAD_DIM), F32)],
    )


def norm(values):
    center = jnp.mean(values, axis=1, keepdims=True)
    shifted = values - center
    inverse = lax.rsqrt(jnp.mean(shifted * shifted, axis=1, keepdims=True) + EPSILON)
    return shifted * inverse, inverse


def norm_back(grad_norm, normed, inverse, gain):
    grad_hat = grad_norm * gain
    return inverse * (
        grad_hat
        - jnp.mean(grad_hat, axis=1, keepdims=True)
        - normed * jnp.mean(grad_hat * normed, axis=1, keepdims=True)
    )


def join_columns(parts_ref, whole_ref):
    count, _, part = parts_ref.shape
    for i in range(count):
        whole_ref[:, i * part : (i + 1) * part] = parts_ref[i]


def turned(rows, blocks_ref):
    flat = rows.T
    count, size, _ = blocks_ref.shape
    for i in range(count):
        blocks_ref[i] = flat[i * size : (i + 1) * size]


def spread_kernel(parts_ref, whole_ref, turned_ref, sum_ref):
    join_columns(parts_ref, whole_ref)
    turned(whole_ref[...], turned_ref)
    sum_ref[...] = jnp.sum(whole_ref[...].astype(F32), axis=0, keepdims=True)


def spread(parts, blocks):
    count, seq, part = parts.shape
    width = count * part
    outs = [
        struct((seq, width), BF16),
        struct((blocks, width // blocks, seq), BF16),
        struct((1, width), F32),
    ]
    return call(
        spread_kernel,
        "spread",
        1,
        [(parts, whole(parts.shape))],
        [(o, whole(o.shape)) for o in outs],
        seq * width,
    )


def project_kernel(
    triple, parts_ref, gain_ref, shift_ref, weight_ref, bias_ref, image_ref, ready_ref, turned_ref, packed_ref
):
    @pl.when(pl.program_id(0) == 0)
    def _():
        join_columns(parts_ref, image_ref)
        for low, high in blocks_of(image_ref.shape[0], ROWS):
            normed, _ = norm(image_ref[low:high].astype(F32))
            ready_ref[low:high] = (normed * gain_ref[...] + shift_ref[...]).astype(BF16)
        turned(ready_ref[...], turned_ref)

    packed = contract(ready_ref[...], weight_ref[0, :, :triple], 1, 0) + bias_ref[0]
    packed_ref[0] = packed.astype(BF16)


def project(parts, gain, shift, weight, bias, blocks):
    count, seq, part = parts.shape
    width = count * part
    groups, _, triple = bias.shape
    outs = [
        (struct((seq, width), BF16), whole((seq, width))),
        (struct((seq, width), BF16), whole((seq, width))),
        (struct((blocks, width // blocks, seq), BF16), whole((blocks, width // blocks, seq))),
        (struct((groups, seq, triple), BF16), nth((groups, seq, triple))),
    ]
    return call(
        functools.partial(project_kernel, triple),
        "project",
        groups,
        [
            (parts, whole(parts.shape)),
            (gain, whole(gain.shape)),
            (shift, whole(shift.shape)),
            (weight, nth(weight.shape)),
            (bias, nth(bias.shape)),
        ],
        outs,
        2 * groups * seq * width * triple,
    )


def mix_kernel(
    image_ref, parts_ref, weight_ref, bias_ref, gain_ref, shift_ref, hidden_ref, ready_ref, turned_ref, joined
):
    join_columns(parts_ref, joined)
    for low, high in blocks_of(image_ref.shape[0], ROWS):
        mixed = contract(joined[low:high], weight_ref[...], 1, 0) + bias_ref[...]
        hidden = image_ref[low:high].astype(F32) + mixed
        hidden_ref[low:high] = hidden
        normed, _ = norm(hidden)
        ready_ref[low:high] = (normed * gain_ref[...] + shift_ref[...]).astype(BF16)
    turned(ready_ref[...], turned_ref)


def mix(image, parts, weight, bias, gain, shift, blocks):
    seq, width = image.shape
    inner = weight.shape[0]
    outs = [
        struct((seq, width), F32),
        struct((seq, width), BF16),
        struct((blocks, width // blocks, seq), BF16),
    ]
    return call(
        mix_kernel,
        "mix",
        1,
        [(a, whole(a.shape)) for a in (image, parts, weight, bias, gain, shift)],
        [(o, whole(o.shape)) for o in outs],
        2 * seq * width * inner,
        [pltpu.VMEM((seq, inner), BF16)],
    )


def expand_kernel(ready_ref, weight_ref, bias_ref, active_ref, slope_ref):
    bend = 0.7978845608028654
    cubic = 0.044715
    for low, high in blocks_of(weight_ref.shape[2], COLS):
        first = contract(ready_ref[...], weight_ref[0, :, low:high], 1, 0) + bias_ref[0, :, low:high]
        square = first * first
        bent = jnp.tanh(bend * (first + cubic * (first * square)))
        half = 0.5 * (1.0 + bent)
        active_ref[0, :, low:high] = (first * half).astype(BF16)
        slope_ref[0, :, low:high] = half + (0.5 * bend) * first * (1.0 - bent * bent) * (
            1.0 + (3.0 * cubic) * square
        )


def expand(ready, weight, bias):
    seq, width = ready.shape
    groups, _, cols = weight.shape
    shape = (groups, seq, cols)
    return call(
        expand_kernel,
        "expand",
        groups,
        [(ready, whole(ready.shape)), (weight, nth(weight.shape)), (bias, nth(bias.shape))],
        [(struct(shape, BF16), nth(shape)), (struct(shape, F32), nth(shape))],
        2 * groups * seq * width * cols,
    )


def narrow_kernel(hidden_ref, active_ref, weight_ref, bias_ref, out_ref, total):
    step = pl.program_id(0)
    term = contract(active_ref[0], weight_ref[0], 1, 1)

    @pl.when(step == 0)
    def _():
        total[...] = hidden_ref[...] + bias_ref[...] + term

    @pl.when(step > 0)
    def _():
        total[...] += term

    @pl.when(step == pl.num_programs(0) - 1)
    def _():
        count, _, part = out_ref.shape
        for i in range(count):
            out_ref[i] = total[:, i * part : (i + 1) * part].astype(BF16)


def narrow(hidden, active, weight, bias, count):
    seq, width = hidden.shape
    groups, _, cols = weight.shape
    shape = (count, seq, width // count)
    return call(
        narrow_kernel,
        "narrow",
        groups,
        [
            (hidden, whole(hidden.shape)),
            (active, nth(active.shape)),
            (weight, nth(weight.shape)),
            (bias, whole(bias.shape)),
        ],
        [(struct(shape, BF16), whole(shape))],
        2 * groups * seq * width * cols,
        [pltpu.VMEM((seq, width), F32)],
    )[0]


def feed_back_kernel(
    grad_ref,
    hidden_ref,
    gain_ref,
    slope_ref,
    second_ref,
    first_ref,
    first_grad_ref,
    first_sum_ref,
    hidden_grad_ref,
    low_ref,
    turned_ref,
    gain_sum_ref,
    shift_sum_ref,
    low_sum_ref,
    total,
):
    step = pl.program_id(0)
    for low, high in blocks_of(second_ref.shape[2], COLS):
        active_grad = contract(grad_ref[...], second_ref[0, :, low:high], 1, 0)
        first_grad = (active_grad * slope_ref[0, :, low:high]).astype(BF16)
        first_grad_ref[0, :, low:high] = first_grad
        first_sum_ref[0, :, low:high] = jnp.sum(first_grad.astype(F32), axis=0, keepdims=True)
    term = contract(first_grad_ref[0], first_ref[0], 1, 1)

    @pl.when(step == 0)
    def _():
        total[...] = term

    @pl.when(step > 0)
    def _():
        total[...] += term

    @pl.when(step == pl.num_programs(0) - 1)
    def _():
        gain_sum = jnp.zeros(gain_sum_ref.shape, F32)
        shift_sum = jnp.zeros(gain_sum_ref.shape, F32)
        low_sum = jnp.zeros(gain_sum_ref.shape, F32)
        for low, high in blocks_of(total.shape[0], ROWS):
            normed, inverse = norm(hidden_ref[low:high])
            ready_grad = total[low:high]
            gain_sum += jnp.sum(ready_grad * normed, axis=0, keepdims=True)
            shift_sum += jnp.sum(ready_grad, axis=0, keepdims=True)
            hidden_grad = grad_ref[low:high].astype(F32) + norm_back(
                ready_grad, normed, inverse, gain_ref[...]
            )
            hidden_grad_ref[low:high] = hidden_grad
            rounded = hidden_grad.astype(BF16)
            low_ref[low:high] = rounded
            low_sum += jnp.sum(rounded.astype(F32), axis=0, keepdims=True)
        gain_sum_ref[...] = gain_sum
        shift_sum_ref[...] = shift_sum
        low_sum_ref[...] = low_sum
        turned(low_ref[...], turned_ref)


def feed_back(grad, hidden, gain, slope, second, first, blocks):
    seq, width = hidden.shape
    groups, _, cols = first.shape
    row = struct((1, width), F32)
    outs = [
        (struct(slope.shape, BF16), nth(slope.shape)),
        (struct((groups, 1, cols), F32), nth((groups, 1, cols))),
    ] + [
        (o, whole(o.shape))
        for o in (
            struct((seq, width), F32),
            struct((seq, width), BF16),
            struct((blocks, width // blocks, seq), BF16),
            row,
            row,
            row,
        )
    ]
    return call(
        feed_back_kernel,
        "feed_back",
        groups,
        [
            (grad, whole(grad.shape)),
            (hidden, whole(hidden.shape)),
            (gain, whole(gain.shape)),
            (slope, nth(slope.shape)),
            (second, nth(second.shape)),
            (first, nth(first.shape)),
        ],
        outs,
        4 * groups * seq * width * cols,
        [pltpu.VMEM((seq, width), F32)],
    )


def mix_back_kernel(grad_ref, weight_ref, out_ref):
    groups, _, part = out_ref.shape
    full = contract(grad_ref[...], weight_ref[...], 1, 1).astype(BF16)
    for j in range(groups):
        out_ref[j] = full[:, j * part : (j + 1) * part]


def mix_back(grad, weight, groups):
    seq, width = grad.shape
    shape = (groups, seq, weight.shape[0] // groups)
    return call(
        mix_back_kernel,
        "mix_back",
        1,
        [(grad, whole(grad.shape)), (weight, whole(weight.shape))],
        [(struct(shape, BF16), whole(shape))],
        2 * seq * width * weight.shape[0],
    )[0]


def project_back_kernel(
    triple, image_ref, gain_ref, hidden_grad_ref, packed_ref, weight_ref, out_ref, gain_sum_ref, shift_sum_ref, total
):
    step = pl.program_id(0)
    term = contract(packed_ref[0], weight_ref[0, :, :triple], 1, 1)

    @pl.when(step == 0)
    def _():
        total[...] = term

    @pl.when(step > 0)
    def _():
        total[...] += term

    @pl.when(step == pl.num_programs(0) - 1)
    def _():
        count, _, part = out_ref.shape
        gain_sum = jnp.zeros(gain_sum_ref.shape, F32)
        shift_sum = jnp.zeros(gain_sum_ref.shape, F32)
        for low, high in blocks_of(total.shape[0], ROWS):
            normed, inverse = norm(image_ref[low:high].astype(F32))
            ready_grad = total[low:high]
            gain_sum += jnp.sum(ready_grad * normed, axis=0, keepdims=True)
            shift_sum += jnp.sum(ready_grad, axis=0, keepdims=True)
            result = hidden_grad_ref[low:high] + norm_back(
                ready_grad, normed, inverse, gain_ref[...]
            )
            for i in range(count):
                out_ref[i, low:high] = result[:, i * part : (i + 1) * part].astype(BF16)
        gain_sum_ref[...] = gain_sum
        shift_sum_ref[...] = shift_sum


def project_back(image, gain, hidden_grad, packed_grad, weight, count):
    seq, width = image.shape
    groups, _, triple = packed_grad.shape
    shape = (count, seq, width // count)
    row = struct((1, width), F32)
    return call(
        functools.partial(project_back_kernel, triple),
        "project_back",
        groups,
        [
            (image, whole(image.shape)),
            (gain, whole(gain.shape)),
            (hidden_grad, whole(hidden_grad.shape)),
            (packed_grad, nth(packed_grad.shape)),
            (weight, nth(weight.shape)),
        ],
        [
            (struct(shape, BF16), whole(shape)),
            (row, whole(row.shape)),
            (row, whole(row.shape)),
        ],
        2 * groups * seq * width * triple,
        [pltpu.VMEM((seq, width), F32)],
    )


def share_kernel(half, added, pick_ref, turned_ref, right_ref, *rest):
    rows = turned_ref.shape[1]
    picked = rest[-1]
    count = picked.shape[0] // rows

    @pl.when(pl.program_id(0) == 0)
    def _():
        for i in range(count):
            picked[i * rows : (i + 1) * rows] = turned_ref[pick_ref[half * count + i]]

    product = contract(picked[...], right_ref[0], 1, 0)
    refs = rest[1:-1] if added else rest[:-1]
    for i in range(count):
        piece = product[i * rows : (i + 1) * rows]
        if added:
            piece = piece + rest[0][i, 0].astype(F32)
        out = refs[0] if len(refs) == 1 else refs[i // 2]
        out[i if len(refs) == 1 else i % 2, 0] = piece.astype(BF16)


def share(pick, turned_rows, right, received=None):
    total, rows, seq = turned_rows.shape
    groups, _, cols = right.shape
    count = total // 2
    spec = lambda n: pl.BlockSpec((n, 1, rows, cols), lambda i, *_: (0, i, 0, 0))
    ins = [(turned_rows, whole(turned_rows.shape)), (right, nth(right.shape))]
    if received is None:
        sizes = [count]
    else:
        ins.append((received, spec(count)))
        sizes = [2] * (count // 2)
    return call(
        functools.partial(share_kernel, 1 if received is None else 0, received is not None),
        "share",
        groups,
        ins,
        [(struct((n, groups, rows, cols), BF16), spec(n)) for n in sizes],
        2 * groups * count * rows * seq * cols,
        [pltpu.VMEM((count * rows, seq), BF16)],
        (pick,),
    )


def swap(array, axis, bit):
    size = lax.axis_size(axis)
    return lax.ppermute(array, axis, [(i, i ^ bit) for i in range(size)])


def shares(pick, turned_rows, right, extra):
    away = share(pick, turned_rows, right)[0]
    kept = share(pick, turned_rows, right, swap(away, "gx", 1))
    mine = [kept[0][0].astype(F32), kept[0][1].astype(F32)]
    if len(kept) == 2:
        arrived = swap(kept[1], "dp", 1)
        mine = [mine[0] + arrived[0].astype(F32), mine[1] + arrived[1].astype(F32)]
    arrived = swap(mine[1].astype(BF16), "gx", 2)
    total = (mine[0] + arrived.astype(F32)).astype(BF16)
    groups, rows, cols = total.shape
    own = lax.psum_scatter(
        total.reshape(groups * rows, cols), "gy", scatter_dimension=0, tiled=True
    )
    if len(kept) == 2:
        own = lax.all_gather(own, "dp", axis=0, tiled=True).astype(F32)
    else:
        own = lax.psum(own.astype(F32), "dp")
    return own if extra == 1.0 else own * extra


def images_here(block, copies):
    rows = block.shape[0] * block.shape[1]
    images = block.reshape(rows // SEQ, SEQ, block.shape[2])
    if copies > 1:
        images = jnp.repeat(images, copies, axis=0)
    return lax.all_to_all(images, "gx", split_axis=0, concat_axis=0, tiled=True)


def images_back(parts, copies, shape):
    parts = lax.all_to_all(parts, "gx", split_axis=0, concat_axis=0, tiled=True)
    if copies > 1:
        parts = parts[::copies]
    return parts.reshape(shape)


def collect(block, order):
    return lax.all_gather(block, order, axis=0, tiled=True)


def on_device(
    tokens,
    cotangent,
    ln1_gain,
    ln1_bias,
    qkv_weight,
    qv_bias,
    out_weight,
    out_bias,
    ln2_gain,
    ln2_bias,
    fc1_weight,
    fc1_bias,
    fc2_weight,
    fc2_bias,
):
    gx = lax.axis_size("gx")
    gy = lax.axis_size("gy")
    halves = 2 if lax.axis_size("dp") == 2 else 1
    blocks = gx * halves
    shape = tokens.shape
    part = shape[2]
    head_cols = qkv_weight.shape[2]
    heads = head_cols // HEAD_DIM
    triple = 3 * head_cols
    hidden_cols = fc1_weight.shape[1]
    width = part * gx
    copies = gx // (MICRO * shape[1] // SEQ)
    extra = 1.0 / copies
    along = ("gy", "gx")

    column = lax.axis_index("gx")
    half = lax.axis_index("dp")
    pick = jnp.stack(
        [
            (column ^ (2 * far + core)) * halves + (half ^ side if halves == 2 else 0)
            for core in range(2)
            for side in range(halves)
            for far in range(2)
        ]
    ).astype(jnp.int32)

    wide = jnp.stack([ln1_gain, ln1_bias, out_bias, ln2_gain, ln2_bias, fc2_bias], axis=1)
    deep = jnp.concatenate([qv_bias[0], qv_bias[1], fc1_bias])
    deep_cols = -(-deep.shape[0] // part)
    deep = jnp.pad(deep, (0, deep_cols * part - deep.shape[0])).reshape(deep_cols, part).T
    whole_qkv = collect(
        jnp.concatenate([qkv_weight.reshape(part, triple), wide, deep], axis=1), along
    ).reshape(gy, width, triple + 6 + deep_cols)
    whole_out = collect(out_weight, ("gx", "gy")).reshape(gx, gy * head_cols, part)
    whole_out = jnp.concatenate([whole_out[i] for i in range(gx)], axis=1)
    whole_fc1 = collect(fc1_weight, along).reshape(gy, width, hidden_cols)
    whole_fc2 = collect(fc2_weight.T, along).reshape(gy, width, hidden_cols)

    wide = whole_qkv[0, :, triple : triple + 6].T.astype(F32)
    gain_one, shift_one, bias_mix, gain_two, shift_two, bias_second = [
        wide[i : i + 1] for i in range(6)
    ]
    deep = whole_qkv[:, :part, triple + 6 :].astype(F32)
    deep = jnp.swapaxes(deep, 1, 2).reshape(gy, 1, deep_cols * part)
    bias_qkv = jnp.concatenate(
        [
            deep[:, :, :head_cols],
            jnp.zeros((gy, 1, head_cols), F32),
            deep[:, :, head_cols : 2 * head_cols],
        ],
        axis=2,
    )
    bias_first = deep[:, :, 2 * head_cols : 2 * head_cols + hidden_cols]

    token_parts = images_here(tokens, copies)
    grad_parts = images_here(cotangent, copies)
    grad_low, grad_turned, grad_sum = spread(grad_parts, blocks)
    image, ready_one, turned_one, packed = project(
        token_parts, gain_one, shift_one, whole_qkv, bias_qkv, blocks
    )
    mixture, log_total = attend(packed, heads)
    hidden, ready_two, turned_two = mix(
        image, mixture, whole_out, bias_mix, gain_two, shift_two, blocks
    )
    active, slope = expand(ready_two, whole_fc1, bias_first)
    grad_fc2 = shares(pick, grad_turned, active, extra).T
    layer_out = images_back(narrow(hidden, active, whole_fc2, bias_second, gx), copies, shape)
    (
        grad_first,
        first_sum,
        grad_hidden,
        grad_hidden_low,
        turned_hidden,
        gain_two_sum,
        shift_two_sum,
        low_sum,
    ) = feed_back(grad_low, hidden, gain_two, slope, whole_fc2, whole_fc1, blocks)
    grad_fc1 = shares(pick, turned_two, grad_first, extra)
    grad_out_weight = shares(pick, turned_hidden, mixture, extra).T
    grad_mixture = mix_back(grad_hidden_low, whole_out, gy)
    grad_packed, packed_sum = attend_back(
        packed, jnp.swapaxes(log_total, 1, 2), grad_mixture, heads
    )
    grad_qkv = shares(pick, turned_one, grad_packed, extra)
    tokens_grad, gain_one_sum, shift_one_sum = project_back(
        image, gain_one, grad_hidden, grad_packed, whole_qkv, gx
    )
    tokens_grad = images_back(tokens_grad, copies, shape)

    wide_sums = jnp.concatenate(
        [gain_one_sum, shift_one_sum, low_sum, gain_two_sum, shift_two_sum, grad_sum]
    )
    deep_sums = jnp.concatenate(
        [packed_sum[:, 0, :head_cols], packed_sum[:, 0, 2 * head_cols :], first_sum[:, 0]], axis=1
    )
    wide_sums, deep_sums = lax.psum((wide_sums, deep_sums), ("dp", "gx", "gy"))
    wide_sums = extra * lax.dynamic_slice_in_dim(wide_sums, column * part, part, 1)
    deep_sums = extra * lax.dynamic_index_in_dim(deep_sums, lax.axis_index("gy"), 0, False)
    return (
        layer_out,
        tokens_grad,
        wide_sums[0],
        wide_sums[1],
        grad_qkv.reshape(part, 3, head_cols),
        deep_sums[: 2 * head_cols].reshape(2, head_cols),
        grad_out_weight,
        wide_sums[2],
        wide_sums[3],
        wide_sums[4],
        grad_fc1,
        deep_sums[2 * head_cols :],
        grad_fc2,
        wide_sums[5],
    )


def solution(mesh):
    specs = (
        P(None, ("dp", "gy"), "gx"),
        P(None, ("dp", "gy"), "gx"),
        P("gx"),
        P("gx"),
        P("gx", None, "gy"),
        P(None, "gy"),
        P("gy", "gx"),
        P("gx"),
        P("gx"),
        P("gx"),
        P("gx", "gy"),
        P("gy"),
        P("gy", "gx"),
        P("gx"),
    )
    return jax.shard_map(
        on_device,
        mesh=mesh,
        in_specs=specs,
        out_specs=specs,
        check_vma=False,
    )
```

```python
import functools

import jax
import jax.numpy as jnp
from jax import lax
from jax.experimental import pallas as pl
from jax.experimental.pallas import tpu as pltpu
from jax.sharding import PartitionSpec as P

HEAD_DIM = 72
SEQ = 729
MICRO = 2
EPSILON = 1e-06
QUERY_ROWS = 384
ROWS = 256
NEAR = 2
COST = 1
RING = False
COLS = 256
BF16 = jnp.bfloat16
F32 = jnp.float32
VMEM_BYTES = 60 * 2**20


def contract(left, right, left_dim, right_dim):
    return lax.dot_general(
        left, right, (((left_dim,), (right_dim,)), ((), ())), preferred_element_type=F32
    )


def blocks_of(total, size):
    return [(low, min(low + size, total)) for low in range(0, total, size)]


def whole(shape):
    return pl.BlockSpec(shape, lambda i, *_: (0,) * len(shape))


def nth(shape):
    return pl.BlockSpec((1,) + tuple(shape[1:]), lambda i, *_: (i,) + (0,) * (len(shape) - 1))


def call(kernel, name, steps, ins, outs, flops, scratch=(), prefetch=()):
    moved = sum(a.size * a.dtype.itemsize for a, _ in list(ins) + list(outs))
    return pl.pallas_call(
        kernel,
        grid_spec=pltpu.PrefetchScalarGridSpec(
            num_scalar_prefetch=len(prefetch),
            grid=(steps,),
            in_specs=[spec for _, spec in ins],
            out_specs=[spec for _, spec in outs],
            scratch_shapes=list(scratch),
        ),
        out_shape=[shape for shape, _ in outs],
        compiler_params=pltpu.CompilerParams(vmem_limit_bytes=VMEM_BYTES),
        cost_estimate=pl.CostEstimate(
            flops=flops * COST, bytes_accessed=moved * COST, transcendentals=0
        ),
        name=name,
    )(*prefetch, *[a for a, _ in ins])


def struct(shape, dtype):
    return jax.ShapeDtypeStruct(tuple(shape), dtype)


def attend_kernel(heads, packed_ref, mix_ref, total_ref):
    seq = packed_ref.shape[1]
    width = heads * HEAD_DIM
    scaling = HEAD_DIM ** (-0.5)
    for head in range(heads):
        first = head * HEAD_DIM
        last = first + HEAD_DIM
        keys = packed_ref[0, :, width + first : width + last]
        values = packed_ref[0, :, 2 * width + first : 2 * width + last]
        for low, high in blocks_of(seq, QUERY_ROWS):
            queries = packed_ref[0, low:high, first:last]
            scores = contract(queries, keys, 1, 1) * scaling
            row_max = jnp.max(scores, axis=1, keepdims=True)
            exponent = jnp.exp(scores - row_max)
            row_total = jnp.sum(exponent, axis=1, keepdims=True)
            probability = (exponent * (1.0 / row_total)).astype(BF16)
            mix_ref[0, low:high, first:last] = contract(probability, values, 1, 0).astype(BF16)
            total_ref[0, low:high, head : head + 1] = row_max + jnp.log(row_total)


def attend(packed, heads):
    groups, seq, _ = packed.shape
    mix = struct((groups, seq, heads * HEAD_DIM), BF16)
    total = struct((groups, seq, heads), F32)
    return call(
        functools.partial(attend_kernel, heads),
        "attend",
        groups,
        [(packed, nth(packed.shape))],
        [(mix, nth(mix.shape)), (total, nth(total.shape))],
        12 * groups * heads * seq * seq * HEAD_DIM,
    )


def attend_back_kernel(
    heads, some, packed_ref, total_ref, grad_ref, out_ref, sum_ref, key_sum, value_sum
):
    seq = packed_ref.shape[1]
    width = heads * HEAD_DIM
    part = len(some) * HEAD_DIM
    scaling = HEAD_DIM ** (-0.5)
    for place, head in enumerate(some):
        first = head * HEAD_DIM
        last = first + HEAD_DIM
        start = place * HEAD_DIM
        stop = start + HEAD_DIM
        keys = packed_ref[0, :, width + first : width + last]
        values = packed_ref[0, :, 2 * width + first : 2 * width + last]
        for low, high in blocks_of(seq, QUERY_ROWS):
            queries = packed_ref[0, low:high, first:last]
            grads = grad_ref[0, low:high, first:last]
            scores = contract(keys, queries, 1, 1) * scaling
            probability = jnp.exp(scores - total_ref[0, head : head + 1, low:high])
            grad_values = contract(probability.astype(BF16), grads, 1, 0)
            grad_prob = contract(values, grads, 1, 1)
            inner = jnp.sum(probability * grad_prob, axis=0, keepdims=True)
            grad_scores = (probability * (grad_prob - inner)).astype(BF16)
            grad_keys = contract(grad_scores, queries, 1, 0)
            grad_queries = contract(grad_scores, keys, 0, 0) * scaling
            out_ref[0, low:high, start:stop] = grad_queries.astype(BF16)
            if low == 0:
                key_sum[...] = grad_keys
                value_sum[...] = grad_values
            else:
                key_sum[...] += grad_keys
                value_sum[...] += grad_values
        out_ref[0, :, part + start : part + stop] = (key_sum[...] * scaling).astype(BF16)
        out_ref[0, :, 2 * part + start : 2 * part + stop] = value_sum[...].astype(BF16)
    sum_ref[0] = jnp.sum(out_ref[0].astype(F32), axis=0, keepdims=True)


def attend_back(packed, total, grads, heads, some):
    groups, seq, _ = packed.shape
    triple = 3 * len(some) * HEAD_DIM
    out = struct((groups, seq, triple), BF16)
    sums = struct((groups, 1, triple), F32)
    return call(
        functools.partial(attend_back_kernel, heads, some),
        "attend_back",
        groups,
        [(packed, nth(packed.shape)), (total, nth(total.shape)), (grads, nth(grads.shape))],
        [(out, nth(out.shape)), (sums, nth(sums.shape))],
        30 * groups * len(some) * seq * seq * HEAD_DIM,
        [pltpu.VMEM((seq, HEAD_DIM), F32), pltpu.VMEM((seq, HEAD_DIM), F32)],
    )


def norm(values):
    center = jnp.mean(values, axis=1, keepdims=True)
    shifted = values - center
    inverse = lax.rsqrt(jnp.mean(shifted * shifted, axis=1, keepdims=True) + EPSILON)
    return shifted * inverse, inverse


def norm_back(grad_norm, normed, inverse, gain):
    grad_hat = grad_norm * gain
    return inverse * (
        grad_hat
        - jnp.mean(grad_hat, axis=1, keepdims=True)
        - normed * jnp.mean(grad_hat * normed, axis=1, keepdims=True)
    )


def on_column(place_ref, count, body):
    for c in range(count):
        pl.when(place_ref[0] == c)(functools.partial(body, c))


def join_parts(place_ref, parts, blocks_ref):
    rows = blocks_ref.shape[1]
    each = parts[0].shape[0] // rows
    for r, ref in enumerate(parts):
        for i in range(each):
            blocks_ref[(place_ref[0] ^ r) * each + i] = ref[i * rows : (i + 1) * rows]


def flat(blocks_ref):
    count, rows, seq = blocks_ref.shape
    return blocks_ref[...].reshape(count * rows, seq)


def split_parts(place_ref, values, parts, blocks_ref):
    turned(values, blocks_ref)
    for r, ref in enumerate(parts):
        ref[...] = blocks_ref[place_ref[0] ^ r]


def join_columns(place_ref, groups, parts_ref, whole_ref):
    part = parts_ref.shape[2]
    for k in range(groups):
        whole_ref[:, k * part : (k + 1) * part] = parts_ref[order_of(place_ref, groups, k)]


def order_of(place_ref, groups, k):
    return place_ref[place_ref.shape[0] - groups + k]


def join_rows(place_ref, pieces, whole_ref, start, stop, k=0):
    for p, ref in enumerate(pieces):
        whole_ref[place_ref[1 + p], :, start:stop] = ref[k, :, : stop - start]


def turned(rows, blocks_ref):
    columns = rows.T
    count, size, _ = blocks_ref.shape
    for i in range(count):
        blocks_ref[i] = columns[i * size : (i + 1) * size]


def cut_kernel(copies, place_ref, rows_ref, *parts):
    seq = parts[0].shape[1]
    each = rows_ref.shape[2] // seq

    def body(c):
        for r, ref in enumerate(parts):
            image = (c ^ r) // copies
            start = (image % each) * seq
            ref[...] = rows_ref[image // each, :, start : start + seq]

    on_column(place_ref, len(parts), body)


def cut(spot, rows, count, copies):
    shape = struct((rows.shape[1], SEQ), BF16)
    return call(
        functools.partial(cut_kernel, copies),
        "cut",
        1,
        [(rows, whole(rows.shape))],
        [(shape, whole(shape.shape))] * count,
        0,
        prefetch=(spot,),
    )


def place_kernel(copies, place_ref, *refs):
    parts, rows_ref = refs[:-1], refs[-1]
    seq = parts[0].shape[1]
    each = rows_ref.shape[2] // seq

    def body(c):
        for image in range(len(parts) // copies):
            start = (image % each) * seq
            rows_ref[image // each, :, start : start + seq] = parts[c ^ (image * copies)][...]

    on_column(place_ref, len(parts), body)


def place(spot, parts, shape, copies):
    return call(
        functools.partial(place_kernel, copies),
        "place",
        1,
        [(a, whole(a.shape)) for a in parts],
        [(struct(shape, BF16), whole(shape))],
        0,
        prefetch=(spot,),
    )[0]


def spread_kernel(place_ref, *refs):
    parts = refs[:-3]
    whole_ref, turned_ref, sum_ref = refs[-3:]
    join_parts(place_ref, parts, turned_ref)
    whole_ref[...] = flat(turned_ref).T
    sum_ref[...] = jnp.sum(whole_ref[...].astype(F32), axis=0, keepdims=True)


def spread(spot, parts, blocks):
    part, seq = parts[0].shape
    width = len(parts) * part
    outs = [
        struct((seq, width), BF16),
        struct((blocks, width // blocks, seq), BF16),
        struct((1, width), F32),
    ]
    return call(
        spread_kernel,
        "spread",
        1,
        [(a, whole(a.shape)) for a in parts],
        [(o, whole(o.shape)) for o in outs],
        seq * width,
        prefetch=(spot,),
    )


def project_kernel(count, triple, place_ref, *refs):
    parts = refs[:count]
    gain_ref, shift_ref, weight_ref, bias_ref = refs[count : count + 4]
    image_ref, ready_ref, turned_ref, packed_ref = refs[count + 4 :]

    @pl.when(pl.program_id(0) == 0)
    def _():
        join_parts(place_ref, parts, turned_ref)
        image_ref[...] = flat(turned_ref).T
        for low, high in blocks_of(image_ref.shape[0], ROWS):
            normed, _ = norm(image_ref[low:high].astype(F32))
            ready_ref[low:high] = (normed * gain_ref[...] + shift_ref[...]).astype(BF16)
        turned(ready_ref[...], turned_ref)

    packed = contract(ready_ref[...], weight_ref[0, :, :triple], 1, 0) + bias_ref[0]
    packed_ref[0] = packed.astype(BF16)


def project(spot, parts, gain, shift, weight, bias, blocks):
    part, seq = parts[0].shape
    width = len(parts) * part
    groups, _, triple = bias.shape
    outs = [
        (struct((seq, width), BF16), whole((seq, width))),
        (struct((seq, width), BF16), whole((seq, width))),
        (struct((blocks, width // blocks, seq), BF16), whole((blocks, width // blocks, seq))),
        (struct((groups, seq, triple), BF16), nth((groups, seq, triple))),
    ]
    return call(
        functools.partial(project_kernel, len(parts), triple),
        "project",
        groups,
        [(a, whole(a.shape)) for a in parts]
        + [
            (gain, whole(gain.shape)),
            (shift, whole(shift.shape)),
            (weight, pl.BlockSpec((1, width, lanes(triple)), lambda i, *_: (i, 0, 0))),
            (bias, nth(bias.shape)),
        ],
        outs,
        2 * groups * seq * width * triple,
        prefetch=(spot,),
    )


def mix_kernel(count, groups, place_ref, image_ref, parts_ref, bias_ref, gain_ref, shift_ref, *refs):
    pieces = refs[:count]
    hidden_ref, ready_ref, turned_ref, weight_ref, joined, blocks = refs[count:]
    part = parts_ref.shape[2]
    join_columns(place_ref, groups, parts_ref, joined)
    for k in range(groups):
        join_rows(place_ref, pieces, blocks, k * part, (k + 1) * part, k)
    weight_ref[...] = flat(blocks)
    for low, high in blocks_of(image_ref.shape[0], ROWS):
        mixed = contract(joined[low:high], weight_ref[...], 1, 1) + bias_ref[...]
        hidden = image_ref[low:high].astype(F32) + mixed
        hidden_ref[low:high] = hidden
        normed, _ = norm(hidden)
        ready_ref[low:high] = (normed * gain_ref[...] + shift_ref[...]).astype(BF16)
    turned(ready_ref[...], turned_ref)


def mix(spot, image, parts, bias, gain, shift, pieces, blocks):
    seq, width = image.shape
    groups, _, part = parts.shape
    inner = groups * part
    size = lanes(part)
    spec = pl.BlockSpec(
        (groups, pieces[0].shape[1], size), lambda i, *_: (0, 0, pieces[0].shape[2] // size - 1)
    )
    outs = [
        struct((seq, width), F32),
        struct((seq, width), BF16),
        struct((blocks, width // blocks, seq), BF16),
        struct((width, inner), BF16),
    ]
    return call(
        functools.partial(mix_kernel, len(pieces), groups),
        "mix",
        1,
        [(a, whole(a.shape)) for a in (image, parts, bias, gain, shift)]
        + [(a, spec) for a in pieces],
        [(o, whole(o.shape)) for o in outs],
        2 * seq * width * inner,
        [pltpu.VMEM((seq, inner), BF16), pltpu.VMEM((blocks, width // blocks, inner), BF16)],
        (spot,),
    )


def expand_kernel(count, place_ref, ready_ref, bias_ref, *refs):
    pieces = refs[:count]
    active_ref, slope_ref, weight = refs[count:]
    bend = 0.7978845608028654
    cubic = 0.044715
    join_rows(place_ref, pieces, weight, 0, weight.shape[2])
    for low, high in blocks_of(active_ref.shape[2], COLS):
        right = weight[:, :, low:high].reshape(-1, high - low)
        first = contract(ready_ref[...], right, 1, 0) + bias_ref[0, :, low:high]
        square = first * first
        bent = jnp.tanh(bend * (first + cubic * (first * square)))
        half = 0.5 * (1.0 + bent)
        active_ref[0, :, low:high] = (first * half).astype(BF16)
        slope_ref[0, :, low:high] = half + (0.5 * bend) * first * (1.0 - bent * bent) * (
            1.0 + (3.0 * cubic) * square
        )


def near_piece(piece, size):
    return pl.BlockSpec((1, piece.shape[1], size), lambda i, *_: (i, 0, 0))


def ordered(groups, shape):
    zeros = (0,) * (len(shape) - 1)
    return pl.BlockSpec(
        (1,) + tuple(shape[1:]), lambda i, spot: (order_of(spot, groups, i),) + zeros
    )


def expand(spot, ready, bias, pieces, blocks):
    seq, width = ready.shape
    groups, _, cols = bias.shape
    shape = (groups, seq, cols)
    size = lanes(cols)
    return call(
        functools.partial(expand_kernel, len(pieces)),
        "expand",
        groups,
        [(ready, whole(ready.shape)), (bias, ordered(groups, bias.shape))]
        + [(a, near_piece(a, size)) for a in pieces],
        [(struct(shape, BF16), ordered(groups, shape)), (struct(shape, F32), ordered(groups, shape))],
        2 * groups * seq * width * cols,
        [pltpu.VMEM((blocks, width // blocks, size), BF16)],
        (spot,),
    )


def narrow_kernel(place_ref, hidden_ref, active_ref, weight_ref, bias_ref, *rest):
    parts = rest[:-2]
    total, blocks = rest[-2:]
    step = pl.program_id(0)
    term = contract(active_ref[0], weight_ref[0, :, : active_ref.shape[2]], 1, 1)

    @pl.when(step == 0)
    def _():
        total[...] = hidden_ref[...] + bias_ref[...] + term

    @pl.when(step > 0)
    def _():
        total[...] += term

    @pl.when(step == pl.num_programs(0) - 1)
    def _():
        split_parts(place_ref, total[...].astype(BF16), parts, blocks)


def narrow(spot, hidden, active, weight, bias, count):
    seq, width = hidden.shape
    groups, _, cols = active.shape
    shape = (width // count, seq)
    return call(
        narrow_kernel,
        "narrow",
        groups,
        [
            (hidden, whole(hidden.shape)),
            (active, nth(active.shape)),
            (weight, nth(weight.shape)),
            (bias, whole(bias.shape)),
        ],
        [(struct(shape, BF16), whole(shape))] * count,
        2 * groups * seq * width * cols,
        [pltpu.VMEM((seq, width), F32), pltpu.VMEM((count, width // count, seq), BF16)],
        (spot,),
    )


def feed_back_kernel(count, place_ref, grad_ref, hidden_ref, gain_ref, slope_ref, second_ref, *refs):
    pieces = refs[:count]
    (
        first_grad_ref,
        first_sum_ref,
        hidden_grad_ref,
        low_ref,
        turned_ref,
        gain_sum_ref,
        shift_sum_ref,
        low_sum_ref,
        total,
        weight,
    ) = refs[count:]
    step = pl.program_id(0)
    join_rows(place_ref, pieces, weight, 0, weight.shape[2])
    for low, high in blocks_of(slope_ref.shape[2], COLS):
        active_grad = contract(grad_ref[...], second_ref[0, :, low:high], 1, 0)
        first_grad = (active_grad * slope_ref[0, :, low:high]).astype(BF16)
        first_grad_ref[0, :, low:high] = first_grad
        first_sum_ref[0, :, low:high] = jnp.sum(first_grad.astype(F32), axis=0, keepdims=True)
    right = flat(weight)[:, : slope_ref.shape[2]]
    term = contract(first_grad_ref[0], right, 1, 1)

    @pl.when(step == 0)
    def _():
        total[...] = term

    @pl.when(step > 0)
    def _():
        total[...] += term

    @pl.when(step == pl.num_programs(0) - 1)
    def _():
        gain_sum = jnp.zeros(gain_sum_ref.shape, F32)
        shift_sum = jnp.zeros(gain_sum_ref.shape, F32)
        low_sum = jnp.zeros(gain_sum_ref.shape, F32)
        for low, high in blocks_of(total.shape[0], ROWS):
            normed, inverse = norm(hidden_ref[low:high])
            ready_grad = total[low:high]
            gain_sum += jnp.sum(ready_grad * normed, axis=0, keepdims=True)
            shift_sum += jnp.sum(ready_grad, axis=0, keepdims=True)
            hidden_grad = grad_ref[low:high].astype(F32) + norm_back(
                ready_grad, normed, inverse, gain_ref[...]
            )
            hidden_grad_ref[low:high] = hidden_grad
            rounded = hidden_grad.astype(BF16)
            low_ref[low:high] = rounded
            low_sum += jnp.sum(rounded.astype(F32), axis=0, keepdims=True)
        gain_sum_ref[...] = gain_sum
        shift_sum_ref[...] = shift_sum
        low_sum_ref[...] = low_sum
        turned(low_ref[...], turned_ref)


def feed_back(spot, grad, hidden, gain, slope, second, pieces, blocks):
    seq, width = hidden.shape
    groups, _, cols = slope.shape
    size = lanes(cols)
    row = struct((1, width), F32)
    outs = [
        (struct(slope.shape, BF16), ordered(groups, slope.shape)),
        (struct((groups, 1, cols), F32), ordered(groups, (groups, 1, cols))),
    ] + [
        (o, whole(o.shape))
        for o in (
            struct((seq, width), F32),
            struct((seq, width), BF16),
            struct((blocks, width // blocks, seq), BF16),
            row,
            row,
            row,
        )
    ]
    return call(
        functools.partial(feed_back_kernel, len(pieces)),
        "feed_back",
        groups,
        [
            (grad, whole(grad.shape)),
            (hidden, whole(hidden.shape)),
            (gain, whole(gain.shape)),
            (slope, ordered(groups, slope.shape)),
            (second, ordered(groups, second.shape)),
        ]
        + [(a, near_piece(a, size)) for a in pieces],
        outs,
        4 * groups * seq * width * cols,
        [pltpu.VMEM((seq, width), F32), pltpu.VMEM((blocks, width // blocks, size), BF16)],
        (spot,),
    )


def mix_back_kernel(groups, place_ref, grad_ref, weight_ref, out_ref):
    part = out_ref.shape[2]
    full = contract(grad_ref[...], weight_ref[...], 1, 0).astype(BF16)
    for k in range(groups):
        out_ref[order_of(place_ref, groups, k)] = full[:, k * part : (k + 1) * part]


def mix_back(spot, grad, weight, groups):
    seq, width = grad.shape
    shape = (groups, seq, weight.shape[1] // groups)
    return call(
        functools.partial(mix_back_kernel, groups),
        "mix_back",
        1,
        [(grad, whole(grad.shape)), (weight, whole(weight.shape))],
        [(struct(shape, BF16), whole(shape))],
        2 * seq * width * weight.shape[1],
        prefetch=(spot,),
    )[0]


def project_back_kernel(
    place_ref, image_ref, gain_ref, hidden_grad_ref, near_ref, far_ref, weight_ref, *rest
):
    parts = rest[:-5]
    gain_sum_ref, shift_sum_ref, total, joined, blocks = rest[-5:]
    step = pl.program_id(0)
    near = near_ref.shape[2] // 3
    far = far_ref.shape[2] // 3
    for i in range(3):
        start = i * (near + far)
        joined[:, start : start + near] = near_ref[0, :, i * near : (i + 1) * near]
        joined[:, start + near : start + near + far] = far_ref[0, :, i * far : (i + 1) * far]
    term = contract(joined[...], weight_ref[0, :, : joined.shape[1]], 1, 1)

    @pl.when(step == 0)
    def _():
        total[...] = term

    @pl.when(step > 0)
    def _():
        total[...] += term

    @pl.when(step == pl.num_programs(0) - 1)
    def _():
        gain_sum = jnp.zeros(gain_sum_ref.shape, F32)
        shift_sum = jnp.zeros(gain_sum_ref.shape, F32)
        for low, high in blocks_of(total.shape[0], ROWS):
            normed, inverse = norm(image_ref[low:high].astype(F32))
            ready_grad = total[low:high]
            gain_sum += jnp.sum(ready_grad * normed, axis=0, keepdims=True)
            shift_sum += jnp.sum(ready_grad, axis=0, keepdims=True)
            result = hidden_grad_ref[low:high] + norm_back(
                ready_grad, normed, inverse, gain_ref[...]
            )
            total[low:high] = result
        gain_sum_ref[...] = gain_sum
        shift_sum_ref[...] = shift_sum
        split_parts(place_ref, total[...].astype(BF16), parts, blocks)


def project_back(spot, image, gain, hidden_grad, near, far, weight, count):
    seq, width = image.shape
    groups = near.shape[0]
    triple = near.shape[2] + far.shape[2]
    shape = (width // count, seq)
    row = struct((1, width), F32)
    return call(
        project_back_kernel,
        "project_back",
        groups,
        [
            (image, whole(image.shape)),
            (gain, whole(gain.shape)),
            (hidden_grad, whole(hidden_grad.shape)),
            (near, nth(near.shape)),
            (far, nth(far.shape)),
            (weight, pl.BlockSpec((1, width, lanes(triple)), lambda i, *_: (i, 0, 0))),
        ],
        [(struct(shape, BF16), whole(shape))] * count
        + [(row, whole(row.shape)), (row, whole(row.shape))],
        2 * groups * seq * width * triple,
        [
            pltpu.VMEM((seq, width), F32),
            pltpu.VMEM((seq, triple), BF16),
            pltpu.VMEM((count, width // count, seq), BF16),
        ],
        (spot,),
    )


def share_kernel(half, added, pick_ref, turned_ref, right_ref, *rest):
    rows = turned_ref.shape[1]
    picked = rest[-1]
    count = picked.shape[0] // rows

    @pl.when(pl.program_id(0) == 0)
    def _():
        for i in range(count):
            picked[i * rows : (i + 1) * rows] = turned_ref[pick_ref[half * count + i]]

    product = contract(picked[...], right_ref[0], 1, 0)
    received = rest[:count] if added else ()
    outs = rest[len(received) : -1]
    for i in range(count):
        piece = product[i * rows : (i + 1) * rows]
        if added:
            piece = piece + received[i][0].astype(F32)
        if len(outs) == count:
            outs[i][0] = piece.astype(BF16)
        else:
            outs[i // 2][i % 2, 0] = piece.astype(BF16)


def share(pick, turned_rows, right, received=()):
    total, rows, seq = turned_rows.shape
    groups, _, cols = right.shape
    count = total // 2
    one = (struct((groups, rows, cols), BF16), nth((groups, rows, cols)))
    two = (
        struct((2, groups, rows, cols), BF16),
        pl.BlockSpec((2, 1, rows, cols), lambda i, *_: (0, i, 0, 0)),
    )
    return call(
        functools.partial(share_kernel, 0 if received else 1, bool(received)),
        "share",
        groups,
        [(turned_rows, whole(turned_rows.shape)), (right, nth(right.shape))]
        + [(a, nth(a.shape)) for a in received],
        [two] * (count // 2) if received else [one] * count,
        2 * groups * count * rows * seq * cols,
        [pltpu.VMEM((count * rows, seq), BF16)],
        (pick,),
    )


def swap(array, axis, bit):
    size = lax.axis_size(axis)
    return lax.ppermute(array, axis, [(i, i ^ bit) for i in range(size)])


def everyone(array):
    for axis in ("gx", "dp", "gy"):
        terms = [array] + [swap(array, axis, k) for k in range(1, lax.axis_size(axis))]
        while len(terms) > 1:
            terms = [a + b for a, b in zip(terms[::2], terms[1::2], strict=True)]
        array = terms[0]
    return array


class Sums:
    def __init__(self, line, pick, turned_rows, halves, half_first, ring=False):
        self.line = line
        self.pick = pick[half_first]
        self.rows = turned_rows
        self.halves = halves
        self.ring = ring
        steps = [("dp", 1), ("gx", 2)] if half_first else [("gx", 2), ("dp", 1)]
        self.steps = steps if halves == 2 else [None, ("gx", 2)]

    def away(self, right):
        self.right = right
        sent = self.line(lambda a: share(self.pick, a, right), self.rows)
        self.arrived = [swap(a, "gx", 1) for a in sent]

    def keep(self):
        kept = self.line(
            lambda a: share(self.pick, a, self.right, self.arrived), self.rows
        )
        self.kept = kept[0]
        if self.halves == 2:
            self.arrived = swap(kept[1], *self.steps[0])

    def mine(self, i, kept):
        value = kept[i].astype(F32)
        return value + self.arrived[i].astype(F32) if self.halves == 2 else value

    def send(self):
        sent = self.line(lambda a: self.mine(1, a).astype(BF16), self.kept)
        self.second = swap(sent, *self.steps[1])

    def total(self):
        total = self.line(
            lambda a: (self.mine(0, a) + self.second.astype(F32)).astype(BF16), self.kept
        )
        groups, rows, cols = total.shape
        if not self.ring:
            self.own = lax.psum_scatter(
                total.reshape(groups * rows, cols), "gy", scatter_dimension=0, tiled=True
            )
            return
        me = lax.axis_index("gy")
        up = [(i, (i + 1) % groups) for i in range(groups)]
        block = lambda k: lax.dynamic_index_in_dim(total, (me + groups - k) % groups, 0, False)
        running = block(1)
        for k in range(2, groups + 1):
            running = lax.ppermute(running, "gy", up)
            running = (running.astype(F32) + block(k % groups).astype(F32)).astype(BF16)
        self.own = running

    def trade(self):
        if self.halves == 2:
            self.own = self.line(lambda a: a, self.own)
            self.other = swap(self.own, "dp", 1)

    def end(self):
        if self.halves == 1:
            return lax.psum(self.own.astype(F32), "dp")
        other = self.other
        first = lax.axis_index("dp") == 0
        return jnp.concatenate(
            [jnp.where(first, self.own, other), jnp.where(first, other, self.own)], axis=0
        ).astype(F32)


class Line:
    def __init__(self):
        self.last = None

    def __call__(self, step, first):
        if self.last is not None:
            first = after(first, self.last)
        result = step(first)
        self.last = jax.tree.leaves(result)[0]
        return result


def after(value, *others):
    return lax.optimization_barrier((value,) + others)[0]


def traded(parts):
    return [part if r == 0 else swap(part, "gx", r) for r, part in enumerate(parts)]


class Pieces:
    def __init__(self, first, mixed, halves):
        rows = first.shape[0] // halves
        size = lanes(mixed.shape[1])
        start = -(-first.shape[1] // size) * size
        both = jnp.concatenate(
            [
                jnp.pad(first, ((0, 0), (0, start - first.shape[1]))),
                jnp.pad(mixed, ((0, 0), (0, size - mixed.shape[1]))),
            ],
            axis=1,
        )
        if halves == 2:
            both = lax.dynamic_slice_in_dim(both, lax.axis_index("dp") * rows, rows, 0)
        count = lax.axis_size("gy")
        up = [(i, (i + 1) % count) for i in range(count)]
        groups = [both]
        for _ in range(count - 1):
            groups.append(lax.ppermute(groups[-1], "gy", up))
        own = jnp.stack(groups)
        self.halves = halves
        self.near = [own, swap(own, "gx", 2)]
        if halves == 2:
            self.near.append(swap(own, "dp", 1))

    def middle(self, anchor):
        near = [after(piece, anchor) for piece in self.near]
        if self.halves == 2:
            self.near.append(swap(near[1], "dp", 1))
        self.far = [swap(piece, "gx", 1) for piece in near]

    def last(self, anchor):
        if self.halves == 2:
            self.far.append(swap(after(self.near[3], anchor), "gx", 1))
        return self.near + self.far


def lanes(cols):
    return -(-cols // 128) * 128


def collect(block, order):
    return lax.all_gather(block, order, axis=0, tiled=True)


def on_device(
    tokens,
    cotangent,
    ln1_gain,
    ln1_bias,
    qkv_weight,
    qv_bias,
    out_weight,
    out_bias,
    ln2_gain,
    ln2_bias,
    fc1_weight,
    fc1_bias,
    fc2_weight,
    fc2_bias,
):
    gx = lax.axis_size("gx")
    gy = lax.axis_size("gy")
    halves = 2 if lax.axis_size("dp") == 2 else 1
    blocks = gx * halves
    shape = tokens.shape
    turned_shape = (shape[0], shape[2], shape[1])
    part = shape[2]
    head_cols = qkv_weight.shape[2]
    heads = head_cols // HEAD_DIM
    triple = 3 * head_cols
    hidden_cols = fc1_weight.shape[1]
    width = part * gx
    copies = gx // (MICRO * shape[1] // SEQ)
    along = ("gy", "gx")

    column = lax.axis_index("gx")
    half = lax.axis_index("dp")

    def block(core, side, far):
        return (column ^ (2 * far + core)) * halves + (half ^ side if halves == 2 else 0)

    bits = range(halves)
    pick = {
        True: jnp.stack([block(c, s, f) for c in range(2) for s in bits for f in range(2)]),
        False: jnp.stack([block(c, s, f) for c in range(2) for f in range(2) for s in bits]),
    }
    here = lax.axis_index("gy")
    spot = jnp.concatenate(
        [
            jnp.reshape(column, (1,)),
            pick[True],
            (here + gy - jnp.arange(gy, dtype=jnp.int32)) % gy,
        ]
    ).astype(jnp.int32)
    line = Line()

    wide = jnp.stack([ln1_gain, ln1_bias, out_bias, ln2_gain, ln2_bias, fc2_bias], axis=1)
    deep = jnp.concatenate([qv_bias[0], qv_bias[1], fc1_bias])
    deep_cols = -(-deep.shape[0] // part)
    deep = jnp.pad(deep, (0, deep_cols * part - deep.shape[0])).reshape(deep_cols, part).T
    early = jnp.concatenate([qkv_weight.reshape(part, triple), wide, deep], axis=1)
    early_cols = lanes(early.shape[1])
    early = jnp.pad(early, ((0, 0), (0, early_cols - early.shape[1])))
    early = collect(early, along).reshape(gy, width, early_cols)
    second = jnp.pad(fc2_weight.T, ((0, 0), (0, lanes(hidden_cols) - hidden_cols)))
    second = collect(second, along).reshape(gy, width, lanes(hidden_cols))
    token_parts = cut(spot, jnp.swapaxes(tokens, 1, 2), gx, copies)
    gathered = Pieces(after(fc1_weight, token_parts[0]), out_weight.T, halves)
    token_parts = traded(token_parts)

    wide = early[0, :, triple : triple + 6].T.astype(F32)
    gain_one, shift_one, bias_mix, gain_two, shift_two, bias_second = [
        wide[i : i + 1] for i in range(6)
    ]
    deep = early[:, :part, triple + 6 : triple + 6 + deep_cols].astype(F32)
    deep = jnp.swapaxes(deep, 1, 2).reshape(gy, 1, deep_cols * part)
    bias_qkv = jnp.concatenate(
        [
            deep[:, :, :head_cols],
            jnp.zeros((gy, 1, head_cols), F32),
            deep[:, :, head_cols : 2 * head_cols],
        ],
        axis=2,
    )
    bias_first = deep[:, :, 2 * head_cols : 2 * head_cols + hidden_cols]

    image, ready_one, turned_one, packed = line(
        lambda a: project(spot, [a] + token_parts[1:], gain_one, shift_one, early, bias_qkv, blocks),
        token_parts[0],
    )
    grad_parts = line(lambda a: cut(spot, a, gx, copies), jnp.swapaxes(cotangent, 1, 2))
    grad_parts = traded(grad_parts)
    gathered.middle(packed)
    mixture, log_total = line(lambda a: attend(a, heads), packed)
    pieces = gathered.last(mixture)
    log_total = jnp.swapaxes(log_total, 1, 2)
    grad_low, grad_turned, grad_sum = line(
        lambda a: spread(spot, [a] + grad_parts[1:], blocks), grad_parts[0]
    )
    hidden, ready_two, turned_two, whole_out = line(
        lambda a: mix(spot, a, mixture, bias_mix, gain_two, shift_two, pieces, blocks), image
    )
    active, slope = line(lambda a: expand(spot, a, bias_first, pieces, blocks), ready_two)

    near = max(1, NEAR * heads // 4)
    fc2 = Sums(line, pick, grad_turned, halves, True)
    fc1 = Sums(line, pick, turned_two, halves, True)
    fc2.away(active)
    out_parts = line(lambda a: narrow(spot, a, active, second, bias_second, gx), hidden)
    out_parts = traded(out_parts)
    fc2.keep()
    (
        grad_first,
        first_sum,
        grad_hidden,
        grad_hidden_low,
        turned_hidden,
        gain_two_sum,
        shift_two_sum,
        low_sum,
    ) = line(
        lambda a: feed_back(spot, a, hidden, gain_two, slope, second, pieces, blocks), grad_low
    )
    out = Sums(line, pick, turned_hidden, halves, False)
    first_heads = Sums(line, pick, turned_one, halves, True)
    last_heads = Sums(line, pick, turned_one, halves, True, RING)
    fc1.away(grad_first)
    grad_mixture = line(lambda a: mix_back(spot, a, whole_out, gy), grad_hidden_low)
    fc1.keep()
    fc2.send()
    near_grad, near_sum = line(
        lambda a: attend_back(a, log_total, grad_mixture, heads, list(range(near))), packed
    )
    out.away(mixture)
    first_heads.away(near_grad)
    fc2.total()
    out.keep()
    first_heads.keep()
    fc1.send()
    fed_sums = everyone(
        line(
            lambda a: jnp.concatenate(
                [b.reshape(-1) for b in (a, gain_two_sum, shift_two_sum, grad_sum, first_sum)]
            ),
            low_sum,
        )
    )
    far_grad, far_sum = line(
        lambda a: attend_back(a, log_total, grad_mixture, heads, list(range(near, heads))), packed
    )
    out.send()
    last_heads.away(far_grad)
    first_heads.send()
    out.total()
    fc1.total()
    last_heads.keep()
    fc2.trade()
    first_heads.total()
    *grad_parts, gain_one_sum, shift_one_sum = line(
        lambda a: project_back(spot, a, gain_one, grad_hidden, near_grad, far_grad, early, gx), image
    )
    last_heads.send()
    grad_parts = traded(grad_parts)
    out.trade()
    fc1.trade()
    layer_out = line(
        lambda a: place(spot, [a] + out_parts[1:], turned_shape, copies), out_parts[0]
    )
    last_heads.total()
    first_heads.trade()
    tokens_grad = line(
        lambda a: place(spot, [a] + grad_parts[1:], turned_shape, copies), grad_parts[0]
    )
    last_heads.trade()
    grad_fc2 = fc2.end().T
    grad_fc1 = fc1.end()
    grad_out_weight = out.end().T
    grad_near = first_heads.end().reshape(part, 3, near * HEAD_DIM)
    grad_far = last_heads.end().reshape(part, 3, (heads - near) * HEAD_DIM)
    grad_qkv = jnp.concatenate([grad_near, grad_far], axis=2)

    near_sum = near_sum.reshape(gy, 3, near * HEAD_DIM)
    far_sum = far_sum.reshape(gy, 3, (heads - near) * HEAD_DIM)
    packed_sum = jnp.concatenate([near_sum, far_sum], axis=2)
    late_sums = everyone(
        jnp.concatenate(
            [a.reshape(-1) for a in (gain_one_sum, shift_one_sum, packed_sum[:, 0], packed_sum[:, 2])]
        )
    )
    wide_sums = jnp.concatenate([late_sums[: 2 * width], fed_sums[: 4 * width]]).reshape(6, width)
    wide_sums = lax.dynamic_slice_in_dim(wide_sums, column * part, part, 1)
    qv_sums = late_sums[2 * width :].reshape(2, gy, head_cols)
    qv_sums = lax.dynamic_index_in_dim(qv_sums, here, 1, False)
    first_sums = fed_sums[4 * width :].reshape(gy, hidden_cols)
    first_sums = lax.dynamic_index_in_dim(first_sums, here, 0, False)
    grads = (
        wide_sums[0],
        wide_sums[1],
        grad_qkv,
        qv_sums,
        grad_out_weight,
        wide_sums[2],
        wide_sums[3],
        wide_sums[4],
        grad_fc1,
        first_sums,
        grad_fc2,
        wide_sums[5],
    )
    if copies > 1:
        grads = tuple(grad * (1.0 / copies) for grad in grads)
    return (jnp.swapaxes(layer_out, 1, 2), jnp.swapaxes(tokens_grad, 1, 2)) + grads


def solution(mesh):
    specs = (
        P(None, ("dp", "gy"), "gx"),
        P(None, ("dp", "gy"), "gx"),
        P("gx"),
        P("gx"),
        P("gx", None, "gy"),
        P(None, "gy"),
        P("gy", "gx"),
        P("gx"),
        P("gx"),
        P("gx"),
        P("gx", "gy"),
        P("gy"),
        P("gy", "gx"),
        P("gx"),
    )
    return jax.shard_map(
        on_device,
        mesh=mesh,
        in_specs=specs,
        out_specs=specs,
        check_vma=False,
    )
```

```python
import functools

import jax
import jax.numpy as jnp
from jax import lax
from jax.experimental import pallas as pl
from jax.experimental.pallas import tpu as pltpu
from jax.sharding import PartitionSpec as P

HEAD_DIM = 72
SEQ = 729
MICRO = 2
EPSILON = 1e-06
QUERY_ROWS = 384
ROWS = 256
FC1 = True
OUT = False
COST = 1
COLS = 256
BF16 = jnp.bfloat16
F32 = jnp.float32
SLOPE = jnp.float32
VMEM_BYTES = 60 * 2**20


def contract(left, right, left_dim, right_dim):
    return lax.dot_general(
        left, right, (((left_dim,), (right_dim,)), ((), ())), preferred_element_type=F32
    )


def blocks_of(total, size):
    return [(low, min(low + size, total)) for low in range(0, total, size)]


def whole(shape):
    return pl.BlockSpec(shape, lambda i, *_: (0,) * len(shape))


def nth(shape):
    return pl.BlockSpec((1,) + tuple(shape[1:]), lambda i, *_: (i,) + (0,) * (len(shape) - 1))


def call(kernel, name, steps, ins, outs, flops, scratch=(), prefetch=()):
    moved = sum(a.size * a.dtype.itemsize for a, _ in list(ins) + list(outs))
    return pl.pallas_call(
        kernel,
        grid_spec=pltpu.PrefetchScalarGridSpec(
            num_scalar_prefetch=len(prefetch),
            grid=(steps,),
            in_specs=[spec for _, spec in ins],
            out_specs=[spec for _, spec in outs],
            scratch_shapes=list(scratch),
        ),
        out_shape=[shape for shape, _ in outs],
        compiler_params=pltpu.CompilerParams(vmem_limit_bytes=VMEM_BYTES),
        cost_estimate=pl.CostEstimate(
            flops=flops * COST, bytes_accessed=moved * COST, transcendentals=0
        ),
        name=name,
    )(*prefetch, *[a for a, _ in ins])


def struct(shape, dtype):
    return jax.ShapeDtypeStruct(tuple(shape), dtype)


def attend_kernel(heads, packed_ref, mix_ref, total_ref):
    seq = packed_ref.shape[1]
    width = heads * HEAD_DIM
    scaling = HEAD_DIM ** (-0.5)
    for head in range(heads):
        first = head * HEAD_DIM
        last = first + HEAD_DIM
        keys = packed_ref[0, :, width + first : width + last]
        values = packed_ref[0, :, 2 * width + first : 2 * width + last]
        for low, high in blocks_of(seq, QUERY_ROWS):
            queries = packed_ref[0, low:high, first:last]
            scores = contract(queries, keys, 1, 1) * scaling
            row_max = jnp.max(scores, axis=1, keepdims=True)
            exponent = jnp.exp(scores - row_max)
            row_total = jnp.sum(exponent, axis=1, keepdims=True)
            probability = (exponent * (1.0 / row_total)).astype(BF16)
            mix_ref[0, low:high, first:last] = contract(probability, values, 1, 0).astype(BF16)
            total_ref[0, low:high, head : head + 1] = row_max + jnp.log(row_total)


def attend(packed, heads):
    groups, seq, _ = packed.shape
    mix = struct((groups, seq, heads * HEAD_DIM), BF16)
    total = struct((groups, seq, heads), F32)
    return call(
        functools.partial(attend_kernel, heads),
        "attend",
        groups,
        [(packed, nth(packed.shape))],
        [(mix, nth(mix.shape)), (total, nth(total.shape))],
        12 * groups * heads * seq * seq * HEAD_DIM,
    )


def attend_back_kernel(
    heads, some, packed_ref, total_ref, grad_ref, out_ref, sum_ref, key_sum, value_sum
):
    seq = packed_ref.shape[1]
    width = heads * HEAD_DIM
    part = len(some) * HEAD_DIM
    scaling = HEAD_DIM ** (-0.5)
    for place, head in enumerate(some):
        first = head * HEAD_DIM
        last = first + HEAD_DIM
        start = place * HEAD_DIM
        stop = start + HEAD_DIM
        keys = packed_ref[0, :, width + first : width + last]
        values = packed_ref[0, :, 2 * width + first : 2 * width + last]
        for low, high in blocks_of(seq, QUERY_ROWS):
            queries = packed_ref[0, low:high, first:last]
            grads = grad_ref[0, low:high, first:last]
            scores = contract(keys, queries, 1, 1) * scaling
            probability = jnp.exp(scores - total_ref[0, head : head + 1, low:high])
            grad_values = contract(probability.astype(BF16), grads, 1, 0)
            grad_prob = contract(values, grads, 1, 1)
            inner = jnp.sum(probability * grad_prob, axis=0, keepdims=True)
            grad_scores = (probability * (grad_prob - inner)).astype(BF16)
            grad_keys = contract(grad_scores, queries, 1, 0)
            grad_queries = contract(grad_scores, keys, 0, 0) * scaling
            out_ref[0, low:high, start:stop] = grad_queries.astype(BF16)
            if low == 0:
                key_sum[...] = grad_keys
                value_sum[...] = grad_values
            else:
                key_sum[...] += grad_keys
                value_sum[...] += grad_values
        out_ref[0, :, part + start : part + stop] = (key_sum[...] * scaling).astype(BF16)
        out_ref[0, :, 2 * part + start : 2 * part + stop] = value_sum[...].astype(BF16)
    sum_ref[0] = jnp.sum(out_ref[0].astype(F32), axis=0, keepdims=True)


def attend_back(packed, total, grads, heads, some):
    groups, seq, _ = packed.shape
    triple = 3 * len(some) * HEAD_DIM
    out = struct((groups, seq, triple), BF16)
    sums = struct((groups, 1, triple), F32)
    return call(
        functools.partial(attend_back_kernel, heads, some),
        "attend_back",
        groups,
        [(packed, nth(packed.shape)), (total, nth(total.shape)), (grads, nth(grads.shape))],
        [(out, nth(out.shape)), (sums, nth(sums.shape))],
        30 * groups * len(some) * seq * seq * HEAD_DIM,
        [pltpu.VMEM((seq, HEAD_DIM), F32), pltpu.VMEM((seq, HEAD_DIM), F32)],
    )


def norm(values):
    center = jnp.mean(values, axis=1, keepdims=True)
    shifted = values - center
    inverse = lax.rsqrt(jnp.mean(shifted * shifted, axis=1, keepdims=True) + EPSILON)
    return shifted * inverse, inverse


def norm_back(grad_norm, normed, inverse, gain):
    grad_hat = grad_norm * gain
    return inverse * (
        grad_hat
        - jnp.mean(grad_hat, axis=1, keepdims=True)
        - normed * jnp.mean(grad_hat * normed, axis=1, keepdims=True)
    )


def on_column(place_ref, count, body):
    for c in range(count):
        pl.when(place_ref[0] == c)(functools.partial(body, c))


def join_parts(place_ref, parts, blocks_ref):
    rows = blocks_ref.shape[1]
    each = parts[0].shape[0] // rows
    for r, ref in enumerate(parts):
        for i in range(each):
            blocks_ref[(place_ref[0] ^ r) * each + i] = ref[i * rows : (i + 1) * rows]


def flat(blocks_ref):
    count, rows, seq = blocks_ref.shape
    return blocks_ref[...].reshape(count * rows, seq)


def split_parts(place_ref, values, parts, blocks_ref):
    turned(values, blocks_ref)
    for r, ref in enumerate(parts):
        ref[...] = blocks_ref[place_ref[0] ^ r]


def join_columns(parts_ref, whole_ref):
    groups, _, part = parts_ref.shape
    for k in range(groups):
        whole_ref[:, k * part : (k + 1) * part] = parts_ref[k]


def order_of(place_ref, groups, k):
    return place_ref[place_ref.shape[0] - groups + k]


def join_rows(place_ref, pieces, whole_ref):
    for p, ref in enumerate(pieces):
        whole_ref[place_ref[1 + p]] = ref[0]


def turned(rows, blocks_ref):
    columns = rows.T
    count, size, _ = blocks_ref.shape
    for i in range(count):
        blocks_ref[i] = columns[i * size : (i + 1) * size]


def cut_kernel(copies, place_ref, rows_ref, *parts):
    seq = parts[0].shape[1]
    each = rows_ref.shape[2] // seq

    def body(c):
        for r, ref in enumerate(parts):
            image = (c ^ r) // copies
            start = (image % each) * seq
            ref[...] = rows_ref[image // each, :, start : start + seq]

    on_column(place_ref, len(parts), body)


def cut(spot, rows, count, copies):
    shape = struct((rows.shape[1], SEQ), BF16)
    return call(
        functools.partial(cut_kernel, copies),
        "cut",
        1,
        [(rows, whole(rows.shape))],
        [(shape, whole(shape.shape))] * count,
        0,
        prefetch=(spot,),
    )


def place_kernel(copies, place_ref, *refs):
    parts, rows_ref = refs[:-1], refs[-1]
    seq = parts[0].shape[1]
    each = rows_ref.shape[2] // seq

    def body(c):
        for image in range(len(parts) // copies):
            start = (image % each) * seq
            rows_ref[image // each, :, start : start + seq] = parts[c ^ (image * copies)][...]

    on_column(place_ref, len(parts), body)


def place(spot, parts, shape, copies):
    return call(
        functools.partial(place_kernel, copies),
        "place",
        1,
        [(a, whole(a.shape)) for a in parts],
        [(struct(shape, BF16), whole(shape))],
        0,
        prefetch=(spot,),
    )[0]


def spread_kernel(place_ref, *refs):
    parts = refs[:-3]
    whole_ref, turned_ref, sum_ref = refs[-3:]
    join_parts(place_ref, parts, turned_ref)
    whole_ref[...] = flat(turned_ref).T
    sum_ref[...] = jnp.sum(whole_ref[...].astype(F32), axis=0, keepdims=True)


def spread(spot, parts, blocks):
    part, seq = parts[0].shape
    width = len(parts) * part
    outs = [
        struct((seq, width), BF16),
        struct((blocks, width // blocks, seq), BF16),
        struct((1, width), F32),
    ]
    return call(
        spread_kernel,
        "spread",
        1,
        [(a, whole(a.shape)) for a in parts],
        [(o, whole(o.shape)) for o in outs],
        seq * width,
        prefetch=(spot,),
    )


def project_kernel(count, triple, place_ref, *refs):
    parts = refs[:count]
    weight_ref = refs[count]
    image_ref, ready_ref, turned_ref, packed_ref, wide_ref, first_ref = refs[count + 1 :]
    part = parts[0].shape[0]
    third = triple // 3
    start = triple // 128 * 128
    notes = weight_ref[0, :, start:].astype(F32).T[triple - start :]

    @pl.when(pl.program_id(0) == 0)
    def _():
        wide_ref[0:6] = notes[0:6]
        join_parts(place_ref, parts, turned_ref)
        image_ref[...] = flat(turned_ref).T
        for low, high in blocks_of(image_ref.shape[0], ROWS):
            normed, _ = norm(image_ref[low:high].astype(F32))
            ready_ref[low:high] = (normed * notes[0:1] + notes[1:2]).astype(BF16)
        turned(ready_ref[...], turned_ref)

    for i, (low, high) in enumerate(blocks_of(first_ref.shape[2], part)):
        first_ref[0, :, low:high] = notes[8 + i : 9 + i, : high - low]
    product = contract(ready_ref[...], weight_ref[0, :, :triple], 1, 0)
    packed_ref[0, :, :third] = (product[:, :third] + notes[6:7, :third]).astype(BF16)
    packed_ref[0, :, third : 2 * third] = product[:, third : 2 * third].astype(BF16)
    packed_ref[0, :, 2 * third :] = (product[:, 2 * third :] + notes[7:8, :third]).astype(BF16)


def project(spot, parts, weight, triple, cols, blocks):
    part, seq = parts[0].shape
    width = len(parts) * part
    groups = weight.shape[0]
    outs = [
        (struct((seq, width), BF16), whole((seq, width))),
        (struct((seq, width), BF16), whole((seq, width))),
        (struct((blocks, width // blocks, seq), BF16), whole((blocks, width // blocks, seq))),
        (struct((groups, seq, triple), BF16), nth((groups, seq, triple))),
        (struct((8, width), F32), whole((8, width))),
        (struct((groups, 1, cols), F32), nth((groups, 1, cols))),
    ]
    return call(
        functools.partial(project_kernel, len(parts), triple),
        "project",
        groups,
        [(a, whole(a.shape)) for a in parts]
        + [(weight, pl.BlockSpec((1, width, lanes(triple)), lambda i, *_: (i, 0, 0)))],
        outs,
        2 * groups * seq * width * triple,
        prefetch=(spot,),
    )


def mix_kernel(count, image_ref, parts_ref, wide_ref, *refs):
    strips = refs[:count]
    hidden_ref, ready_ref, turned_ref, weight_ref, joined = refs[count:]
    groups, _, part = parts_ref.shape
    join_columns(parts_ref, joined)
    for strip, (low, high) in zip(strips, blocks_of(part, 128), strict=True):
        for k in range(groups):
            weight_ref[:, k * part + low : k * part + high] = strip[k, :, : high - low]
    for low, high in blocks_of(image_ref.shape[0], ROWS):
        mixed = contract(joined[low:high], weight_ref[...], 1, 1) + wide_ref[2:3]
        hidden = image_ref[low:high].astype(F32) + mixed
        hidden_ref[low:high] = hidden
        normed, _ = norm(hidden)
        ready_ref[low:high] = (normed * wide_ref[3:4] + wide_ref[4:5]).astype(BF16)
    turned(ready_ref[...], turned_ref)


def mix(image, parts, wide, weight, start, blocks):
    seq, width = image.shape
    groups, _, part = parts.shape
    inner = groups * part
    strips = [
        pl.BlockSpec((groups, width, 128), lambda i, *_, at=at: (0, 0, at))
        for at in range(start // 128, start // 128 + len(blocks_of(part, 128)))
    ]
    outs = [
        struct((seq, width), F32),
        struct((seq, width), BF16),
        struct((blocks, width // blocks, seq), BF16),
        struct((width, inner), BF16),
    ]
    return call(
        functools.partial(mix_kernel, len(strips)),
        "mix",
        1,
        [(a, whole(a.shape)) for a in (image, parts, wide)] + [(weight, strip) for strip in strips],
        [(o, whole(o.shape)) for o in outs],
        2 * seq * width * inner,
        [pltpu.VMEM((seq, inner), BF16)],
    )


def expand_kernel(count, place_ref, ready_ref, bias_ref, *refs):
    pieces = refs[:count]
    active_ref, slope_ref, weight = refs[count:]
    bend = 0.7978845608028654
    cubic = 0.044715
    join_rows(place_ref, pieces, weight)
    for low, high in blocks_of(active_ref.shape[2], COLS):
        right = weight[:, :, low:high].reshape(-1, high - low)
        first = contract(ready_ref[...], right, 1, 0) + bias_ref[0, :, low:high]
        square = first * first
        bent = jnp.tanh(bend * (first + cubic * (first * square)))
        half = 0.5 * (1.0 + bent)
        active_ref[0, :, low:high] = (first * half).astype(BF16)
        slope = half + (0.5 * bend) * first * (1.0 - bent * bent) * (1.0 + (3.0 * cubic) * square)
        slope_ref[0, :, low:high] = slope.astype(SLOPE)


def near_piece(piece, size):
    return pl.BlockSpec((1, piece.shape[1], size), lambda i, *_: (i, 0, 0))


def ordered(groups, shape):
    zeros = (0,) * (len(shape) - 1)
    return pl.BlockSpec(
        (1,) + tuple(shape[1:]), lambda i, spot: (order_of(spot, groups, i),) + zeros
    )


def expand(spot, ready, bias, pieces, blocks):
    seq, width = ready.shape
    groups, _, cols = bias.shape
    shape = (groups, seq, cols)
    size = lanes(cols)
    return call(
        functools.partial(expand_kernel, len(pieces)),
        "expand",
        groups,
        [(ready, whole(ready.shape)), (bias, ordered(groups, bias.shape))]
        + [(a, near_piece(a, size)) for a in pieces],
        [(struct(shape, BF16), ordered(groups, shape)), (struct(shape, SLOPE), ordered(groups, shape))],
        2 * groups * seq * width * cols,
        [pltpu.VMEM((blocks, width // blocks, size), BF16)],
        (spot,),
    )


def narrow_kernel(place_ref, hidden_ref, active_ref, weight_ref, bias_ref, *rest):
    parts = rest[:-2]
    total, blocks = rest[-2:]
    step = pl.program_id(0)
    term = contract(active_ref[0], weight_ref[0, :, : active_ref.shape[2]], 1, 1)

    @pl.when(step == 0)
    def _():
        total[...] = hidden_ref[...] + bias_ref[5:6] + term

    @pl.when(step > 0)
    def _():
        total[...] += term

    @pl.when(step == pl.num_programs(0) - 1)
    def _():
        split_parts(place_ref, total[...].astype(BF16), parts, blocks)


def narrow(spot, hidden, active, weight, bias, count):
    seq, width = hidden.shape
    groups, _, cols = active.shape
    shape = (width // count, seq)
    return call(
        narrow_kernel,
        "narrow",
        groups,
        [
            (hidden, whole(hidden.shape)),
            (active, nth(active.shape)),
            (weight, nth(weight.shape)),
            (bias, whole(bias.shape)),
        ],
        [(struct(shape, BF16), whole(shape))] * count,
        2 * groups * seq * width * cols,
        [pltpu.VMEM((seq, width), F32), pltpu.VMEM((count, width // count, seq), BF16)],
        (spot,),
    )


def feed_back_kernel(
    count, place_ref, grad_ref, sum_ref, hidden_ref, gain_ref, slope_ref, second_ref, *refs
):
    pieces = refs[:count]
    (
        first_grad_ref,
        hidden_grad_ref,
        low_ref,
        turned_ref,
        sums_ref,
        total,
        weight,
        firsts,
    ) = refs[count:]
    step = pl.program_id(0)
    groups = place_ref.shape[0] - 1 - count
    place = order_of(place_ref, groups, step)
    join_rows(place_ref, pieces, weight)
    for low, high in blocks_of(slope_ref.shape[2], COLS):
        active_grad = contract(grad_ref[...], second_ref[0, :, low:high], 1, 0)
        first_grad = (active_grad * slope_ref[0, :, low:high].astype(F32)).astype(BF16)
        first_grad_ref[0, :, low:high] = first_grad
        firsts[place, :, low:high] = jnp.sum(first_grad.astype(F32), axis=0, keepdims=True)
    right = flat(weight)[:, : slope_ref.shape[2]]
    term = contract(first_grad_ref[0], right, 1, 1)

    @pl.when(step == 0)
    def _():
        total[...] = term

    @pl.when(step > 0)
    def _():
        total[...] += term

    @pl.when(step == pl.num_programs(0) - 1)
    def _():
        gain_sum = jnp.zeros((1, total.shape[1]), F32)
        shift_sum = gain_sum
        low_sum = gain_sum
        for low, high in blocks_of(total.shape[0], ROWS):
            normed, inverse = norm(hidden_ref[low:high])
            ready_grad = total[low:high]
            gain_sum += jnp.sum(ready_grad * normed, axis=0, keepdims=True)
            shift_sum += jnp.sum(ready_grad, axis=0, keepdims=True)
            hidden_grad = grad_ref[low:high].astype(F32) + norm_back(
                ready_grad, normed, inverse, gain_ref[3:4]
            )
            hidden_grad_ref[low:high] = hidden_grad
            rounded = hidden_grad.astype(BF16)
            low_ref[low:high] = rounded
            low_sum += jnp.sum(rounded.astype(F32), axis=0, keepdims=True)
        sums_ref[...] = jnp.zeros(sums_ref.shape, F32)
        for k in range(groups):
            sums_ref[4 + k : 5 + k, : firsts.shape[2]] = firsts[k]
        sums_ref[0:1] = low_sum
        sums_ref[1:2] = gain_sum
        sums_ref[2:3] = shift_sum
        sums_ref[3:4] = sum_ref[...]
        turned(low_ref[...], turned_ref)


def feed_back(spot, grad, grad_sum, hidden, gain, slope, second, pieces, blocks):
    seq, width = hidden.shape
    groups, _, cols = slope.shape
    size = lanes(cols)
    rows = -(-(4 + groups) // 8) * 8
    outs = [(struct(slope.shape, BF16), ordered(groups, slope.shape))] + [
        (o, whole(o.shape))
        for o in (
            struct((seq, width), F32),
            struct((seq, width), BF16),
            struct((blocks, width // blocks, seq), BF16),
            struct((rows, width), F32),
        )
    ]
    return call(
        functools.partial(feed_back_kernel, len(pieces)),
        "feed_back",
        groups,
        [
            (grad, whole(grad.shape)),
            (grad_sum, whole(grad_sum.shape)),
            (hidden, whole(hidden.shape)),
            (gain, whole(gain.shape)),
            (slope, ordered(groups, slope.shape)),
            (second, ordered(groups, second.shape)),
        ]
        + [(a, near_piece(a, size)) for a in pieces],
        outs,
        4 * groups * seq * width * cols,
        [
            pltpu.VMEM((seq, width), F32),
            pltpu.VMEM((blocks, width // blocks, size), BF16),
            pltpu.VMEM((groups, 1, cols), F32),
        ],
        (spot,),
    )


def mix_back_kernel(grad_ref, weight_ref, out_ref):
    groups, _, part = out_ref.shape
    full = contract(grad_ref[...], weight_ref[...], 1, 0).astype(BF16)
    for k in range(groups):
        out_ref[k] = full[:, k * part : (k + 1) * part]


def mix_back(grad, weight, groups):
    seq, width = grad.shape
    shape = (groups, seq, weight.shape[1] // groups)
    return call(
        mix_back_kernel,
        "mix_back",
        1,
        [(grad, whole(grad.shape)), (weight, whole(weight.shape))],
        [(struct(shape, BF16), whole(shape))],
        2 * seq * width * weight.shape[1],
    )[0]


def project_back_kernel(
    place_ref,
    image_ref,
    gain_ref,
    hidden_grad_ref,
    packed_ref,
    packed_sum_ref,
    weight_ref,
    *rest,
):
    parts = rest[:-3]
    sums_ref, total, blocks = rest[-3:]
    step = pl.program_id(0)
    term = contract(packed_ref[0], weight_ref[0, :, : packed_ref.shape[2]], 1, 1)

    @pl.when(step == 0)
    def _():
        total[...] = term

    @pl.when(step > 0)
    def _():
        total[...] += term

    @pl.when(step == pl.num_programs(0) - 1)
    def _():
        sums_ref[...] = jnp.zeros(sums_ref.shape, F32)
        gain_sum = jnp.zeros((1, total.shape[1]), F32)
        shift_sum = gain_sum
        for low, high in blocks_of(total.shape[0], ROWS):
            normed, inverse = norm(image_ref[low:high].astype(F32))
            ready_grad = total[low:high]
            gain_sum += jnp.sum(ready_grad * normed, axis=0, keepdims=True)
            shift_sum += jnp.sum(ready_grad, axis=0, keepdims=True)
            result = hidden_grad_ref[low:high] + norm_back(
                ready_grad, normed, inverse, gain_ref[0:1]
            )
            total[low:high] = result
        sums_ref[0:1] = gain_sum
        sums_ref[1:2] = shift_sum
        for k in range(packed_sum_ref.shape[0]):
            sums_ref[2 + k : 3 + k, : packed_ref.shape[2]] = packed_sum_ref[k]
        split_parts(place_ref, total[...].astype(BF16), parts, blocks)


def project_back(spot, image, gain, hidden_grad, packed_grad, packed_sum, weight, count):
    seq, width = image.shape
    groups, _, triple = packed_grad.shape
    shape = (width // count, seq)
    sums = struct((-(-(2 + groups) // 8) * 8, width), F32)
    return call(
        project_back_kernel,
        "project_back",
        groups,
        [
            (image, whole(image.shape)),
            (gain, whole(gain.shape)),
            (hidden_grad, whole(hidden_grad.shape)),
            (packed_grad, nth(packed_grad.shape)),
            (packed_sum, whole(packed_sum.shape)),
            (weight, pl.BlockSpec((1, width, lanes(triple)), lambda i, *_: (i, 0, 0))),
        ],
        [(struct(shape, BF16), whole(shape))] * count
        + [(sums, whole(sums.shape))],
        2 * groups * seq * width * triple,
        [
            pltpu.VMEM((seq, width), F32),
            pltpu.VMEM((count, width // count, seq), BF16),
        ],
        (spot,),
    )


def share_kernel(half, cuts, pick_ref, turned_ref, right_ref, *rest):
    rows = turned_ref.shape[1]
    picked = rest[-1]
    count = picked.shape[0] // rows

    @pl.when(pl.program_id(0) == 0)
    def _():
        for i in range(count):
            picked[i * rows : (i + 1) * rows] = turned_ref[pick_ref[1 + half * count + i]]

    product = contract(picked[...], right_ref[0], 1, 0)
    if not cuts:
        for i in range(count):
            rest[i][0] = product[i * rows : (i + 1) * rows].astype(BF16)
        return
    received, outs = rest[:count], rest[count:-1]
    each = len(outs) // len(cuts)
    for i in range(count):
        piece = product[i * rows : (i + 1) * rows] + received[i][0].astype(F32)
        for n, (low, high, side_first) in enumerate(cuts):
            place = (i // 2, i % 2) if side_first else (i % 2, i // 2)
            outs[n * each + place[0]][place[1], 0] = piece[:, low:high].astype(BF16)


def share(spot, turned_rows, right, received=(), cuts=()):
    total, rows, seq = turned_rows.shape
    groups, _, cols = right.shape
    count = total // 2

    def two(size):
        return (
            struct((2, groups, rows, size), BF16),
            pl.BlockSpec((2, 1, rows, size), lambda i, *_: (0, i, 0, 0)),
        )

    if received:
        outs = [two(high - low) for low, high, _ in cuts for _ in range(count // 2)]
    else:
        outs = [(struct((groups, rows, cols), BF16), nth((groups, rows, cols)))] * count
    return call(
        functools.partial(share_kernel, 0 if received else 1, cuts),
        "share",
        groups,
        [(turned_rows, whole(turned_rows.shape)), (right, nth(right.shape))]
        + [(a, nth(a.shape)) for a in received],
        outs,
        2 * groups * count * rows * seq * cols,
        [pltpu.VMEM((count * rows, seq), BF16)],
        (spot,),
    )


def swap(array, axis, bit):
    size = lax.axis_size(axis)
    return lax.ppermute(array, axis, [(i, i ^ bit) for i in range(size)])


def everyone(array):
    for axis in ("gx", "dp", "gy"):
        terms = [array] + [swap(array, axis, k) for k in range(1, lax.axis_size(axis))]
        while len(terms) > 1:
            terms = [a + b for a, b in zip(terms[::2], terms[1::2], strict=True)]
        array = terms[0]
    return array


class Sums:
    def __init__(self, line, spot, turned_rows, right, halves, *cuts):
        self.line = line
        self.spot = spot
        self.rows = turned_rows
        self.right = right
        self.halves = halves
        if halves == 1:
            cuts = [(0, right.shape[2], True)]
        self.cuts = [Cut(line, halves, *cut) for cut in cuts]

    def away(self):
        sent = self.line(lambda a: share(self.spot, a, self.right), self.rows)
        self.arrived = [swap(a, "gx", 1) for a in sent]

    def keep(self):
        cuts = [(cut.low, cut.high, cut.side_first) for cut in self.cuts]
        kept = self.line(
            lambda a: share(self.spot, a, self.right, self.arrived, cuts), self.rows
        )
        each = len(kept) // len(cuts)
        for n, cut in enumerate(self.cuts):
            cut.begin(kept[n * each : (n + 1) * each])

    def send(self):
        for cut in self.cuts:
            cut.send()

    def total(self):
        for cut in self.cuts:
            cut.total()


class Cut:
    def __init__(self, line, halves, low, high, side_first):
        self.line = line
        self.low = low
        self.high = high
        self.side_first = side_first
        steps = [("dp", 1), ("gx", 2)] if side_first else [("gx", 2), ("dp", 1)]
        self.steps = steps if halves == 2 else [None, ("gx", 2)]

    def begin(self, kept):
        self.kept = kept[0]
        self.arrived = swap(kept[1], *self.steps[0]) if len(kept) == 2 else None

    def mine(self, i, kept):
        value = kept[i].astype(F32)
        return value if self.arrived is None else value + self.arrived[i].astype(F32)

    def send(self):
        sent = self.line(lambda a: self.mine(1, a).astype(BF16), self.kept)
        self.second = swap(sent, *self.steps[1])

    def total(self):
        self.sum = self.line(
            lambda a: (self.mine(0, a) + self.second.astype(F32)).astype(BF16), self.kept
        )


class Shared:
    def __init__(self, line, halves, *weights):
        sums = [cut for weight in weights for cut in weight.cuts]
        self.line = line
        self.halves = halves
        self.cols = [one.sum.shape[2] for one in sums]
        groups, rows, _ = sums[0].sum.shape
        wide = [jnp.pad(a.sum, ((0, 0), (0, 0), (0, lanes(c) - c))) for a, c in zip(sums, self.cols)]
        wide = line(lambda a: jnp.concatenate([a] + wide[1:], axis=2), wide[0])
        self.own = lax.psum_scatter(
            wide.reshape(groups * rows, wide.shape[2]), "gy", scatter_dimension=0, tiled=True
        )

    def trade(self):
        if self.halves == 2:
            self.own = self.line(lambda a: a, self.own)
            self.other = swap(self.own, "dp", 1)

    def end(self):
        if self.halves == 1:
            full = lax.psum(self.own.astype(F32), "dp")
        else:
            first = lax.axis_index("dp") == 0
            low = jnp.where(first, self.own, self.other)
            high = jnp.where(first, self.other, self.own)
            full = jnp.concatenate([low, high], axis=0).astype(F32)
        starts = [sum(lanes(c) for c in self.cols[:i]) for i in range(len(self.cols))]
        return [full[:, start : start + c] for start, c in zip(starts, self.cols)]


class Line:
    def __init__(self):
        self.last = None

    def __call__(self, step, first):
        if self.last is not None:
            first = after(first, self.last)
        result = step(first)
        self.last = jax.tree.leaves(result)[0]
        return result


def after(value, *others):
    return lax.optimization_barrier((value,) + others)[0]


def traded(parts):
    return [part if r == 0 else swap(part, "gx", r) for r, part in enumerate(parts)]


class Pieces:
    def __init__(self, weight, halves):
        rows = weight.shape[0] // halves
        cols = weight.shape[1]
        both = jnp.pad(weight, ((0, 0), (0, lanes(cols) - cols)))
        if halves == 2:
            both = lax.dynamic_slice_in_dim(both, lax.axis_index("dp") * rows, rows, 0)
        count = lax.axis_size("gy")
        up = [(i, (i + 1) % count) for i in range(count)]
        groups = [both]
        for _ in range(count - 1):
            groups.append(lax.ppermute(groups[-1], "gy", up))
        own = jnp.stack(groups)
        self.halves = halves
        self.near = [own, swap(own, "gx", 2)]
        if halves == 2:
            self.near.append(swap(own, "dp", 1))

    def middle(self, anchor):
        near = [after(piece, anchor) for piece in self.near]
        if self.halves == 2:
            self.near.append(swap(near[1], "dp", 1))
        self.far = [swap(piece, "gx", 1) for piece in near]

    def last(self, anchor):
        if self.halves == 2:
            self.far.append(swap(after(self.near[3], anchor), "gx", 1))
        return self.near + self.far


def lanes(cols):
    return -(-cols // 128) * 128


def collect(block, order):
    return lax.all_gather(block, order, axis=0, tiled=True)


def on_device(
    tokens,
    cotangent,
    ln1_gain,
    ln1_bias,
    qkv_weight,
    qv_bias,
    out_weight,
    out_bias,
    ln2_gain,
    ln2_bias,
    fc1_weight,
    fc1_bias,
    fc2_weight,
    fc2_bias,
):
    gx = lax.axis_size("gx")
    gy = lax.axis_size("gy")
    halves = 2 if lax.axis_size("dp") == 2 else 1
    blocks = gx * halves
    shape = tokens.shape
    turned_shape = (shape[0], shape[2], shape[1])
    part = shape[2]
    head_cols = qkv_weight.shape[2]
    heads = head_cols // HEAD_DIM
    triple = 3 * head_cols
    hidden_cols = fc1_weight.shape[1]
    width = part * gx
    copies = gx // (MICRO * shape[1] // SEQ)
    along = ("gy", "gx")

    column = lax.axis_index("gx")
    half = lax.axis_index("dp")

    def block(core, side, far):
        return (column ^ (2 * far + core)) * halves + (half ^ side if halves == 2 else 0)

    pick = [block(c, s, f) for c in range(2) for s in range(halves) for f in range(2)]
    here = lax.axis_index("gy")
    spot = jnp.concatenate(
        [
            jnp.reshape(column, (1,)),
            jnp.stack(pick),
            (here + gy - jnp.arange(gy, dtype=jnp.int32)) % gy,
        ]
    ).astype(jnp.int32)
    line = Line()

    early = [qkv_weight.reshape(part, triple)]
    early += [a[:, None] for a in (ln1_gain, ln1_bias, out_bias, ln2_gain, ln2_bias, fc2_bias)]
    for vector in (qv_bias[0], qv_bias[1], fc1_bias):
        count = -(-vector.shape[0] // part)
        vector = jnp.pad(vector, (0, count * part - vector.shape[0]))
        early.append(vector.reshape(count, part).T)
    early = jnp.concatenate(early, axis=1)
    early_cols = lanes(early.shape[1])
    early = jnp.concatenate(
        [
            jnp.pad(early, ((0, 0), (0, early_cols - early.shape[1]))),
            jnp.pad(out_weight.T, ((0, 0), (0, lanes(head_cols) - head_cols))),
        ],
        axis=1,
    )
    early = collect(early, along).reshape(gy, width, early.shape[1])
    second = jnp.pad(fc2_weight.T, ((0, 0), (0, lanes(hidden_cols) - hidden_cols)))
    second = collect(second, along).reshape(gy, width, lanes(hidden_cols))
    token_parts = cut(spot, jnp.swapaxes(tokens, 1, 2), gx, copies)
    line.last = token_parts[0]
    grad_parts = line(lambda a: cut(spot, a, gx, copies), jnp.swapaxes(cotangent, 1, 2))
    gathered = Pieces(after(fc1_weight, token_parts[0]), halves)
    token_parts = traded(token_parts)

    image, ready_one, turned_one, packed, wide, bias_first = line(
        lambda a: project(spot, [a] + token_parts[1:], early, triple, hidden_cols, blocks),
        token_parts[0],
    )
    gathered.middle(packed)
    grad_parts = traded([after(a, packed) for a in grad_parts])
    mixture, log_total = line(lambda a: attend(a, heads), packed)
    pieces = gathered.last(mixture)
    log_total = jnp.swapaxes(log_total, 1, 2)
    hidden, ready_two, turned_two, whole_out = line(
        lambda a: mix(a, mixture, wide, early, early_cols, blocks), image
    )
    active, slope = line(lambda a: expand(spot, a, bias_first, pieces, blocks), ready_two)
    grad_low, grad_turned, grad_sum = line(
        lambda a: spread(spot, [a] + grad_parts[1:], blocks), grad_parts[0]
    )

    fc2 = Sums(line, spot, grad_turned, active, halves, (0, hidden_cols, True))
    fc2.away()
    out_parts = line(lambda a: narrow(spot, a, active, second, wide, gx), hidden)
    out_parts = traded(out_parts)
    fc2.keep()
    (
        grad_first,
        grad_hidden,
        grad_hidden_low,
        turned_hidden,
        fed_sums,
    ) = line(
        lambda a: feed_back(spot, a, grad_sum, hidden, wide, slope, second, pieces, blocks), grad_low
    )
    fc1 = Sums(line, spot, turned_two, grad_first, halves, (0, hidden_cols, FC1))
    out = Sums(line, spot, turned_hidden, mixture, halves, (0, head_cols, OUT))
    layer_out = line(
        lambda a: place(spot, [a] + out_parts[1:], turned_shape, copies), out_parts[0]
    )
    fc1.away()
    grad_mixture = line(lambda a: mix_back(a, whole_out, gy), grad_hidden_low)
    fc1.keep()
    fc2.send()
    packed_grad, packed_sum = line(
        lambda a: attend_back(a, log_total, grad_mixture, heads, list(range(heads))), packed
    )
    middle = max(1, triple // 256) * 128
    qkv = Sums(
        line, spot, turned_one, packed_grad, halves, (0, middle, True), (middle, triple, False)
    )
    qkv.away()
    out.away()
    fc2.total()
    fc2_end = Shared(line, halves, fc2)
    fc1.send()
    qkv.keep()
    out.keep()
    fed_sums = everyone(line(lambda a: a, fed_sums))
    fc1.total()
    fc1_end = Shared(line, halves, fc1)
    *grad_parts, late_sums = line(
        lambda a: project_back(spot, a, wide, grad_hidden, packed_grad, packed_sum, early, gx),
        image,
    )
    qkv.send()
    out.send()
    grad_parts = traded(grad_parts)
    late_sums = everyone(line(lambda a: a, late_sums))
    fc2_end.trade()
    qkv.total()
    out.total()
    last_end = Shared(line, halves, out, qkv)
    fc1_end.trade()
    last_end.trade()
    tokens_grad = line(
        lambda a: place(spot, [a] + grad_parts[1:], turned_shape, copies), grad_parts[0]
    )
    grad_fc2 = fc2_end.end()[0].T
    grad_fc1 = fc1_end.end()[0]
    grad_out_weight, *grad_qkv = last_end.end()
    grad_out_weight = grad_out_weight.T
    grad_qkv = jnp.concatenate(grad_qkv, axis=1).reshape(part, 3, head_cols)

    first_sums = lax.dynamic_index_in_dim(fed_sums, 4 + here, 0, False)[:hidden_cols]
    qv_sums = lax.dynamic_index_in_dim(late_sums, 2 + here, 0, False)
    qv_sums = qv_sums[:triple].reshape(3, head_cols)[::2]
    wide_sums = jnp.concatenate([late_sums[:2], fed_sums[:4]])
    wide_sums = lax.dynamic_slice_in_dim(wide_sums, column * part, part, 1)
    grads = (
        wide_sums[0],
        wide_sums[1],
        grad_qkv,
        qv_sums,
        grad_out_weight,
        wide_sums[2],
        wide_sums[3],
        wide_sums[4],
        grad_fc1,
        first_sums,
        grad_fc2,
        wide_sums[5],
    )
    if copies > 1:
        grads = tuple(grad * (1.0 / copies) for grad in grads)
    return (jnp.swapaxes(layer_out, 1, 2), jnp.swapaxes(tokens_grad, 1, 2)) + grads


def solution(mesh):
    specs = (
        P(None, ("dp", "gy"), "gx"),
        P(None, ("dp", "gy"), "gx"),
        P("gx"),
        P("gx"),
        P("gx", None, "gy"),
        P(None, "gy"),
        P("gy", "gx"),
        P("gx"),
        P("gx"),
        P("gx"),
        P("gx", "gy"),
        P("gy"),
        P("gy", "gx"),
        P("gx"),
    )
    return jax.shard_map(
        on_device,
        mesh=mesh,
        in_specs=specs,
        out_specs=specs,
        check_vma=False,
    )
```

```python
import functools

import jax
import jax.numpy as jnp
from jax import lax
from jax.experimental import pallas as pl
from jax.experimental.pallas import tpu as pltpu
from jax.sharding import PartitionSpec as P

HEAD_DIM = 72
SEQ = 729
MICRO = 2
EPSILON = 1e-06
QUERY_ROWS = 384
ROWS = 256
COST = 1
CUT = 8
COLS = 256
BF16 = jnp.bfloat16
F32 = jnp.float32
SLOPE = jnp.float32
VMEM_BYTES = 60 * 2**20


def contract(left, right, left_dim, right_dim):
    return lax.dot_general(
        left, right, (((left_dim,), (right_dim,)), ((), ())), preferred_element_type=F32
    )


def blocks_of(total, size):
    return [(low, min(low + size, total)) for low in range(0, total, size)]


def whole(shape):
    return pl.BlockSpec(shape, lambda i, *_: (0,) * len(shape))


def nth(shape):
    return pl.BlockSpec((1,) + tuple(shape[1:]), lambda i, *_: (i,) + (0,) * (len(shape) - 1))


def call(kernel, name, steps, ins, outs, flops, scratch=(), prefetch=()):
    moved = sum(a.size * a.dtype.itemsize for a, _ in list(ins) + list(outs))
    return pl.pallas_call(
        kernel,
        grid_spec=pltpu.PrefetchScalarGridSpec(
            num_scalar_prefetch=len(prefetch),
            grid=(steps,),
            in_specs=[spec for _, spec in ins],
            out_specs=[spec for _, spec in outs],
            scratch_shapes=list(scratch),
        ),
        out_shape=[shape for shape, _ in outs],
        compiler_params=pltpu.CompilerParams(vmem_limit_bytes=VMEM_BYTES),
        cost_estimate=pl.CostEstimate(
            flops=flops * COST, bytes_accessed=moved * COST, transcendentals=0
        ),
        name=name,
    )(*prefetch, *[a for a, _ in ins])


def struct(shape, dtype):
    return jax.ShapeDtypeStruct(tuple(shape), dtype)


def attend_kernel(heads, packed_ref, mix_ref, total_ref):
    seq = packed_ref.shape[1]
    width = heads * HEAD_DIM
    scaling = HEAD_DIM ** (-0.5)
    for head in range(heads):
        first = head * HEAD_DIM
        last = first + HEAD_DIM
        keys = packed_ref[0, :, width + first : width + last]
        values = packed_ref[0, :, 2 * width + first : 2 * width + last]
        for low, high in blocks_of(seq, QUERY_ROWS):
            queries = packed_ref[0, low:high, first:last]
            scores = contract(queries, keys, 1, 1) * scaling
            row_max = jnp.max(scores, axis=1, keepdims=True)
            exponent = jnp.exp(scores - row_max)
            row_total = jnp.sum(exponent, axis=1, keepdims=True)
            probability = (exponent * (1.0 / row_total)).astype(BF16)
            mix_ref[0, low:high, first:last] = contract(probability, values, 1, 0).astype(BF16)
            total_ref[0, low:high, head : head + 1] = row_max + jnp.log(row_total)


def attend(packed, heads):
    groups, seq, _ = packed.shape
    mix = struct((groups, seq, heads * HEAD_DIM), BF16)
    total = struct((groups, seq, heads), F32)
    return call(
        functools.partial(attend_kernel, heads),
        "attend",
        groups,
        [(packed, nth(packed.shape))],
        [(mix, nth(mix.shape)), (total, nth(total.shape))],
        12 * groups * heads * seq * seq * HEAD_DIM,
    )


def attend_back_kernel(
    heads, some, packed_ref, total_ref, grad_ref, out_ref, sum_ref, key_sum, value_sum
):
    seq = packed_ref.shape[1]
    width = heads * HEAD_DIM
    part = len(some) * HEAD_DIM
    scaling = HEAD_DIM ** (-0.5)
    for place, head in enumerate(some):
        first = head * HEAD_DIM
        last = first + HEAD_DIM
        start = place * HEAD_DIM
        stop = start + HEAD_DIM
        keys = packed_ref[0, :, width + first : width + last]
        values = packed_ref[0, :, 2 * width + first : 2 * width + last]
        for low, high in blocks_of(seq, QUERY_ROWS):
            queries = packed_ref[0, low:high, first:last]
            grads = grad_ref[0, low:high, first:last]
            scores = contract(keys, queries, 1, 1) * scaling
            probability = jnp.exp(scores - total_ref[0, head : head + 1, low:high])
            grad_values = contract(probability.astype(BF16), grads, 1, 0)
            grad_prob = contract(values, grads, 1, 1)
            inner = jnp.sum(probability * grad_prob, axis=0, keepdims=True)
            grad_scores = (probability * (grad_prob - inner)).astype(BF16)
            grad_keys = contract(grad_scores, queries, 1, 0)
            grad_queries = contract(grad_scores, keys, 0, 0) * scaling
            out_ref[0, low:high, start:stop] = grad_queries.astype(BF16)
            if low == 0:
                key_sum[...] = grad_keys
                value_sum[...] = grad_values
            else:
                key_sum[...] += grad_keys
                value_sum[...] += grad_values
        out_ref[0, :, part + start : part + stop] = (key_sum[...] * scaling).astype(BF16)
        out_ref[0, :, 2 * part + start : 2 * part + stop] = value_sum[...].astype(BF16)
    sum_ref[0] = jnp.sum(out_ref[0].astype(F32), axis=0, keepdims=True)


def attend_back(packed, total, grads, heads, some):
    groups, seq, _ = packed.shape
    triple = 3 * len(some) * HEAD_DIM
    out = struct((groups, seq, triple), BF16)
    sums = struct((groups, 1, triple), F32)
    return call(
        functools.partial(attend_back_kernel, heads, some),
        "attend_back",
        groups,
        [(packed, nth(packed.shape)), (total, nth(total.shape)), (grads, nth(grads.shape))],
        [(out, nth(out.shape)), (sums, nth(sums.shape))],
        30 * groups * len(some) * seq * seq * HEAD_DIM,
        [pltpu.VMEM((seq, HEAD_DIM), F32), pltpu.VMEM((seq, HEAD_DIM), F32)],
    )


def norm(values):
    center = jnp.mean(values, axis=1, keepdims=True)
    shifted = values - center
    inverse = lax.rsqrt(jnp.mean(shifted * shifted, axis=1, keepdims=True) + EPSILON)
    return shifted * inverse, inverse


def norm_back(grad_norm, normed, inverse, gain):
    grad_hat = grad_norm * gain
    return inverse * (
        grad_hat
        - jnp.mean(grad_hat, axis=1, keepdims=True)
        - normed * jnp.mean(grad_hat * normed, axis=1, keepdims=True)
    )


def on_column(place_ref, count, body):
    for c in range(count):
        pl.when(place_ref[0] == c)(functools.partial(body, c))


def join_parts(place_ref, parts, blocks_ref):
    rows = blocks_ref.shape[1]
    each = parts[0].shape[0] // rows
    for r, ref in enumerate(parts):
        for i in range(each):
            blocks_ref[(place_ref[0] ^ r) * each + i] = ref[i * rows : (i + 1) * rows]


def flat(blocks_ref):
    count, rows, seq = blocks_ref.shape
    return blocks_ref[...].reshape(count * rows, seq)


def split_parts(place_ref, values, parts, blocks_ref):
    turned(values, blocks_ref)
    for r, ref in enumerate(parts):
        ref[...] = blocks_ref[place_ref[0] ^ r]


def join_columns(parts_ref, whole_ref):
    groups, _, part = parts_ref.shape
    for k in range(groups):
        whole_ref[:, k * part : (k + 1) * part] = parts_ref[k]


def order_of(place_ref, groups, k):
    return place_ref[place_ref.shape[0] - groups + k]


def join_rows(place_ref, pieces, whole_ref):
    for p, ref in enumerate(pieces):
        whole_ref[place_ref[1 + p]] = ref[0]


def turned(rows, blocks_ref):
    columns = rows.T
    count, size, _ = blocks_ref.shape
    for i in range(count):
        blocks_ref[i] = columns[i * size : (i + 1) * size]


def cut_kernel(copies, place_ref, rows_ref, *parts):
    seq = parts[0].shape[1]
    each = rows_ref.shape[2] // seq

    def body(c):
        for r, ref in enumerate(parts):
            image = (c ^ r) // copies
            start = (image % each) * seq
            ref[...] = rows_ref[image // each, :, start : start + seq]

    on_column(place_ref, len(parts), body)


def cut(spot, rows, count, copies):
    shape = struct((rows.shape[1], SEQ), BF16)
    return call(
        functools.partial(cut_kernel, copies),
        "cut",
        1,
        [(rows, whole(rows.shape))],
        [(shape, whole(shape.shape))] * count,
        0,
        prefetch=(spot,),
    )


def place_kernel(copies, place_ref, *refs):
    parts, rows_ref = refs[:-1], refs[-1]
    seq = parts[0].shape[1]
    each = rows_ref.shape[2] // seq

    def body(c):
        for image in range(len(parts) // copies):
            start = (image % each) * seq
            rows_ref[image // each, :, start : start + seq] = parts[c ^ (image * copies)][...]

    on_column(place_ref, len(parts), body)


def place(spot, parts, shape, copies):
    return call(
        functools.partial(place_kernel, copies),
        "place",
        1,
        [(a, whole(a.shape)) for a in parts],
        [(struct(shape, BF16), whole(shape))],
        0,
        prefetch=(spot,),
    )[0]


def spread_kernel(place_ref, *refs):
    parts = refs[:-3]
    whole_ref, turned_ref, sum_ref = refs[-3:]
    join_parts(place_ref, parts, turned_ref)
    whole_ref[...] = flat(turned_ref).T
    sum_ref[...] = jnp.sum(whole_ref[...].astype(F32), axis=0, keepdims=True)


def spread(spot, parts, blocks):
    part, seq = parts[0].shape
    width = len(parts) * part
    outs = [
        struct((seq, width), BF16),
        struct((blocks, width // blocks, seq), BF16),
        struct((1, width), F32),
    ]
    return call(
        spread_kernel,
        "spread",
        1,
        [(a, whole(a.shape)) for a in parts],
        [(o, whole(o.shape)) for o in outs],
        seq * width,
        prefetch=(spot,),
    )


def project_kernel(count, triple, place_ref, *refs):
    parts = refs[:count]
    weight_ref = refs[count]
    image_ref, ready_ref, turned_ref, packed_ref, wide_ref, first_ref = refs[count + 1 :]
    part = parts[0].shape[0]
    third = triple // 3
    start = triple // 128 * 128
    notes = weight_ref[0, :, start:].astype(F32).T[triple - start :]

    @pl.when(pl.program_id(0) == 0)
    def _():
        wide_ref[0:6] = notes[0:6]
        join_parts(place_ref, parts, turned_ref)
        image_ref[...] = flat(turned_ref).T
        for low, high in blocks_of(image_ref.shape[0], ROWS):
            normed, _ = norm(image_ref[low:high].astype(F32))
            ready_ref[low:high] = (normed * notes[0:1] + notes[1:2]).astype(BF16)
        turned(ready_ref[...], turned_ref)

    for i, (low, high) in enumerate(blocks_of(first_ref.shape[2], part)):
        first_ref[0, :, low:high] = notes[8 + i : 9 + i, : high - low]
    product = contract(ready_ref[...], weight_ref[0, :, :triple], 1, 0)
    packed_ref[0, :, :third] = (product[:, :third] + notes[6:7, :third]).astype(BF16)
    packed_ref[0, :, third : 2 * third] = product[:, third : 2 * third].astype(BF16)
    packed_ref[0, :, 2 * third :] = (product[:, 2 * third :] + notes[7:8, :third]).astype(BF16)


def project(spot, parts, weight, triple, cols, blocks):
    part, seq = parts[0].shape
    width = len(parts) * part
    groups = weight.shape[0]
    outs = [
        (struct((seq, width), BF16), whole((seq, width))),
        (struct((seq, width), BF16), whole((seq, width))),
        (struct((blocks, width // blocks, seq), BF16), whole((blocks, width // blocks, seq))),
        (struct((groups, seq, triple), BF16), nth((groups, seq, triple))),
        (struct((8, width), F32), whole((8, width))),
        (struct((groups, 1, cols), F32), nth((groups, 1, cols))),
    ]
    return call(
        functools.partial(project_kernel, len(parts), triple),
        "project",
        groups,
        [(a, whole(a.shape)) for a in parts]
        + [(weight, pl.BlockSpec((1, width, lanes(triple)), lambda i, *_: (i, 0, 0)))],
        outs,
        2 * groups * seq * width * triple,
        prefetch=(spot,),
    )


def mix_kernel(count, image_ref, parts_ref, wide_ref, *refs):
    strips = refs[:count]
    hidden_ref, ready_ref, turned_ref, weight_ref, joined = refs[count:]
    groups, _, part = parts_ref.shape
    join_columns(parts_ref, joined)
    for strip, (low, high) in zip(strips, blocks_of(part, 128), strict=True):
        for k in range(groups):
            weight_ref[:, k * part + low : k * part + high] = strip[k, :, : high - low]
    for low, high in blocks_of(image_ref.shape[0], ROWS):
        mixed = contract(joined[low:high], weight_ref[...], 1, 1) + wide_ref[2:3]
        hidden = image_ref[low:high].astype(F32) + mixed
        hidden_ref[low:high] = hidden
        normed, _ = norm(hidden)
        ready_ref[low:high] = (normed * wide_ref[3:4] + wide_ref[4:5]).astype(BF16)
    turned(ready_ref[...], turned_ref)


def mix(image, parts, wide, weight, start, blocks):
    seq, width = image.shape
    groups, _, part = parts.shape
    inner = groups * part
    strips = [
        pl.BlockSpec((groups, width, 128), lambda i, *_, at=at: (0, 0, at))
        for at in range(start // 128, start // 128 + len(blocks_of(part, 128)))
    ]
    outs = [
        struct((seq, width), F32),
        struct((seq, width), BF16),
        struct((blocks, width // blocks, seq), BF16),
        struct((width, inner), BF16),
    ]
    return call(
        functools.partial(mix_kernel, len(strips)),
        "mix",
        1,
        [(a, whole(a.shape)) for a in (image, parts, wide)] + [(weight, strip) for strip in strips],
        [(o, whole(o.shape)) for o in outs],
        2 * seq * width * inner,
        [pltpu.VMEM((seq, inner), BF16)],
    )


def expand_kernel(count, place_ref, ready_ref, bias_ref, *refs):
    pieces = refs[:count]
    active_ref, slope_ref, weight = refs[count:]
    bend = 0.7978845608028654
    cubic = 0.044715
    join_rows(place_ref, pieces, weight)
    for low, high in blocks_of(active_ref.shape[2], COLS):
        right = weight[:, :, low:high].reshape(-1, high - low)
        first = contract(ready_ref[...], right, 1, 0) + bias_ref[0, :, low:high]
        square = first * first
        bent = jnp.tanh(bend * (first + cubic * (first * square)))
        half = 0.5 * (1.0 + bent)
        active_ref[0, :, low:high] = (first * half).astype(BF16)
        slope = half + (0.5 * bend) * first * (1.0 - bent * bent) * (1.0 + (3.0 * cubic) * square)
        slope_ref[0, :, low:high] = slope.astype(SLOPE)


def near_piece(piece, size):
    return pl.BlockSpec((1, piece.shape[1], size), lambda i, *_: (i, 0, 0))


def ordered(groups, shape):
    zeros = (0,) * (len(shape) - 1)
    return pl.BlockSpec(
        (1,) + tuple(shape[1:]), lambda i, spot: (order_of(spot, groups, i),) + zeros
    )


def expand(spot, ready, bias, pieces, blocks):
    seq, width = ready.shape
    groups, _, cols = bias.shape
    shape = (groups, seq, cols)
    size = lanes(cols)
    return call(
        functools.partial(expand_kernel, len(pieces)),
        "expand",
        groups,
        [(ready, whole(ready.shape)), (bias, ordered(groups, bias.shape))]
        + [(a, near_piece(a, size)) for a in pieces],
        [(struct(shape, BF16), ordered(groups, shape)), (struct(shape, SLOPE), ordered(groups, shape))],
        2 * groups * seq * width * cols,
        [pltpu.VMEM((blocks, width // blocks, size), BF16)],
        (spot,),
    )


def narrow_kernel(place_ref, hidden_ref, active_ref, weight_ref, bias_ref, *rest):
    parts = rest[:-2]
    total, blocks = rest[-2:]
    step = pl.program_id(0)
    term = contract(active_ref[0], weight_ref[0, :, : active_ref.shape[2]], 1, 1)

    @pl.when(step == 0)
    def _():
        total[...] = hidden_ref[...] + bias_ref[5:6] + term

    @pl.when(step > 0)
    def _():
        total[...] += term

    @pl.when(step == pl.num_programs(0) - 1)
    def _():
        split_parts(place_ref, total[...].astype(BF16), parts, blocks)


def narrow(spot, hidden, active, weight, bias, count):
    seq, width = hidden.shape
    groups, _, cols = active.shape
    shape = (width // count, seq)
    return call(
        narrow_kernel,
        "narrow",
        groups,
        [
            (hidden, whole(hidden.shape)),
            (active, nth(active.shape)),
            (weight, nth(weight.shape)),
            (bias, whole(bias.shape)),
        ],
        [(struct(shape, BF16), whole(shape))] * count,
        2 * groups * seq * width * cols,
        [pltpu.VMEM((seq, width), F32), pltpu.VMEM((count, width // count, seq), BF16)],
        (spot,),
    )


def feed_back_kernel(
    count, place_ref, grad_ref, sum_ref, hidden_ref, gain_ref, slope_ref, second_ref, *refs
):
    pieces = refs[:count]
    (
        first_grad_ref,
        hidden_grad_ref,
        low_ref,
        turned_ref,
        sums_ref,
        total,
        weight,
        firsts,
    ) = refs[count:]
    step = pl.program_id(0)
    groups = place_ref.shape[0] - 1 - count
    place = order_of(place_ref, groups, step)
    join_rows(place_ref, pieces, weight)
    for low, high in blocks_of(slope_ref.shape[2], COLS):
        active_grad = contract(grad_ref[...], second_ref[0, :, low:high], 1, 0)
        first_grad = (active_grad * slope_ref[0, :, low:high].astype(F32)).astype(BF16)
        first_grad_ref[0, :, low:high] = first_grad
        firsts[place, :, low:high] = jnp.sum(first_grad.astype(F32), axis=0, keepdims=True)
    right = flat(weight)[:, : slope_ref.shape[2]]
    term = contract(first_grad_ref[0], right, 1, 1)

    @pl.when(step == 0)
    def _():
        total[...] = term

    @pl.when(step > 0)
    def _():
        total[...] += term

    @pl.when(step == pl.num_programs(0) - 1)
    def _():
        gain_sum = jnp.zeros((1, total.shape[1]), F32)
        shift_sum = gain_sum
        low_sum = gain_sum
        for low, high in blocks_of(total.shape[0], ROWS):
            normed, inverse = norm(hidden_ref[low:high])
            ready_grad = total[low:high]
            gain_sum += jnp.sum(ready_grad * normed, axis=0, keepdims=True)
            shift_sum += jnp.sum(ready_grad, axis=0, keepdims=True)
            hidden_grad = grad_ref[low:high].astype(F32) + norm_back(
                ready_grad, normed, inverse, gain_ref[3:4]
            )
            hidden_grad_ref[low:high] = hidden_grad
            rounded = hidden_grad.astype(BF16)
            low_ref[low:high] = rounded
            low_sum += jnp.sum(rounded.astype(F32), axis=0, keepdims=True)
        sums_ref[...] = jnp.zeros(sums_ref.shape, F32)
        for k in range(groups):
            sums_ref[4 + k : 5 + k, : firsts.shape[2]] = firsts[k]
        sums_ref[0:1] = low_sum
        sums_ref[1:2] = gain_sum
        sums_ref[2:3] = shift_sum
        sums_ref[3:4] = sum_ref[...]
        turned(low_ref[...], turned_ref)


def feed_back(spot, grad, grad_sum, hidden, gain, slope, second, pieces, blocks):
    seq, width = hidden.shape
    groups, _, cols = slope.shape
    size = lanes(cols)
    rows = -(-(4 + groups) // 8) * 8
    outs = [(struct(slope.shape, BF16), ordered(groups, slope.shape))] + [
        (o, whole(o.shape))
        for o in (
            struct((seq, width), F32),
            struct((seq, width), BF16),
            struct((blocks, width // blocks, seq), BF16),
            struct((rows, width), F32),
        )
    ]
    return call(
        functools.partial(feed_back_kernel, len(pieces)),
        "feed_back",
        groups,
        [
            (grad, whole(grad.shape)),
            (grad_sum, whole(grad_sum.shape)),
            (hidden, whole(hidden.shape)),
            (gain, whole(gain.shape)),
            (slope, ordered(groups, slope.shape)),
            (second, ordered(groups, second.shape)),
        ]
        + [(a, near_piece(a, size)) for a in pieces],
        outs,
        4 * groups * seq * width * cols,
        [
            pltpu.VMEM((seq, width), F32),
            pltpu.VMEM((blocks, width // blocks, size), BF16),
            pltpu.VMEM((groups, 1, cols), F32),
        ],
        (spot,),
    )


def mix_back_kernel(grad_ref, weight_ref, out_ref):
    groups, _, part = out_ref.shape
    full = contract(grad_ref[...], weight_ref[...], 1, 0).astype(BF16)
    for k in range(groups):
        out_ref[k] = full[:, k * part : (k + 1) * part]


def mix_back(grad, weight, groups):
    seq, width = grad.shape
    shape = (groups, seq, weight.shape[1] // groups)
    return call(
        mix_back_kernel,
        "mix_back",
        1,
        [(grad, whole(grad.shape)), (weight, whole(weight.shape))],
        [(struct(shape, BF16), whole(shape))],
        2 * seq * width * weight.shape[1],
    )[0]


def project_back_kernel(
    place_ref,
    image_ref,
    gain_ref,
    hidden_grad_ref,
    packed_ref,
    packed_sum_ref,
    weight_ref,
    *rest,
):
    parts = rest[:-3]
    sums_ref, total, blocks = rest[-3:]
    step = pl.program_id(0)
    term = contract(packed_ref[0], weight_ref[0, :, : packed_ref.shape[2]], 1, 1)

    @pl.when(step == 0)
    def _():
        total[...] = term

    @pl.when(step > 0)
    def _():
        total[...] += term

    @pl.when(step == pl.num_programs(0) - 1)
    def _():
        sums_ref[...] = jnp.zeros(sums_ref.shape, F32)
        gain_sum = jnp.zeros((1, total.shape[1]), F32)
        shift_sum = gain_sum
        for low, high in blocks_of(total.shape[0], ROWS):
            normed, inverse = norm(image_ref[low:high].astype(F32))
            ready_grad = total[low:high]
            gain_sum += jnp.sum(ready_grad * normed, axis=0, keepdims=True)
            shift_sum += jnp.sum(ready_grad, axis=0, keepdims=True)
            result = hidden_grad_ref[low:high] + norm_back(
                ready_grad, normed, inverse, gain_ref[0:1]
            )
            total[low:high] = result
        sums_ref[0:1] = gain_sum
        sums_ref[1:2] = shift_sum
        for k in range(packed_sum_ref.shape[0]):
            sums_ref[2 + k : 3 + k, : packed_ref.shape[2]] = packed_sum_ref[k]
        split_parts(place_ref, total[...].astype(BF16), parts, blocks)


def project_back(spot, image, gain, hidden_grad, packed_grad, packed_sum, weight, count):
    seq, width = image.shape
    groups, _, triple = packed_grad.shape
    shape = (width // count, seq)
    sums = struct((-(-(2 + groups) // 8) * 8, width), F32)
    return call(
        project_back_kernel,
        "project_back",
        groups,
        [
            (image, whole(image.shape)),
            (gain, whole(gain.shape)),
            (hidden_grad, whole(hidden_grad.shape)),
            (packed_grad, nth(packed_grad.shape)),
            (packed_sum, whole(packed_sum.shape)),
            (weight, pl.BlockSpec((1, width, lanes(triple)), lambda i, *_: (i, 0, 0))),
        ],
        [(struct(shape, BF16), whole(shape))] * count
        + [(sums, whole(sums.shape))],
        2 * groups * seq * width * triple,
        [
            pltpu.VMEM((seq, width), F32),
            pltpu.VMEM((count, width // count, seq), BF16),
        ],
        (spot,),
    )


def share_kernel(half, cuts, starts, pick_ref, *refs):
    pairs = len(starts)
    turned_refs, right_refs = refs[:pairs], refs[pairs : 2 * pairs]
    rest, picked = refs[2 * pairs : -pairs], refs[-pairs:]
    rows = turned_refs[0].shape[1]
    count = picked[0].shape[0] // rows

    @pl.when(pl.program_id(0) == 0)
    def _():
        for turned_ref, chosen in zip(turned_refs, picked, strict=True):
            for i in range(count):
                chosen[i * rows : (i + 1) * rows] = turned_ref[pick_ref[1 + half * count + i]]

    received, outs = (rest[: pairs * count], rest[pairs * count :]) if cuts else ((), rest)
    each = len(outs) // max(1, len(cuts))
    for p, (start, right_ref, chosen) in enumerate(zip(starts, right_refs, picked, strict=True)):
        product = contract(chosen[...], right_ref[0], 1, 0)
        stop = start + product.shape[1]
        for i in range(count):
            piece = product[i * rows : (i + 1) * rows]
            if not cuts:
                outs[p * count + i][0] = piece.astype(BF16)
            else:
                piece = piece + received[p * count + i][0].astype(F32)
            for n, (low, high, side_first) in enumerate(cuts):
                place = (i // 2, i % 2) if side_first else (i % 2, i // 2)
                first, last = max(low, start), min(high, stop)
                if first < last:
                    outs[n * each + place[0]][place[1], 0, :, first - low : last - low] = piece[
                        :, first - start : last - start
                    ].astype(BF16)


def side_by_side(pairs):
    starts = []
    cols = 0
    for _, right in pairs:
        starts.append(lanes(cols))
        cols = starts[-1] + right.shape[2]
    return starts, cols


def share(spot, first, pairs, received=(), cuts=()):
    turned_rows = [first] + [a for a, _ in pairs[1:]]
    rights = [b for _, b in pairs]
    total, rows, seq = first.shape
    groups = rights[0].shape[0]
    starts, cols = side_by_side(pairs)
    count = total // 2

    def two(size):
        return (
            struct((2, groups, rows, size), BF16),
            pl.BlockSpec((2, 1, rows, size), lambda i, *_: (0, i, 0, 0)),
        )

    if received:
        outs = [two(high - low) for low, high, _ in cuts for _ in range(count // 2)]
    else:
        outs = [
            (struct((groups, rows, b.shape[2]), BF16), nth((groups, rows, b.shape[2])))
            for b in rights
            for _ in range(count)
        ]
    return call(
        functools.partial(share_kernel, 0 if received else 1, cuts, starts),
        "share",
        groups,
        [(a, whole(a.shape)) for a in turned_rows]
        + [(a, nth(a.shape)) for a in rights]
        + [(a, nth(a.shape)) for a in received],
        outs,
        2 * groups * count * rows * seq * cols,
        [pltpu.VMEM((count * rows, seq), BF16)] * len(pairs),
        (spot,),
    )


def swap(array, axis, bit):
    size = lax.axis_size(axis)
    return lax.ppermute(array, axis, [(i, i ^ bit) for i in range(size)])


def everyone(array):
    for axis in ("gx", "dp", "gy"):
        terms = [array] + [swap(array, axis, k) for k in range(1, lax.axis_size(axis))]
        while len(terms) > 1:
            terms = [a + b for a, b in zip(terms[::2], terms[1::2], strict=True)]
        array = terms[0]
    return array


class Sums:
    def __init__(self, line, spot, pairs, halves, *cuts):
        self.line = line
        self.spot = spot
        self.pairs = pairs
        if halves == 1 or not cuts:
            cuts = [(0, side_by_side(pairs)[1], True)]
        self.cuts = [Cut(line, halves, *cut) for cut in cuts]

    def away(self):
        sent = self.line(lambda a: share(self.spot, a, self.pairs), self.pairs[0][0])
        self.arrived = [swap(a, "gx", 1) for a in sent]

    def keep(self):
        cuts = [(cut.low, cut.high, cut.side_first) for cut in self.cuts]
        kept = self.line(
            lambda a: share(self.spot, a, self.pairs, self.arrived, cuts), self.pairs[0][0]
        )
        each = len(kept) // len(cuts)
        for n, cut in enumerate(self.cuts):
            cut.begin(kept[n * each : (n + 1) * each])

    def send(self):
        for cut in self.cuts:
            cut.send()

    def total(self):
        for cut in self.cuts:
            cut.total()


class Cut:
    def __init__(self, line, halves, low, high, side_first):
        self.line = line
        self.low = low
        self.high = high
        self.side_first = side_first
        steps = [("dp", 1), ("gx", 2)] if side_first else [("gx", 2), ("dp", 1)]
        self.steps = steps if halves == 2 else [None, ("gx", 2)]

    def begin(self, kept):
        self.kept = kept[0]
        self.arrived = swap(kept[1], *self.steps[0]) if len(kept) == 2 else None

    def mine(self, i, kept):
        value = kept[i].astype(F32)
        return value if self.arrived is None else value + self.arrived[i].astype(F32)

    def send(self):
        sent = self.line(lambda a: self.mine(1, a).astype(BF16), self.kept)
        self.second = swap(sent, *self.steps[1])

    def total(self):
        self.sum = self.line(
            lambda a: (self.mine(0, a) + self.second.astype(F32)).astype(BF16), self.kept
        )


class Shared:
    def __init__(self, line, halves, *weights):
        sums = [cut for weight in weights for cut in weight.cuts]
        self.line = line
        self.halves = halves
        self.cols = [one.sum.shape[2] for one in sums]
        groups, rows, _ = sums[0].sum.shape
        wide = [jnp.pad(a.sum, ((0, 0), (0, 0), (0, lanes(c) - c))) for a, c in zip(sums, self.cols)]
        wide = line(lambda a: jnp.concatenate([a] + wide[1:], axis=2), wide[0])
        self.own = lax.psum_scatter(
            wide.reshape(groups * rows, wide.shape[2]), "gy", scatter_dimension=0, tiled=True
        )

    def trade(self):
        if self.halves == 2:
            self.own = self.line(lambda a: a, self.own)
            self.other = swap(self.own, "dp", 1)

    def end(self):
        if self.halves == 1:
            full = lax.psum(self.own.astype(F32), "dp")
        else:
            first = lax.axis_index("dp") == 0
            low = jnp.where(first, self.own, self.other)
            high = jnp.where(first, self.other, self.own)
            full = jnp.concatenate([low, high], axis=0).astype(F32)
        starts = [sum(lanes(c) for c in self.cols[:i]) for i in range(len(self.cols))]
        return [full[:, start : start + c] for start, c in zip(starts, self.cols)]


class Line:
    def __init__(self):
        self.last = None

    def __call__(self, step, first):
        if self.last is not None:
            first = after(first, self.last)
        result = step(first)
        self.last = jax.tree.leaves(result)[0]
        return result


def after(value, *others):
    return lax.optimization_barrier((value,) + others)[0]


def traded(parts):
    return [part if r == 0 else swap(part, "gx", r) for r, part in enumerate(parts)]


class Pieces:
    def __init__(self, weight, halves):
        rows = weight.shape[0] // halves
        cols = weight.shape[1]
        both = jnp.pad(weight, ((0, 0), (0, lanes(cols) - cols)))
        if halves == 2:
            both = lax.dynamic_slice_in_dim(both, lax.axis_index("dp") * rows, rows, 0)
        count = lax.axis_size("gy")
        up = [(i, (i + 1) % count) for i in range(count)]
        groups = [both]
        for _ in range(count - 1):
            groups.append(lax.ppermute(groups[-1], "gy", up))
        own = jnp.stack(groups)
        self.halves = halves
        self.near = [own, swap(own, "gx", 2)]
        if halves == 2:
            self.near.append(swap(own, "dp", 1))

    def middle(self, anchor):
        near = [after(piece, anchor) for piece in self.near]
        if self.halves == 2:
            self.near.append(swap(near[1], "dp", 1))
        self.far = [swap(piece, "gx", 1) for piece in near]

    def last(self, anchor):
        if self.halves == 2:
            self.far.append(swap(after(self.near[3], anchor), "gx", 1))
        return self.near + self.far


def lanes(cols):
    return -(-cols // 128) * 128


def collect(block, order):
    return lax.all_gather(block, order, axis=0, tiled=True)


def on_device(
    tokens,
    cotangent,
    ln1_gain,
    ln1_bias,
    qkv_weight,
    qv_bias,
    out_weight,
    out_bias,
    ln2_gain,
    ln2_bias,
    fc1_weight,
    fc1_bias,
    fc2_weight,
    fc2_bias,
):
    gx = lax.axis_size("gx")
    gy = lax.axis_size("gy")
    halves = 2 if lax.axis_size("dp") == 2 else 1
    blocks = gx * halves
    shape = tokens.shape
    turned_shape = (shape[0], shape[2], shape[1])
    part = shape[2]
    head_cols = qkv_weight.shape[2]
    heads = head_cols // HEAD_DIM
    triple = 3 * head_cols
    hidden_cols = fc1_weight.shape[1]
    width = part * gx
    copies = gx // (MICRO * shape[1] // SEQ)
    along = ("gy", "gx")

    column = lax.axis_index("gx")
    half = lax.axis_index("dp")

    def block(core, side, far):
        return (column ^ (2 * far + core)) * halves + (half ^ side if halves == 2 else 0)

    pick = [block(c, s, f) for c in range(2) for s in range(halves) for f in range(2)]
    here = lax.axis_index("gy")
    spot = jnp.concatenate(
        [
            jnp.reshape(column, (1,)),
            jnp.stack(pick),
            (here + gy - jnp.arange(gy, dtype=jnp.int32)) % gy,
        ]
    ).astype(jnp.int32)
    line = Line()

    early = [qkv_weight.reshape(part, triple)]
    early += [a[:, None] for a in (ln1_gain, ln1_bias, out_bias, ln2_gain, ln2_bias, fc2_bias)]
    for vector in (qv_bias[0], qv_bias[1], fc1_bias):
        count = -(-vector.shape[0] // part)
        vector = jnp.pad(vector, (0, count * part - vector.shape[0]))
        early.append(vector.reshape(count, part).T)
    early = jnp.concatenate(early, axis=1)
    early_cols = lanes(early.shape[1])
    early = jnp.concatenate(
        [
            jnp.pad(early, ((0, 0), (0, early_cols - early.shape[1]))),
            jnp.pad(out_weight.T, ((0, 0), (0, lanes(head_cols) - head_cols))),
        ],
        axis=1,
    )
    early = collect(early, along).reshape(gy, width, early.shape[1])
    second = jnp.pad(fc2_weight.T, ((0, 0), (0, lanes(hidden_cols) - hidden_cols)))
    second = collect(second, along).reshape(gy, width, lanes(hidden_cols))
    token_parts = cut(spot, jnp.swapaxes(tokens, 1, 2), gx, copies)
    line.last = token_parts[0]
    grad_parts = line(lambda a: cut(spot, a, gx, copies), jnp.swapaxes(cotangent, 1, 2))
    gathered = Pieces(after(fc1_weight, token_parts[0]), halves)
    token_parts = traded(token_parts)

    image, ready_one, turned_one, packed, wide, bias_first = line(
        lambda a: project(spot, [a] + token_parts[1:], early, triple, hidden_cols, blocks),
        token_parts[0],
    )
    gathered.middle(packed)
    grad_parts = traded([after(a, packed) for a in grad_parts])
    mixture, log_total = line(lambda a: attend(a, heads), packed)
    pieces = gathered.last(mixture)
    log_total = jnp.swapaxes(log_total, 1, 2)
    hidden, ready_two, turned_two, whole_out = line(
        lambda a: mix(a, mixture, wide, early, early_cols, blocks), image
    )
    active, slope = line(lambda a: expand(spot, a, bias_first, pieces, blocks), ready_two)
    grad_low, grad_turned, grad_sum = line(
        lambda a: spread(spot, [a] + grad_parts[1:], blocks), grad_parts[0]
    )

    fc2 = Sums(line, spot, [(grad_turned, active)], halves)
    fc2.away()
    out_parts = line(lambda a: narrow(spot, a, active, second, wide, gx), hidden)
    out_parts = traded(out_parts)
    fc2.keep()
    (
        grad_first,
        grad_hidden,
        grad_hidden_low,
        turned_hidden,
        fed_sums,
    ) = line(
        lambda a: feed_back(spot, a, grad_sum, hidden, wide, slope, second, pieces, blocks), grad_low
    )
    fc1_pairs = [(turned_two, grad_first), (turned_hidden, mixture)]
    fc1_cols = side_by_side(fc1_pairs)[1]
    cut_at = fc1_cols * CUT // 1280 * 128
    fc1 = Sums(line, spot, fc1_pairs, halves, (0, cut_at, True), (cut_at, fc1_cols, False))
    layer_out = line(
        lambda a: place(spot, [a] + out_parts[1:], turned_shape, copies), out_parts[0]
    )
    fc1.away()
    grad_mixture = line(lambda a: mix_back(a, whole_out, gy), grad_hidden_low)
    fc2.send()
    fc1.keep()
    packed_grad, packed_sum = line(
        lambda a: attend_back(a, log_total, grad_mixture, heads, list(range(heads))), packed
    )
    middle = max(1, triple // 256) * 128
    qkv = Sums(
        line, spot, [(turned_one, packed_grad)], halves, (0, middle, True), (middle, triple, False)
    )
    qkv.away()
    fc2.total()
    fc2_end = Shared(line, halves, fc2)
    fc1.send()
    qkv.keep()
    fed_sums = everyone(line(lambda a: a, fed_sums))
    fc1.total()
    fc1_end = Shared(line, halves, fc1)
    *grad_parts, late_sums = line(
        lambda a: project_back(spot, a, wide, grad_hidden, packed_grad, packed_sum, early, gx),
        image,
    )
    qkv.send()
    grad_parts = traded(grad_parts)
    fc2_end.trade()
    fc1_end.trade()
    qkv.total()
    last_end = Shared(line, halves, qkv)
    late_sums = everyone(line(lambda a: a, late_sums))
    last_end.trade()
    tokens_grad = line(
        lambda a: place(spot, [a] + grad_parts[1:], turned_shape, copies), grad_parts[0]
    )
    grad_fc2 = fc2_end.end()[0].T
    grad_fc1 = jnp.concatenate(fc1_end.end(), axis=1)
    grad_out_weight = grad_fc1[:, lanes(hidden_cols) :].T
    grad_fc1 = grad_fc1[:, :hidden_cols]
    grad_qkv = last_end.end()
    grad_qkv = jnp.concatenate(grad_qkv, axis=1).reshape(part, 3, head_cols)

    first_sums = lax.dynamic_index_in_dim(fed_sums, 4 + here, 0, False)[:hidden_cols]
    qv_sums = lax.dynamic_index_in_dim(late_sums, 2 + here, 0, False)
    qv_sums = qv_sums[:triple].reshape(3, head_cols)[::2]
    wide_sums = jnp.concatenate([late_sums[:2], fed_sums[:4]])
    wide_sums = lax.dynamic_slice_in_dim(wide_sums, column * part, part, 1)
    grads = (
        wide_sums[0],
        wide_sums[1],
        grad_qkv,
        qv_sums,
        grad_out_weight,
        wide_sums[2],
        wide_sums[3],
        wide_sums[4],
        grad_fc1,
        first_sums,
        grad_fc2,
        wide_sums[5],
    )
    if copies > 1:
        grads = tuple(grad * (1.0 / copies) for grad in grads)
    return (jnp.swapaxes(layer_out, 1, 2), jnp.swapaxes(tokens_grad, 1, 2)) + grads


def solution(mesh):
    specs = (
        P(None, ("dp", "gy"), "gx"),
        P(None, ("dp", "gy"), "gx"),
        P("gx"),
        P("gx"),
        P("gx", None, "gy"),
        P(None, "gy"),
        P("gy", "gx"),
        P("gx"),
        P("gx"),
        P("gx"),
        P("gx", "gy"),
        P("gy"),
        P("gy", "gx"),
        P("gx"),
    )
    return jax.shard_map(
        on_device,
        mesh=mesh,
        in_specs=specs,
        out_specs=specs,
        check_vma=False,
    )
```

```python
import functools

import jax
import jax.numpy as jnp
from jax import lax
from jax.experimental import pallas as pl
from jax.experimental.pallas import tpu as pltpu
from jax.sharding import PartitionSpec as P

HEAD_DIM = 72
SEQ = 729
MICRO = 2
EPSILON = 1e-06
QUERY_ROWS = 384
BACK_ROWS = 768
ROWS = 256
COST = 1
CUT = 8
COLS = 256
BF16 = jnp.bfloat16
F32 = jnp.float32
SLOPE = jnp.float32
VMEM_BYTES = 60 * 2**20


def contract(left, right, left_dim, right_dim):
    return lax.dot_general(
        left, right, (((left_dim,), (right_dim,)), ((), ())), preferred_element_type=F32
    )


def blocks_of(total, size):
    return [(low, min(low + size, total)) for low in range(0, total, size)]


def whole(shape):
    return pl.BlockSpec(shape, lambda i, *_: (0,) * len(shape))


def nth(shape):
    return pl.BlockSpec((1,) + tuple(shape[1:]), lambda i, *_: (i,) + (0,) * (len(shape) - 1))


def call(kernel, name, steps, ins, outs, flops, scratch=(), prefetch=()):
    moved = sum(a.size * a.dtype.itemsize for a, _ in list(ins) + list(outs))
    return pl.pallas_call(
        kernel,
        grid_spec=pltpu.PrefetchScalarGridSpec(
            num_scalar_prefetch=len(prefetch),
            grid=(steps,),
            in_specs=[spec for _, spec in ins],
            out_specs=[spec for _, spec in outs],
            scratch_shapes=list(scratch),
        ),
        out_shape=[shape for shape, _ in outs],
        compiler_params=pltpu.CompilerParams(vmem_limit_bytes=VMEM_BYTES),
        cost_estimate=pl.CostEstimate(
            flops=flops * COST, bytes_accessed=moved * COST, transcendentals=0
        ),
        name=name,
    )(*prefetch, *[a for a, _ in ins])


def struct(shape, dtype):
    return jax.ShapeDtypeStruct(tuple(shape), dtype)


def attend_kernel(heads, packed_ref, mix_ref, total_ref):
    seq = packed_ref.shape[1]
    width = heads * HEAD_DIM
    scaling = HEAD_DIM ** (-0.5)
    for head in range(heads):
        first = head * HEAD_DIM
        last = first + HEAD_DIM
        keys = packed_ref[0, :, width + first : width + last]
        values = packed_ref[0, :, 2 * width + first : 2 * width + last]
        for low, high in blocks_of(seq, QUERY_ROWS):
            queries = packed_ref[0, low:high, first:last]
            scores = contract(queries, keys, 1, 1) * scaling
            row_max = jnp.max(scores, axis=1, keepdims=True)
            exponent = jnp.exp(scores - row_max)
            row_total = jnp.sum(exponent, axis=1, keepdims=True)
            probability = (exponent * (1.0 / row_total)).astype(BF16)
            mix_ref[0, low:high, first:last] = contract(probability, values, 1, 0).astype(BF16)
            total_ref[0, low:high, head : head + 1] = row_max + jnp.log(row_total)


def attend(packed, heads):
    groups, seq, _ = packed.shape
    mix = struct((groups, seq, heads * HEAD_DIM), BF16)
    total = struct((groups, seq, heads), F32)
    return call(
        functools.partial(attend_kernel, heads),
        "attend",
        groups,
        [(packed, nth(packed.shape))],
        [(mix, nth(mix.shape)), (total, nth(total.shape))],
        12 * groups * heads * seq * seq * HEAD_DIM,
    )


def attend_back_kernel(
    heads, some, packed_ref, total_ref, grad_ref, out_ref, sum_ref, key_sum, value_sum
):
    seq = packed_ref.shape[1]
    width = heads * HEAD_DIM
    part = len(some) * HEAD_DIM
    scaling = HEAD_DIM ** (-0.5)
    for place, head in enumerate(some):
        first = head * HEAD_DIM
        last = first + HEAD_DIM
        start = place * HEAD_DIM
        stop = start + HEAD_DIM
        keys = packed_ref[0, :, width + first : width + last]
        values = packed_ref[0, :, 2 * width + first : 2 * width + last]
        for low, high in blocks_of(seq, BACK_ROWS):
            queries = packed_ref[0, low:high, first:last]
            grads = grad_ref[0, low:high, first:last]
            scores = contract(keys, queries, 1, 1) * scaling
            probability = jnp.exp(scores - total_ref[0, head : head + 1, low:high])
            grad_values = contract(probability.astype(BF16), grads, 1, 0)
            grad_prob = contract(values, grads, 1, 1)
            inner = jnp.sum(probability * grad_prob, axis=0, keepdims=True)
            grad_scores = (probability * (grad_prob - inner)).astype(BF16)
            grad_keys = contract(grad_scores, queries, 1, 0)
            grad_queries = contract(grad_scores, keys, 0, 0) * scaling
            out_ref[0, low:high, start:stop] = grad_queries.astype(BF16)
            if low == 0:
                key_sum[...] = grad_keys
                value_sum[...] = grad_values
            else:
                key_sum[...] += grad_keys
                value_sum[...] += grad_values
        out_ref[0, :, part + start : part + stop] = (key_sum[...] * scaling).astype(BF16)
        out_ref[0, :, 2 * part + start : 2 * part + stop] = value_sum[...].astype(BF16)
    sum_ref[0] = jnp.sum(out_ref[0].astype(F32), axis=0, keepdims=True)


def attend_back(packed, total, grads, heads, some):
    groups, seq, _ = packed.shape
    triple = 3 * len(some) * HEAD_DIM
    out = struct((groups, seq, triple), BF16)
    sums = struct((groups, 1, triple), F32)
    return call(
        functools.partial(attend_back_kernel, heads, some),
        "attend_back",
        groups,
        [(packed, nth(packed.shape)), (total, nth(total.shape)), (grads, nth(grads.shape))],
        [(out, nth(out.shape)), (sums, nth(sums.shape))],
        30 * groups * len(some) * seq * seq * HEAD_DIM,
        [pltpu.VMEM((seq, HEAD_DIM), F32), pltpu.VMEM((seq, HEAD_DIM), F32)],
    )


def norm(values):
    center = jnp.mean(values, axis=1, keepdims=True)
    shifted = values - center
    inverse = lax.rsqrt(jnp.mean(shifted * shifted, axis=1, keepdims=True) + EPSILON)
    return shifted * inverse, inverse


def norm_back(grad_norm, normed, inverse, gain):
    grad_hat = grad_norm * gain
    return inverse * (
        grad_hat
        - jnp.mean(grad_hat, axis=1, keepdims=True)
        - normed * jnp.mean(grad_hat * normed, axis=1, keepdims=True)
    )


def on_column(place_ref, count, body):
    for c in range(count):
        pl.when(place_ref[0] == c)(functools.partial(body, c))


def join_parts(place_ref, parts, blocks_ref):
    rows = blocks_ref.shape[1]
    each = parts[0].shape[0] // rows
    for r, ref in enumerate(parts):
        for i in range(each):
            blocks_ref[(place_ref[0] ^ r) * each + i] = ref[i * rows : (i + 1) * rows]


def flat(blocks_ref):
    count, rows, seq = blocks_ref.shape
    return blocks_ref[...].reshape(count * rows, seq)


def split_parts(place_ref, values, parts, blocks_ref):
    turned(values, blocks_ref)
    for r, ref in enumerate(parts):
        ref[...] = blocks_ref[place_ref[0] ^ r]


def join_columns(parts_ref, whole_ref):
    groups, _, part = parts_ref.shape
    for k in range(groups):
        whole_ref[:, k * part : (k + 1) * part] = parts_ref[k]


def order_of(place_ref, groups, k):
    return place_ref[place_ref.shape[0] - groups + k]


def join_rows(place_ref, pieces, whole_ref):
    for p, ref in enumerate(pieces):
        whole_ref[place_ref[1 + p]] = ref[0]


def turned(rows, blocks_ref):
    columns = rows.T
    count, size, _ = blocks_ref.shape
    for i in range(count):
        blocks_ref[i] = columns[i * size : (i + 1) * size]


def cut_kernel(copies, place_ref, rows_ref, *parts):
    seq = parts[0].shape[1]
    each = rows_ref.shape[2] // seq

    def body(c):
        for r, ref in enumerate(parts):
            image = (c ^ r) // copies
            start = (image % each) * seq
            ref[...] = rows_ref[image // each, :, start : start + seq]

    on_column(place_ref, len(parts), body)


def cut(spot, rows, count, copies):
    shape = struct((rows.shape[1], SEQ), BF16)
    return call(
        functools.partial(cut_kernel, copies),
        "cut",
        1,
        [(rows, whole(rows.shape))],
        [(shape, whole(shape.shape))] * count,
        0,
        prefetch=(spot,),
    )


def place_kernel(copies, place_ref, *refs):
    parts, rows_ref = refs[:-1], refs[-1]
    seq = parts[0].shape[1]
    each = rows_ref.shape[2] // seq

    def body(c):
        for image in range(len(parts) // copies):
            start = (image % each) * seq
            rows_ref[image // each, :, start : start + seq] = parts[c ^ (image * copies)][...]

    on_column(place_ref, len(parts), body)


def place(spot, parts, shape, copies):
    return call(
        functools.partial(place_kernel, copies),
        "place",
        1,
        [(a, whole(a.shape)) for a in parts],
        [(struct(shape, BF16), whole(shape))],
        0,
        prefetch=(spot,),
    )[0]


def spread_kernel(place_ref, *refs):
    parts = refs[:-3]
    whole_ref, turned_ref, sum_ref = refs[-3:]
    join_parts(place_ref, parts, turned_ref)
    whole_ref[...] = flat(turned_ref).T
    sum_ref[...] = jnp.sum(whole_ref[...].astype(F32), axis=0, keepdims=True)


def spread(spot, parts, blocks):
    part, seq = parts[0].shape
    width = len(parts) * part
    outs = [
        struct((seq, width), BF16),
        struct((blocks, width // blocks, seq), BF16),
        struct((1, width), F32),
    ]
    return call(
        spread_kernel,
        "spread",
        1,
        [(a, whole(a.shape)) for a in parts],
        [(o, whole(o.shape)) for o in outs],
        seq * width,
        prefetch=(spot,),
    )


def project_kernel(count, triple, place_ref, *refs):
    parts = refs[:count]
    weight_ref = refs[count]
    image_ref, ready_ref, turned_ref, packed_ref, wide_ref, first_ref = refs[count + 1 :]
    part = parts[0].shape[0]
    third = triple // 3
    start = triple // 128 * 128
    notes = weight_ref[0, :, start:].astype(F32).T[triple - start :]

    @pl.when(pl.program_id(0) == 0)
    def _():
        wide_ref[0:6] = notes[0:6]
        join_parts(place_ref, parts, turned_ref)
        image_ref[...] = flat(turned_ref).T
        for low, high in blocks_of(image_ref.shape[0], ROWS):
            normed, _ = norm(image_ref[low:high].astype(F32))
            ready_ref[low:high] = (normed * notes[0:1] + notes[1:2]).astype(BF16)
        turned(ready_ref[...], turned_ref)

    for i, (low, high) in enumerate(blocks_of(first_ref.shape[2], part)):
        first_ref[0, :, low:high] = notes[8 + i : 9 + i, : high - low]
    product = contract(ready_ref[...], weight_ref[0, :, :triple], 1, 0)
    packed_ref[0, :, :third] = (product[:, :third] + notes[6:7, :third]).astype(BF16)
    packed_ref[0, :, third : 2 * third] = product[:, third : 2 * third].astype(BF16)
    packed_ref[0, :, 2 * third :] = (product[:, 2 * third :] + notes[7:8, :third]).astype(BF16)


def project(spot, parts, weight, triple, cols, blocks):
    part, seq = parts[0].shape
    width = len(parts) * part
    groups = weight.shape[0]
    outs = [
        (struct((seq, width), BF16), whole((seq, width))),
        (struct((seq, width), BF16), whole((seq, width))),
        (struct((blocks, width // blocks, seq), BF16), whole((blocks, width // blocks, seq))),
        (struct((groups, seq, triple), BF16), nth((groups, seq, triple))),
        (struct((8, width), F32), whole((8, width))),
        (struct((groups, 1, cols), F32), nth((groups, 1, cols))),
    ]
    return call(
        functools.partial(project_kernel, len(parts), triple),
        "project",
        groups,
        [(a, whole(a.shape)) for a in parts]
        + [(weight, pl.BlockSpec((1, width, lanes(triple)), lambda i, *_: (i, 0, 0)))],
        outs,
        2 * groups * seq * width * triple,
        prefetch=(spot,),
    )


def mix_kernel(count, image_ref, parts_ref, wide_ref, *refs):
    strips = refs[:count]
    hidden_ref, ready_ref, turned_ref, weight_ref, joined = refs[count:]
    groups, _, part = parts_ref.shape
    join_columns(parts_ref, joined)
    for strip, (low, high) in zip(strips, blocks_of(part, 128), strict=True):
        for k in range(groups):
            weight_ref[:, k * part + low : k * part + high] = strip[k, :, : high - low]
    for low, high in blocks_of(image_ref.shape[0], ROWS):
        mixed = contract(joined[low:high], weight_ref[...], 1, 1) + wide_ref[2:3]
        hidden = image_ref[low:high].astype(F32) + mixed
        hidden_ref[low:high] = hidden
        normed, _ = norm(hidden)
        ready_ref[low:high] = (normed * wide_ref[3:4] + wide_ref[4:5]).astype(BF16)
    turned(ready_ref[...], turned_ref)


def mix(image, parts, wide, weight, start, blocks):
    seq, width = image.shape
    groups, _, part = parts.shape
    inner = groups * part
    strips = [
        pl.BlockSpec((groups, width, 128), lambda i, *_, at=at: (0, 0, at))
        for at in range(start // 128, start // 128 + len(blocks_of(part, 128)))
    ]
    outs = [
        struct((seq, width), F32),
        struct((seq, width), BF16),
        struct((blocks, width // blocks, seq), BF16),
        struct((width, inner), BF16),
    ]
    return call(
        functools.partial(mix_kernel, len(strips)),
        "mix",
        1,
        [(a, whole(a.shape)) for a in (image, parts, wide)] + [(weight, strip) for strip in strips],
        [(o, whole(o.shape)) for o in outs],
        2 * seq * width * inner,
        [pltpu.VMEM((seq, inner), BF16)],
    )


def expand_kernel(count, place_ref, ready_ref, bias_ref, *refs):
    pieces = refs[:count]
    active_ref, slope_ref, weight = refs[count:]
    bend = 0.7978845608028654
    cubic = 0.044715
    join_rows(place_ref, pieces, weight)
    for low, high in blocks_of(active_ref.shape[2], COLS):
        right = weight[:, :, low:high].reshape(-1, high - low)
        first = contract(ready_ref[...], right, 1, 0) + bias_ref[0, :, low:high]
        square = first * first
        bent = jnp.tanh(bend * (first + cubic * (first * square)))
        half = 0.5 * (1.0 + bent)
        active_ref[0, :, low:high] = (first * half).astype(BF16)
        slope = half + (0.5 * bend) * first * (1.0 - bent * bent) * (1.0 + (3.0 * cubic) * square)
        slope_ref[0, :, low:high] = slope.astype(SLOPE)


def near_piece(piece, size):
    return pl.BlockSpec((1, piece.shape[1], size), lambda i, *_: (i, 0, 0))


def ordered(groups, shape):
    zeros = (0,) * (len(shape) - 1)
    return pl.BlockSpec(
        (1,) + tuple(shape[1:]), lambda i, spot: (order_of(spot, groups, i),) + zeros
    )


def expand(spot, ready, bias, pieces, blocks):
    seq, width = ready.shape
    groups, _, cols = bias.shape
    shape = (groups, seq, cols)
    size = lanes(cols)
    return call(
        functools.partial(expand_kernel, len(pieces)),
        "expand",
        groups,
        [(ready, whole(ready.shape)), (bias, ordered(groups, bias.shape))]
        + [(a, near_piece(a, size)) for a in pieces],
        [(struct(shape, BF16), ordered(groups, shape)), (struct(shape, SLOPE), ordered(groups, shape))],
        2 * groups * seq * width * cols,
        [pltpu.VMEM((blocks, width // blocks, size), BF16)],
        (spot,),
    )


def narrow_kernel(place_ref, hidden_ref, active_ref, weight_ref, bias_ref, *rest):
    parts = rest[:-2]
    total, blocks = rest[-2:]
    step = pl.program_id(0)
    term = contract(active_ref[0], weight_ref[0, :, : active_ref.shape[2]], 1, 1)

    @pl.when(step == 0)
    def _():
        total[...] = hidden_ref[...] + bias_ref[5:6] + term

    @pl.when(step > 0)
    def _():
        total[...] += term

    @pl.when(step == pl.num_programs(0) - 1)
    def _():
        split_parts(place_ref, total[...].astype(BF16), parts, blocks)


def narrow(spot, hidden, active, weight, bias, count):
    seq, width = hidden.shape
    groups, _, cols = active.shape
    shape = (width // count, seq)
    return call(
        narrow_kernel,
        "narrow",
        groups,
        [
            (hidden, whole(hidden.shape)),
            (active, nth(active.shape)),
            (weight, nth(weight.shape)),
            (bias, whole(bias.shape)),
        ],
        [(struct(shape, BF16), whole(shape))] * count,
        2 * groups * seq * width * cols,
        [pltpu.VMEM((seq, width), F32), pltpu.VMEM((count, width // count, seq), BF16)],
        (spot,),
    )


def feed_back_kernel(
    count, place_ref, grad_ref, sum_ref, hidden_ref, gain_ref, slope_ref, second_ref, *refs
):
    pieces = refs[:count]
    (
        first_grad_ref,
        hidden_grad_ref,
        low_ref,
        turned_ref,
        sums_ref,
        total,
        weight,
        firsts,
    ) = refs[count:]
    step = pl.program_id(0)
    groups = place_ref.shape[0] - 1 - count
    place = order_of(place_ref, groups, step)
    join_rows(place_ref, pieces, weight)
    for low, high in blocks_of(slope_ref.shape[2], COLS):
        active_grad = contract(grad_ref[...], second_ref[0, :, low:high], 1, 0)
        first_grad = (active_grad * slope_ref[0, :, low:high].astype(F32)).astype(BF16)
        first_grad_ref[0, :, low:high] = first_grad
        firsts[place, :, low:high] = jnp.sum(first_grad.astype(F32), axis=0, keepdims=True)
    right = flat(weight)[:, : slope_ref.shape[2]]
    term = contract(first_grad_ref[0], right, 1, 1)

    @pl.when(step == 0)
    def _():
        total[...] = term

    @pl.when(step > 0)
    def _():
        total[...] += term

    @pl.when(step == pl.num_programs(0) - 1)
    def _():
        gain_sum = jnp.zeros((1, total.shape[1]), F32)
        shift_sum = gain_sum
        low_sum = gain_sum
        for low, high in blocks_of(total.shape[0], ROWS):
            normed, inverse = norm(hidden_ref[low:high])
            ready_grad = total[low:high]
            gain_sum += jnp.sum(ready_grad * normed, axis=0, keepdims=True)
            shift_sum += jnp.sum(ready_grad, axis=0, keepdims=True)
            hidden_grad = grad_ref[low:high].astype(F32) + norm_back(
                ready_grad, normed, inverse, gain_ref[3:4]
            )
            hidden_grad_ref[low:high] = hidden_grad
            rounded = hidden_grad.astype(BF16)
            low_ref[low:high] = rounded
            low_sum += jnp.sum(rounded.astype(F32), axis=0, keepdims=True)
        sums_ref[...] = jnp.zeros(sums_ref.shape, F32)
        for k in range(groups):
            sums_ref[4 + k : 5 + k, : firsts.shape[2]] = firsts[k]
        sums_ref[0:1] = low_sum
        sums_ref[1:2] = gain_sum
        sums_ref[2:3] = shift_sum
        sums_ref[3:4] = sum_ref[...]
        turned(low_ref[...], turned_ref)


def feed_back(spot, grad, grad_sum, hidden, gain, slope, second, pieces, blocks):
    seq, width = hidden.shape
    groups, _, cols = slope.shape
    size = lanes(cols)
    rows = -(-(4 + groups) // 8) * 8
    outs = [(struct(slope.shape, BF16), ordered(groups, slope.shape))] + [
        (o, whole(o.shape))
        for o in (
            struct((seq, width), F32),
            struct((seq, width), BF16),
            struct((blocks, width // blocks, seq), BF16),
            struct((rows, width), F32),
        )
    ]
    return call(
        functools.partial(feed_back_kernel, len(pieces)),
        "feed_back",
        groups,
        [
            (grad, whole(grad.shape)),
            (grad_sum, whole(grad_sum.shape)),
            (hidden, whole(hidden.shape)),
            (gain, whole(gain.shape)),
            (slope, ordered(groups, slope.shape)),
            (second, ordered(groups, second.shape)),
        ]
        + [(a, near_piece(a, size)) for a in pieces],
        outs,
        4 * groups * seq * width * cols,
        [
            pltpu.VMEM((seq, width), F32),
            pltpu.VMEM((blocks, width // blocks, size), BF16),
            pltpu.VMEM((groups, 1, cols), F32),
        ],
        (spot,),
    )


def mix_back_kernel(grad_ref, weight_ref, out_ref):
    groups, _, part = out_ref.shape
    full = contract(grad_ref[...], weight_ref[...], 1, 0).astype(BF16)
    for k in range(groups):
        out_ref[k] = full[:, k * part : (k + 1) * part]


def mix_back(grad, weight, groups):
    seq, width = grad.shape
    shape = (groups, seq, weight.shape[1] // groups)
    return call(
        mix_back_kernel,
        "mix_back",
        1,
        [(grad, whole(grad.shape)), (weight, whole(weight.shape))],
        [(struct(shape, BF16), whole(shape))],
        2 * seq * width * weight.shape[1],
    )[0]


def project_back_kernel(
    place_ref,
    image_ref,
    gain_ref,
    hidden_grad_ref,
    packed_ref,
    packed_sum_ref,
    weight_ref,
    *rest,
):
    parts = rest[:-3]
    sums_ref, total, blocks = rest[-3:]
    step = pl.program_id(0)
    term = contract(packed_ref[0], weight_ref[0, :, : packed_ref.shape[2]], 1, 1)

    @pl.when(step == 0)
    def _():
        total[...] = term

    @pl.when(step > 0)
    def _():
        total[...] += term

    @pl.when(step == pl.num_programs(0) - 1)
    def _():
        sums_ref[...] = jnp.zeros(sums_ref.shape, F32)
        gain_sum = jnp.zeros((1, total.shape[1]), F32)
        shift_sum = gain_sum
        for low, high in blocks_of(total.shape[0], ROWS):
            normed, inverse = norm(image_ref[low:high].astype(F32))
            ready_grad = total[low:high]
            gain_sum += jnp.sum(ready_grad * normed, axis=0, keepdims=True)
            shift_sum += jnp.sum(ready_grad, axis=0, keepdims=True)
            result = hidden_grad_ref[low:high] + norm_back(
                ready_grad, normed, inverse, gain_ref[0:1]
            )
            total[low:high] = result
        sums_ref[0:1] = gain_sum
        sums_ref[1:2] = shift_sum
        for k in range(packed_sum_ref.shape[0]):
            sums_ref[2 + k : 3 + k, : packed_ref.shape[2]] = packed_sum_ref[k]
        split_parts(place_ref, total[...].astype(BF16), parts, blocks)


def project_back(spot, image, gain, hidden_grad, packed_grad, packed_sum, weight, count):
    seq, width = image.shape
    groups, _, triple = packed_grad.shape
    shape = (width // count, seq)
    sums = struct((-(-(2 + groups) // 8) * 8, width), F32)
    return call(
        project_back_kernel,
        "project_back",
        groups,
        [
            (image, whole(image.shape)),
            (gain, whole(gain.shape)),
            (hidden_grad, whole(hidden_grad.shape)),
            (packed_grad, nth(packed_grad.shape)),
            (packed_sum, whole(packed_sum.shape)),
            (weight, pl.BlockSpec((1, width, lanes(triple)), lambda i, *_: (i, 0, 0))),
        ],
        [(struct(shape, BF16), whole(shape))] * count
        + [(sums, whole(sums.shape))],
        2 * groups * seq * width * triple,
        [
            pltpu.VMEM((seq, width), F32),
            pltpu.VMEM((count, width // count, seq), BF16),
        ],
        (spot,),
    )


def share_kernel(half, cuts, starts, pick_ref, *refs):
    pairs = len(starts)
    turned_refs, right_refs = refs[:pairs], refs[pairs : 2 * pairs]
    rest, picked = refs[2 * pairs : -pairs], refs[-pairs:]
    rows = turned_refs[0].shape[1]
    count = picked[0].shape[0] // rows

    @pl.when(pl.program_id(0) == 0)
    def _():
        for turned_ref, chosen in zip(turned_refs, picked, strict=True):
            for i in range(count):
                chosen[i * rows : (i + 1) * rows] = turned_ref[pick_ref[1 + half * count + i]]

    received, outs = (rest[: pairs * count], rest[pairs * count :]) if cuts else ((), rest)
    each = len(outs) // max(1, len(cuts))
    for p, (start, right_ref, chosen) in enumerate(zip(starts, right_refs, picked, strict=True)):
        product = contract(chosen[...], right_ref[0], 1, 0)
        stop = start + product.shape[1]
        for i in range(count):
            piece = product[i * rows : (i + 1) * rows]
            if not cuts:
                outs[p * count + i][0] = piece.astype(BF16)
            else:
                piece = piece + received[p * count + i][0].astype(F32)
            for n, (low, high, side_first) in enumerate(cuts):
                place = (i // 2, i % 2) if side_first else (i % 2, i // 2)
                first, last = max(low, start), min(high, stop)
                if first < last:
                    outs[n * each + place[0]][place[1], 0, :, first - low : last - low] = piece[
                        :, first - start : last - start
                    ].astype(BF16)


def side_by_side(pairs):
    starts = []
    cols = 0
    for _, right in pairs:
        starts.append(lanes(cols))
        cols = starts[-1] + right.shape[2]
    return starts, cols


def share(spot, first, pairs, received=(), cuts=()):
    turned_rows = [first] + [a for a, _ in pairs[1:]]
    rights = [b for _, b in pairs]
    total, rows, seq = first.shape
    groups = rights[0].shape[0]
    starts, cols = side_by_side(pairs)
    count = total // 2

    def two(size):
        return (
            struct((2, groups, rows, size), BF16),
            pl.BlockSpec((2, 1, rows, size), lambda i, *_: (0, i, 0, 0)),
        )

    if received:
        outs = [two(high - low) for low, high, _ in cuts for _ in range(count // 2)]
    else:
        outs = [
            (struct((groups, rows, b.shape[2]), BF16), nth((groups, rows, b.shape[2])))
            for b in rights
            for _ in range(count)
        ]
    return call(
        functools.partial(share_kernel, 0 if received else 1, cuts, starts),
        "share",
        groups,
        [(a, whole(a.shape)) for a in turned_rows]
        + [(a, nth(a.shape)) for a in rights]
        + [(a, nth(a.shape)) for a in received],
        outs,
        2 * groups * count * rows * seq * cols,
        [pltpu.VMEM((count * rows, seq), BF16)] * len(pairs),
        (spot,),
    )


def swap(array, axis, bit):
    size = lax.axis_size(axis)
    return lax.ppermute(array, axis, [(i, i ^ bit) for i in range(size)])


def everyone(array):
    for axis in ("gx", "dp", "gy"):
        terms = [array] + [swap(array, axis, k) for k in range(1, lax.axis_size(axis))]
        while len(terms) > 1:
            terms = [a + b for a, b in zip(terms[::2], terms[1::2], strict=True)]
        array = terms[0]
    return array


class Sums:
    def __init__(self, line, spot, pairs, halves, *cuts):
        self.line = line
        self.spot = spot
        self.pairs = pairs
        if halves == 1 or not cuts:
            cuts = [(0, side_by_side(pairs)[1], True)]
        self.cuts = [Cut(line, halves, *cut) for cut in cuts]

    def away(self):
        sent = self.line(lambda a: share(self.spot, a, self.pairs), self.pairs[0][0])
        self.arrived = [swap(a, "gx", 1) for a in sent]

    def keep(self):
        cuts = [(cut.low, cut.high, cut.side_first) for cut in self.cuts]
        kept = self.line(
            lambda a: share(self.spot, a, self.pairs, self.arrived, cuts), self.pairs[0][0]
        )
        each = len(kept) // len(cuts)
        for n, cut in enumerate(self.cuts):
            cut.begin(kept[n * each : (n + 1) * each])

    def send(self):
        for cut in self.cuts:
            cut.send()

    def total(self):
        for cut in self.cuts:
            cut.total()


class Cut:
    def __init__(self, line, halves, low, high, side_first):
        self.line = line
        self.low = low
        self.high = high
        self.side_first = side_first
        steps = [("dp", 1), ("gx", 2)] if side_first else [("gx", 2), ("dp", 1)]
        self.steps = steps if halves == 2 else [None, ("gx", 2)]

    def begin(self, kept):
        self.kept = kept[0]
        self.arrived = swap(kept[1], *self.steps[0]) if len(kept) == 2 else None

    def mine(self, i, kept):
        value = kept[i].astype(F32)
        return value if self.arrived is None else value + self.arrived[i].astype(F32)

    def send(self):
        sent = self.line(lambda a: self.mine(1, a).astype(BF16), self.kept)
        self.second = swap(sent, *self.steps[1])

    def total(self):
        self.sum = self.line(
            lambda a: (self.mine(0, a) + self.second.astype(F32)).astype(BF16), self.kept
        )


class Shared:
    def __init__(self, line, halves, *weights):
        sums = [cut for weight in weights for cut in weight.cuts]
        self.line = line
        self.halves = halves
        self.cols = [one.sum.shape[2] for one in sums]
        groups, rows, _ = sums[0].sum.shape
        wide = [jnp.pad(a.sum, ((0, 0), (0, 0), (0, lanes(c) - c))) for a, c in zip(sums, self.cols)]
        wide = line(lambda a: jnp.concatenate([a] + wide[1:], axis=2), wide[0])
        self.own = lax.psum_scatter(
            wide.reshape(groups * rows, wide.shape[2]), "gy", scatter_dimension=0, tiled=True
        )

    def trade(self):
        if self.halves == 2:
            self.own = self.line(lambda a: a, self.own)
            self.other = swap(self.own, "dp", 1)

    def end(self):
        if self.halves == 1:
            full = lax.psum(self.own.astype(F32), "dp")
        else:
            first = lax.axis_index("dp") == 0
            low = jnp.where(first, self.own, self.other)
            high = jnp.where(first, self.other, self.own)
            full = jnp.concatenate([low, high], axis=0).astype(F32)
        starts = [sum(lanes(c) for c in self.cols[:i]) for i in range(len(self.cols))]
        return [full[:, start : start + c] for start, c in zip(starts, self.cols)]


class Line:
    def __init__(self):
        self.last = None

    def __call__(self, step, first):
        if self.last is not None:
            first = after(first, self.last)
        result = step(first)
        self.last = jax.tree.leaves(result)[0]
        return result


def after(value, *others):
    return lax.optimization_barrier((value,) + others)[0]


def traded(parts):
    return [part if r == 0 else swap(part, "gx", r) for r, part in enumerate(parts)]


class Pieces:
    def __init__(self, weight, halves):
        rows = weight.shape[0] // halves
        cols = weight.shape[1]
        both = jnp.pad(weight, ((0, 0), (0, lanes(cols) - cols)))
        if halves == 2:
            both = lax.dynamic_slice_in_dim(both, lax.axis_index("dp") * rows, rows, 0)
        count = lax.axis_size("gy")
        up = [(i, (i + 1) % count) for i in range(count)]
        groups = [both]
        for _ in range(count - 1):
            groups.append(lax.ppermute(groups[-1], "gy", up))
        own = jnp.stack(groups)
        self.halves = halves
        self.near = [own, swap(own, "gx", 2)]
        if halves == 2:
            self.near.append(swap(own, "dp", 1))

    def middle(self, anchor):
        near = [after(piece, anchor) for piece in self.near]
        if self.halves == 2:
            self.near.append(swap(near[1], "dp", 1))
        self.far = [swap(piece, "gx", 1) for piece in near]

    def last(self, anchor):
        if self.halves == 2:
            self.far.append(swap(after(self.near[3], anchor), "gx", 1))
        return self.near + self.far


def lanes(cols):
    return -(-cols // 128) * 128


def collect(block, order):
    return lax.all_gather(block, order, axis=0, tiled=True)


def on_device(
    tokens,
    cotangent,
    ln1_gain,
    ln1_bias,
    qkv_weight,
    qv_bias,
    out_weight,
    out_bias,
    ln2_gain,
    ln2_bias,
    fc1_weight,
    fc1_bias,
    fc2_weight,
    fc2_bias,
):
    gx = lax.axis_size("gx")
    gy = lax.axis_size("gy")
    halves = 2 if lax.axis_size("dp") == 2 else 1
    blocks = gx * halves
    shape = tokens.shape
    turned_shape = (shape[0], shape[2], shape[1])
    part = shape[2]
    head_cols = qkv_weight.shape[2]
    heads = head_cols // HEAD_DIM
    triple = 3 * head_cols
    hidden_cols = fc1_weight.shape[1]
    width = part * gx
    copies = gx // (MICRO * shape[1] // SEQ)
    along = ("gy", "gx")

    column = lax.axis_index("gx")
    half = lax.axis_index("dp")

    def block(core, side, far):
        return (column ^ (2 * far + core)) * halves + (half ^ side if halves == 2 else 0)

    pick = [block(c, s, f) for c in range(2) for s in range(halves) for f in range(2)]
    here = lax.axis_index("gy")
    spot = jnp.concatenate(
        [
            jnp.reshape(column, (1,)),
            jnp.stack(pick),
            (here + gy - jnp.arange(gy, dtype=jnp.int32)) % gy,
        ]
    ).astype(jnp.int32)
    line = Line()

    early = [qkv_weight.reshape(part, triple)]
    early += [a[:, None] for a in (ln1_gain, ln1_bias, out_bias, ln2_gain, ln2_bias, fc2_bias)]
    for vector in (qv_bias[0], qv_bias[1], fc1_bias):
        count = -(-vector.shape[0] // part)
        vector = jnp.pad(vector, (0, count * part - vector.shape[0]))
        early.append(vector.reshape(count, part).T)
    early = jnp.concatenate(early, axis=1)
    early_cols = lanes(early.shape[1])
    early = jnp.concatenate(
        [
            jnp.pad(early, ((0, 0), (0, early_cols - early.shape[1]))),
            jnp.pad(out_weight.T, ((0, 0), (0, lanes(head_cols) - head_cols))),
        ],
        axis=1,
    )
    early = collect(early, along).reshape(gy, width, early.shape[1])
    second = jnp.pad(fc2_weight.T, ((0, 0), (0, lanes(hidden_cols) - hidden_cols)))
    second = collect(second, along).reshape(gy, width, lanes(hidden_cols))
    token_parts = cut(spot, jnp.swapaxes(tokens, 1, 2), gx, copies)
    line.last = token_parts[0]
    grad_parts = line(lambda a: cut(spot, a, gx, copies), jnp.swapaxes(cotangent, 1, 2))
    gathered = Pieces(after(fc1_weight, token_parts[0]), halves)
    token_parts = traded(token_parts)

    image, ready_one, turned_one, packed, wide, bias_first = line(
        lambda a: project(spot, [a] + token_parts[1:], early, triple, hidden_cols, blocks),
        token_parts[0],
    )
    gathered.middle(packed)
    grad_parts = traded([after(a, packed) for a in grad_parts])
    mixture, log_total = line(lambda a: attend(a, heads), packed)
    pieces = gathered.last(mixture)
    log_total = jnp.swapaxes(log_total, 1, 2)
    hidden, ready_two, turned_two, whole_out = line(
        lambda a: mix(a, mixture, wide, early, early_cols, blocks), image
    )
    active, slope = line(lambda a: expand(spot, a, bias_first, pieces, blocks), ready_two)
    grad_low, grad_turned, grad_sum = line(
        lambda a: spread(spot, [a] + grad_parts[1:], blocks), grad_parts[0]
    )

    fc2 = Sums(line, spot, [(grad_turned, active)], halves)
    fc2.away()
    out_parts = line(lambda a: narrow(spot, a, active, second, wide, gx), hidden)
    out_parts = traded(out_parts)
    fc2.keep()
    (
        grad_first,
        grad_hidden,
        grad_hidden_low,
        turned_hidden,
        fed_sums,
    ) = line(
        lambda a: feed_back(spot, a, grad_sum, hidden, wide, slope, second, pieces, blocks), grad_low
    )
    fc1_pairs = [(turned_two, grad_first), (turned_hidden, mixture)]
    fc1_cols = side_by_side(fc1_pairs)[1]
    cut_at = fc1_cols * CUT // 1280 * 128
    fc1 = Sums(line, spot, fc1_pairs, halves, (0, cut_at, True), (cut_at, fc1_cols, False))
    layer_out = line(
        lambda a: place(spot, [a] + out_parts[1:], turned_shape, copies), out_parts[0]
    )
    fc1.away()
    grad_mixture = line(lambda a: mix_back(a, whole_out, gy), grad_hidden_low)
    fc2.send()
    fc1.keep()
    packed_grad, packed_sum = line(
        lambda a: attend_back(a, log_total, grad_mixture, heads, list(range(heads))), packed
    )
    middle = max(1, triple // 256) * 128
    qkv = Sums(
        line, spot, [(turned_one, packed_grad)], halves, (0, middle, True), (middle, triple, False)
    )
    qkv.away()
    fc2.total()
    fc2_end = Shared(line, halves, fc2)
    fc1.send()
    qkv.keep()
    fc1.total()
    fc1_end = Shared(line, halves, fc1)
    *grad_parts, late_sums = line(
        lambda a: project_back(spot, a, wide, grad_hidden, packed_grad, packed_sum, early, gx),
        image,
    )
    qkv.send()
    grad_parts = traded(grad_parts)
    fc2_end.trade()
    fc1_end.trade()
    qkv.total()
    last_end = Shared(line, halves, qkv)
    top = fed_sums.shape[0]
    sums = everyone(line(lambda a: jnp.concatenate([fed_sums, a]), late_sums))
    fed_sums, late_sums = sums[:top], sums[top:]
    last_end.trade()
    tokens_grad = line(
        lambda a: place(spot, [a] + grad_parts[1:], turned_shape, copies), grad_parts[0]
    )
    grad_fc2 = fc2_end.end()[0].T
    grad_fc1 = jnp.concatenate(fc1_end.end(), axis=1)
    grad_out_weight = grad_fc1[:, lanes(hidden_cols) :].T
    grad_fc1 = grad_fc1[:, :hidden_cols]
    grad_qkv = last_end.end()
    grad_qkv = jnp.concatenate(grad_qkv, axis=1).reshape(part, 3, head_cols)

    first_sums = lax.dynamic_index_in_dim(fed_sums, 4 + here, 0, False)[:hidden_cols]
    qv_sums = lax.dynamic_index_in_dim(late_sums, 2 + here, 0, False)
    qv_sums = qv_sums[:triple].reshape(3, head_cols)[::2]
    wide_sums = jnp.concatenate([late_sums[:2], fed_sums[:4]])
    wide_sums = lax.dynamic_slice_in_dim(wide_sums, column * part, part, 1)
    grads = (
        wide_sums[0],
        wide_sums[1],
        grad_qkv,
        qv_sums,
        grad_out_weight,
        wide_sums[2],
        wide_sums[3],
        wide_sums[4],
        grad_fc1,
        first_sums,
        grad_fc2,
        wide_sums[5],
    )
    if copies > 1:
        grads = tuple(grad * (1.0 / copies) for grad in grads)
    return (jnp.swapaxes(layer_out, 1, 2), jnp.swapaxes(tokens_grad, 1, 2)) + grads


def solution(mesh):
    specs = (
        P(None, ("dp", "gy"), "gx"),
        P(None, ("dp", "gy"), "gx"),
        P("gx"),
        P("gx"),
        P("gx", None, "gy"),
        P(None, "gy"),
        P("gy", "gx"),
        P("gx"),
        P("gx"),
        P("gx"),
        P("gx", "gy"),
        P("gy"),
        P("gy", "gx"),
        P("gx"),
    )
    return jax.shard_map(
        on_device,
        mesh=mesh,
        in_specs=specs,
        out_specs=specs,
        check_vma=False,
    )
```
